32 devices in a mesh: lat: 4 (over y, core), lon: 8 (over z, x).
Axes of the slice: x: 2, y: 2, z: 4, core: 2. Of those that a mesh axis runs over, the one named last changes fastest.
Arguments:
- queries: bfloat16 [64, 128, 512], P('lat', 'lon'), may hold values from -6 to 6
- keys: bfloat16 [64, 128, 512], P('lat', 'lon'), may hold values from -6 to 6
- values: bfloat16 [64, 128, 512], P('lat', 'lon'), may hold values from -16 to 16
- rel_bias: float32 [8, 13, 13], replicated, may hold values from -4 to 4
- out_weight: bfloat16 [512, 1024], replicated, may hold values from -0.25 to 0.25
- cotangent: bfloat16 [64, 128, 1024], P('lat', 'lon'), may hold values from -16 to 16
Outputs:
- block_out: bfloat16 [64, 128, 1024], P('lat', 'lon')
- query_grad: bfloat16 [64, 128, 512], P('lat', 'lon')
- key_grad: bfloat16 [64, 128, 512], P('lat', 'lon')
- value_grad: bfloat16 [64, 128, 512], P('lat', 'lon')
- weight_grad: bfloat16 [512, 1024], replicated
- bias_grad: float32 [8, 13, 13], replicated
The draws below stay inside these ranges and needn't reach their ends.
All inputs are finite; a program needn't handle non-finite values.
Results may differ from the reference program's by a relative error of at most 0.007.
Values may be sent and summed in bfloat16 or wider, within the bound.
No kernel may reach another device: no remote copies, remote signals or barrier semaphores. Data moves between devices by JAX's collectives and lax.ppermute only.
A program may use at most 128 MiB of HBM per device.

```python
import jax
import jax.numpy as jnp
from jax import lax

D = 1024
HEADS = 8
HEAD = 64
RAD = 6
NLAT = 64
NLON = 128


def draw_queries(key, part):
    drawn = jnp.clip(jax.random.normal(jax.random.fold_in(key, 1), (NLAT, NLON, HEADS * HEAD), jnp.float32), -6.0, 6.0)
    return drawn.astype(jnp.bfloat16)


def draw_keys(key, part):
    drawn = jnp.clip(jax.random.normal(jax.random.fold_in(key, 2), (NLAT, NLON, HEADS * HEAD), jnp.float32), -6.0, 6.0)
    return drawn.astype(jnp.bfloat16)


def shard_levels(rng, shape, shards, smallest, top_value):
    factor_of = 1.0
    for position, blocks in shards:
        steps = jax.random.uniform(jax.random.fold_in(jax.random.fold_in(rng, 6), position), (blocks,), jnp.float32, smallest / len(shards), top_value / len(shards))
        factor_of = factor_of * jnp.repeat(jnp.exp(steps), shape[position] // blocks).reshape((-1,) + (1,) * (len(shape) - 1 - position))
    return factor_of


def noise(stream_key, dims, width, bound, shards=(), kind=jnp.bfloat16):
    values = jax.random.normal(stream_key, dims, jnp.float32) * width
    if len(shards) > 0:
        values = shard_levels(stream_key, dims, shards, -0.22, 0.18) * values
    return jnp.clip(values, min=-bound, max=bound).astype(kind)


def setup_inputs(seed: int = 0) -> dict:
    key_list = jax.random.split(jax.random.key(seed), 7)
    return {
        "queries": draw_queries(jax.random.fold_in(key_list[6], 71), 0),
        "keys": draw_keys(jax.random.fold_in(key_list[6], 71), 0),
        "values": noise(key_list[2], (NLAT, NLON, HEADS * HEAD), 3.0, 16.0, ((0, 4), (1, 8))),
        "rel_bias": noise(key_list[3], (HEADS, 2 * RAD + 1, 2 * RAD + 1), 1.0, 4.0, (), jnp.float32),
        "out_weight": noise(key_list[4], (HEADS * HEAD, D), (HEADS * HEAD) ** -0.5, 0.25),
        "cotangent": noise(key_list[5], (NLAT, NLON, D), 3.0, 16.0, ((0, 4), (1, 8))),
    }


def pad_field(field):
    wrapped = jnp.concatenate([field[:, NLON - RAD:], field, field[:, :RAD]], axis=1)
    return jnp.pad(wrapped, ((RAD, RAD), (0, 0), (0, 0)))


def split_heads(field):
    return field.reshape(field.shape[0], field.shape[1], HEADS, HEAD).transpose(2, 0, 1, 3)


def merge_heads(field):
    return field.transpose(1, 2, 0, 3).reshape(NLAT, NLON, HEADS * HEAD)


def window_at(padded, offset):
    span = 2 * RAD + 1
    start = (offset // span, offset % span, jnp.zeros((), jnp.int32))
    return lax.dynamic_slice(padded, start, (NLAT, NLON, HEAD))


def offsets_all():
    span = 2 * RAD + 1
    return jnp.arange(span * span, dtype=jnp.int32)


def head_probs(query_one, key_pad, bias_one):
    span = 2 * RAD + 1
    scale = HEAD ** -0.5
    rows = jnp.arange(NLAT, dtype=jnp.int32)
    query_wide = query_one.astype(jnp.float32)

    def score_at(offset):
        row_off = offset // span
        col_off = offset % span
        shifted = window_at(key_pad, offset).astype(jnp.float32)
        scores = jnp.sum(query_wide * shifted, -1) * scale + bias_one[row_off, col_off]
        inside = (rows + row_off - RAD >= 0) & (rows + row_off - RAD < NLAT)
        return jnp.where(inside[:, None], scores, -jnp.inf)

    scores = lax.map(score_at, offsets_all())
    return jax.nn.softmax(scores, axis=0)


def forward_head(items):
    query_one, key_pad, value_pad, bias_one = items
    rounded = head_probs(query_one, key_pad, bias_one).astype(jnp.bfloat16)

    def accumulate(total, offset):
        shifted = window_at(value_pad, offset).astype(jnp.float32)
        return total + rounded[offset].astype(jnp.float32)[:, :, None] * shifted, None

    total, unused = lax.scan(accumulate, jnp.zeros((NLAT, NLON, HEAD), jnp.float32), offsets_all())
    return total


def fold_margins(padded):
    inner = padded[RAD:RAD + NLAT]
    main = inner[:, RAD:RAD + NLON]
    main = main.at[:, NLON - RAD:].add(inner[:, :RAD])
    main = main.at[:, :RAD].add(inner[:, RAD + NLON:])
    return main


def backward_head(items):
    query_one, key_pad, value_pad, grad_one, bias_one = items
    span = 2 * RAD + 1
    scale = HEAD ** -0.5
    probs = head_probs(query_one, key_pad, bias_one)
    rounded = probs.astype(jnp.bfloat16)
    grad_wide = grad_one.astype(jnp.float32)
    query_wide = query_one.astype(jnp.float32)

    def slope_at(offset):
        return jnp.sum(grad_wide * window_at(value_pad, offset).astype(jnp.float32), -1)

    slopes = lax.map(slope_at, offsets_all())
    inner_sum = jnp.sum(probs * slopes, 0)
    score_grad = probs * (slopes - inner_sum)
    bias_part = jnp.sum(score_grad, axis=(1, 2)).reshape(span, span)
    score_round = score_grad.astype(jnp.bfloat16)
    pad_shape = (NLAT + 2 * RAD, NLON + 2 * RAD, HEAD)

    def spread(carry, offset):
        query_acc, key_acc, value_acc = carry
        start = (offset // span, offset % span, jnp.zeros((), jnp.int32))
        size = (NLAT, NLON, HEAD)
        weight_score = score_round[offset].astype(jnp.float32)[:, :, None]
        weight_prob = rounded[offset].astype(jnp.float32)[:, :, None]
        query_acc = query_acc + weight_score * window_at(key_pad, offset).astype(jnp.float32)
        key_acc = lax.dynamic_update_slice(key_acc, lax.dynamic_slice(key_acc, start, size) + weight_score * query_wide, start)
        value_acc = lax.dynamic_update_slice(value_acc, lax.dynamic_slice(value_acc, start, size) + weight_prob * grad_wide, start)
        return (query_acc, key_acc, value_acc), None

    start_carry = (jnp.zeros((NLAT, NLON, HEAD), jnp.float32), jnp.zeros(pad_shape, jnp.float32), jnp.zeros(pad_shape, jnp.float32))
    (query_acc, key_acc, value_acc), unused = lax.scan(spread, start_carry, offsets_all())
    return query_acc * scale, fold_margins(key_acc) * scale, fold_margins(value_acc), bias_part


def reference(queries, keys, values, rel_bias, out_weight, cotangent):
    query_heads = split_heads(queries)
    key_heads = split_heads(pad_field(keys))
    value_heads = split_heads(pad_field(values))
    mixed = lax.map(forward_head, (query_heads, key_heads, value_heads, rel_bias))
    attended = merge_heads(mixed).reshape(NLAT * NLON, HEADS * HEAD).astype(jnp.bfloat16)
    block_out = jnp.dot(attended, out_weight, preferred_element_type=jnp.float32).astype(jnp.bfloat16).reshape(NLAT, NLON, D)
    grad_rows = cotangent.reshape(NLAT * NLON, D)
    attended_grad = lax.dot_general(grad_rows, out_weight, (((1,), (1,)), ((), ())), preferred_element_type=jnp.float32).astype(jnp.bfloat16)
    norm_factor = (NLAT * NLON) ** -0.5
    weight_sum = lax.dot_general(attended, grad_rows, (((0,), (0,)), ((), ())), preferred_element_type=jnp.float32)
    weight_grad = (weight_sum * norm_factor).astype(jnp.bfloat16)
    grad_heads = split_heads(attended_grad.reshape(NLAT, NLON, HEADS * HEAD))
    query_part, key_part, value_part, bias_part = lax.map(backward_head, (query_heads, key_heads, value_heads, grad_heads, rel_bias))
    query_grad = merge_heads(query_part).astype(jnp.bfloat16)
    key_grad = merge_heads(key_part).astype(jnp.bfloat16)
    value_grad = merge_heads(value_part).astype(jnp.bfloat16)
    return block_out, query_grad, key_grad, value_grad, weight_grad, bias_part * norm_factor
```

```python
import functools

import jax
import jax.numpy as jnp
from jax import lax
from jax.experimental import pallas as pl
from jax.experimental.pallas import tpu as pltpu
from jax.sharding import PartitionSpec as P

RAD = 6
SPAN = 2 * RAD + 1
TILE = 4
GROUP = 4
NEG = -1e30
NT = (((1,), (1,)), ((), ()))
F32 = jnp.float32
BF16 = jnp.bfloat16


def dot(a, b):
    return jnp.dot(a, b, preferred_element_type=F32)


def dot_nt(a, b):
    return lax.dot_general(a, b, NT, preferred_element_type=F32)


def head_of_lane(shape, axis, head_size):
    return lax.broadcasted_iota(jnp.int32, shape, axis) // head_size


def spread_heads(tile, cols, head_size):
    lane = head_of_lane((cols, tile.shape[1]), 1, head_size)
    zero = jnp.zeros((cols, tile.shape[1]), tile.dtype)
    parts = []
    for i in range(TILE):
        rows = tile[i * cols : (i + 1) * cols]
        for h in range(GROUP):
            parts.append(jnp.where(lane == h, rows, zero))
    return jnp.concatenate(parts, 0)


def head_mask(cols, head_size):
    shape = (GROUP * head_size, TILE * GROUP * cols)
    feature = lax.broadcasted_iota(jnp.int32, shape, 0) // head_size
    column = (lax.broadcasted_iota(jnp.int32, shape, 1) // cols) % GROUP
    return feature == column


def picker(cols):
    shape = (TILE * cols, TILE * GROUP * cols)
    row = lax.broadcasted_iota(jnp.int32, shape, 0)
    col = lax.broadcasted_iota(jnp.int32, shape, 1)
    same = (row // cols == col // (GROUP * cols)) & (row % cols == col % cols)
    return same.astype(F32).astype(BF16)


def scores_of(k_win, q_bd, bias, first_row, rows_all, cols_pad):
    shape = (k_win.shape[0], q_bd.shape[0])
    row = first_row + lax.broadcasted_iota(jnp.int32, shape, 0) // cols_pad
    keep = (row >= 0) & (row < rows_all)
    return jnp.where(keep, dot_nt(k_win, q_bd) + bias, NEG)


def fwd_kernel(sizes, lat_ref, q_ref, k_ref, v_ref, bias_ref, out_ref, m_ref, l_ref, vt_ref):
    lat_dev, cols, cols_pad, head_size, rows_all = sizes
    scale = head_size ** (-0.5)
    vt_ref[...] = v_ref[...].T
    mask = head_mask(cols, head_size)
    pick = picker(cols)
    win = (TILE + 2 * RAD) * cols_pad
    for t in range(lat_dev // TILE):
        lo = t * TILE * cols_pad
        qs = pl.ds(t * TILE * cols, TILE * cols)
        q_bd = spread_heads(q_ref[qs, :] * jnp.asarray(scale, BF16), cols, head_size)
        first = lat_ref[0] * lat_dev + t * TILE - RAD
        st = scores_of(k_ref[pl.ds(lo, win), :], q_bd, bias_ref[...], first, rows_all, cols_pad)
        m = jnp.max(st, 0, keepdims=True)
        e = jnp.exp(st - m)
        total = jnp.sum(e, 0, keepdims=True)
        p = (e * (1.0 / total)).astype(BF16)
        ot = dot(vt_ref[:, pl.ds(lo, win)], p)
        ot = jnp.where(mask, ot, 0.0).astype(BF16)
        out_ref[qs, :] = dot_nt(pick, ot).astype(BF16)
        m_ref[0, t : t + 1, :] = m
        l_ref[0, t : t + 1, :] = 1.0 / total


def bwd_kernel(
    sizes, lat_ref, q_ref, g_ref, k_ref, v_ref, bias_ref, m_ref, l_ref,
    dq_ref, dk_ref, dv_ref, db_ref, kt_ref,
):
    lat_dev, cols, cols_pad, head_size, rows_all = sizes
    scale = head_size ** (-0.5)
    kt_ref[...] = k_ref[...].T
    mask = head_mask(cols, head_size)
    pick = picker(cols)
    win = (TILE + 2 * RAD) * cols_pad
    dk_ref[...] = jnp.zeros_like(dk_ref)
    dv_ref[...] = jnp.zeros_like(dv_ref)
    for t in range(lat_dev // TILE):
        lo = t * TILE * cols_pad
        qs = pl.ds(t * TILE * cols, TILE * cols)
        ws = pl.ds(lo, win)
        q_bd = spread_heads(q_ref[qs, :] * jnp.asarray(scale, BF16), cols, head_size)
        g_bd = spread_heads(g_ref[qs, :], cols, head_size)
        first = lat_ref[0] * lat_dev + t * TILE - RAD
        st = scores_of(k_ref[ws, :], q_bd, bias_ref[...], first, rows_all, cols_pad)
        p = jnp.exp(st - m_ref[0, t : t + 1, :]) * l_ref[0, t : t + 1, :]
        slope = dot_nt(v_ref[ws, :], g_bd)
        inner = jnp.sum(p * slope, 0, keepdims=True)
        sg = p * (slope - inner)
        if t == 0:
            db_ref[...] = sg
        else:
            db_ref[...] += sg
        sgb = sg.astype(BF16)
        dqt = jnp.where(mask, dot(kt_ref[:, ws], sgb) * scale, 0.0).astype(BF16)
        dq_ref[qs, :] = dot_nt(pick, dqt).astype(BF16)
        dk_ref[ws, :] += dot(sgb, q_bd)
        dv_ref[ws, :] += dot(p.astype(BF16), g_bd)


def bits_of(mesh_shape):
    order = []
    for axis in ("lat", "lon"):
        n = mesh_shape[axis]
        bit = 1
        while bit < n:
            order.append((axis, bit, n))
            bit *= 2
    return order


def swap(x, axis, bit, n):
    return lax.ppermute(x, axis, [(i, i ^ bit) for i in range(n)])


def split_f32(x):
    hi = lax.reduce_precision(x, 8, 7)
    return hi.astype(BF16), (x - hi).astype(BF16)


def reduce_all(weight, bias, mesh_shape):
    order = bits_of(mesh_shape)
    part = weight
    for axis, bit, n in order[:-1]:
        mine = (lax.axis_index(axis) // bit) % 2
        half = part.shape[0] // 2
        keep = lax.dynamic_slice_in_dim(part, mine * half, half, 0)
        send = lax.dynamic_slice_in_dim(part, (1 - mine) * half, half, 0)
        got = swap(send, axis, bit, n)
        part = (keep.astype(F32) + got.astype(F32)).astype(BF16)
    nb = bias.shape[0]
    for step, (axis, bit, n) in enumerate(order[::-1]):
        rows = part.shape[0]
        hi, lo = split_f32(bias)
        got = swap(jnp.concatenate([hi, lo, part], 0), axis, bit, n)
        bias = bias + (got[:nb].astype(F32) + got[nb : 2 * nb].astype(F32))
        other = got[2 * nb :]
        if step == 0:
            part = part.astype(F32) + other.astype(F32)
            part = part.astype(BF16)
        else:
            mine = (lax.axis_index(axis) // bit) % 2
            both = jnp.zeros((2 * rows, part.shape[1]), BF16)
            both = lax.dynamic_update_slice_in_dim(both, part, mine * rows, 0)
            part = lax.dynamic_update_slice_in_dim(both, other, (1 - mine) * rows, 0)
    return part, bias


def bias_tables(rel_bias, cols, cols_pad):
    heads = rel_bias.shape[0]
    slot = jnp.arange(cols_pad, dtype=jnp.int32)
    pos = jnp.where(
        slot < cols,
        slot + RAD,
        jnp.where(slot < cols + RAD, slot - cols, jnp.where(slot < cols + 2 * RAD, slot, -1000)),
    )
    offset = pos[:, None] - jnp.arange(cols, dtype=jnp.int32)[None, :]
    hot = (offset[None] == jnp.arange(SPAN, dtype=jnp.int32)[:, None, None]).astype(F32)
    table = jnp.einsum("hab,blj->alhj", rel_bias, hot, precision=lax.Precision.HIGHEST)
    inside = (offset >= 0) & (offset < SPAN)
    table = jnp.where(inside[None, :, None, :], table, NEG)
    table = table.reshape(SPAN, cols_pad, heads // GROUP, 1, GROUP * cols)
    edge = TILE - 1
    table = jnp.pad(table, ((edge, edge), (0, 0), (0, 0), (0, 0), (0, 0)), constant_values=NEG)
    rows = TILE + 2 * RAD
    full = jnp.concatenate([table[edge - i : edge - i + rows] for i in range(TILE)], 3)
    return full.reshape(rows * cols_pad, heads * TILE * cols), hot


def shards(mesh_shape, queries, keys, values, rel_bias, out_weight, cotangent):
    lat_dev, lon_dev, width = queries.shape
    heads = rel_bias.shape[0]
    head_size = width // heads
    groups = heads // GROUP
    lanes = GROUP * head_size
    n_lat, n_lon = mesh_shape["lat"], mesh_shape["lon"]
    cols_pad = 32
    outer_lat = lat_dev + 2 * RAD
    tokens = lat_dev * lon_dev
    norm_factor = (tokens * n_lat * n_lon) ** (-0.5)
    east = [(i, (i + 1) % n_lon) for i in range(n_lon)]
    west = [(i, (i - 1) % n_lon) for i in range(n_lon)]
    down = [(i, i + 1) for i in range(n_lat - 1)]
    up = [(i + 1, i) for i in range(n_lat - 1)]

    paired = jnp.concatenate((keys, values), 2)
    from_west = lax.ppermute(paired[:, lon_dev - RAD :], "lon", east)
    from_east = lax.ppermute(paired[:, :RAD], "lon", west)
    fill = jnp.zeros((lat_dev, cols_pad - lon_dev - 2 * RAD, 2 * width), BF16)
    wide = jnp.concatenate((paired, from_west, from_east, fill), 1)
    from_above = lax.ppermute(wide[lat_dev - RAD :], "lat", down)
    from_below = lax.ppermute(wide[:RAD], "lat", up)
    outer = jnp.concatenate((from_above, wide, from_below), 0)
    outer = outer.reshape(outer_lat * cols_pad, 2 * width)
    bias_full, hot = bias_tables(rel_bias, lon_dev, cols_pad)

    q_flat = queries.reshape(tokens, width)
    cot = cotangent.reshape(tokens, cotangent.shape[2])
    attended_grad = lax.dot_general(cot, out_weight, NT, preferred_element_type=F32).astype(BF16)
    lat_index = lax.axis_index("lat").astype(jnp.int32).reshape(1)

    sizes = (lat_dev, lon_dev, cols_pad, head_size, lat_dev * n_lat)
    win = (TILE + 2 * RAD) * cols_pad
    tiles = lat_dev // TILE
    lanes_q = TILE * GROUP * lon_dev
    n_keys = outer_lat * cols_pad
    smem = pl.BlockSpec(memory_space=pltpu.SMEM)
    tok_spec = pl.BlockSpec((tokens, lanes), lambda g: (0, g))
    k_spec = pl.BlockSpec((n_keys, lanes), lambda g: (0, g))
    v_spec = pl.BlockSpec((n_keys, lanes), lambda g: (0, g + groups))
    b_spec = pl.BlockSpec((win, lanes_q), lambda g: (0, g))
    s_spec = pl.BlockSpec((1, tiles, lanes_q), lambda g: (g, 0, 0))
    params = pltpu.CompilerParams(vmem_limit_bytes=40 << 20)
    attended, m, inv = pl.pallas_call(
        functools.partial(fwd_kernel, sizes),
        grid=(groups,),
        in_specs=[smem, tok_spec, k_spec, v_spec, b_spec],
        out_specs=[tok_spec, s_spec, s_spec],
        out_shape=[
            jax.ShapeDtypeStruct((tokens, width), BF16),
            jax.ShapeDtypeStruct((groups, tiles, lanes_q), F32),
            jax.ShapeDtypeStruct((groups, tiles, lanes_q), F32),
        ],
        scratch_shapes=[pltpu.VMEM((lanes, n_keys), BF16)],
        compiler_params=params,
        name="attend_fwd",
    )(lat_index, q_flat, outer, outer, bias_full)

    weight_local = lax.dot_general(
        attended, cot, (((0,), (0,)), ((), ())), preferred_element_type=F32
    ).astype(BF16)
    block_out = dot(attended, out_weight).astype(BF16)

    query_grad, dk, dv, db = pl.pallas_call(
        functools.partial(bwd_kernel, sizes),
        grid=(groups,),
        in_specs=[smem, tok_spec, tok_spec, k_spec, v_spec, b_spec, s_spec, s_spec],
        out_specs=[tok_spec, k_spec, k_spec, b_spec],
        out_shape=[
            jax.ShapeDtypeStruct((tokens, width), BF16),
            jax.ShapeDtypeStruct((n_keys, width), F32),
            jax.ShapeDtypeStruct((n_keys, width), F32),
            jax.ShapeDtypeStruct((win, groups * lanes_q), F32),
        ],
        scratch_shapes=[pltpu.VMEM((lanes, n_keys), BF16)],
        compiler_params=params,
        name="attend_bwd",
    )(lat_index, q_flat, attended_grad, outer, outer, bias_full, m, inv)

    terms = jnp.concatenate((dk, dv), 1).reshape(outer_lat, cols_pad, 2 * width)
    get_below = lax.ppermute(terms[:RAD].astype(BF16), "lat", up)
    get_above = lax.ppermute(terms[outer_lat - RAD :].astype(BF16), "lat", down)
    middle = terms[RAD : RAD + lat_dev]
    middle = middle.at[lat_dev - RAD :].add(get_below.astype(F32))
    middle = middle.at[:RAD].add(get_above.astype(F32))
    to_west = middle[:, lon_dev : lon_dev + RAD].astype(BF16)
    to_east = middle[:, lon_dev + RAD : lon_dev + 2 * RAD].astype(BF16)
    get_east = lax.ppermute(to_west, "lon", west)
    get_west = lax.ppermute(to_east, "lon", east)
    center = middle[:, :lon_dev]
    center = center.at[:, lon_dev - RAD :].add(get_east.astype(F32))
    center = center.at[:, :RAD].add(get_west.astype(F32))
    key_grad = center[:, :, :width].astype(BF16)
    value_grad = center[:, :, width:].astype(BF16)

    db = db.reshape(TILE + 2 * RAD, cols_pad, groups, TILE, GROUP * lon_dev)
    db = sum(db[i : i + SPAN, :, :, i] for i in range(TILE))
    db = db.reshape(SPAN, cols_pad, heads, lon_dev)
    bias_local = jnp.einsum("alhj,blj->hab", db, hot, precision=lax.Precision.HIGHEST)
    flat = bias_local.reshape(-1)
    packed = jnp.pad(flat, (0, 8 * 1024 - flat.shape[0])).reshape(8, 1024)
    weight_total, bias_total = reduce_all(weight_local, packed, mesh_shape)
    weight_grad = (weight_total.astype(F32) * norm_factor).astype(BF16)
    bias_grad = bias_total.reshape(-1)[: flat.shape[0]].reshape(rel_bias.shape) * norm_factor
    return (
        block_out.reshape(lat_dev, lon_dev, -1),
        query_grad.reshape(lat_dev, lon_dev, width),
        key_grad,
        value_grad,
        weight_grad,
        bias_grad,
    )


def solution(mesh):
    spec = P("lat", "lon", None)
    return jax.shard_map(
        functools.partial(shards, dict(mesh.shape)),
        mesh=mesh,
        in_specs=(spec, spec, spec, P(), P(), spec),
        out_specs=(spec, spec, spec, spec, P(), P()),
        check_vma=False,
    )
```

```python
import functools

import jax
import jax.numpy as jnp
from jax import lax
from jax.experimental import pallas as pl
from jax.experimental.pallas import tpu as pltpu
from jax.sharding import PartitionSpec as P

RAD = 6
SPAN = 2 * RAD + 1
TILE = 4
GROUP = 4
NEG = -1e30
NT = (((1,), (1,)), ((), ()))
F32 = jnp.float32
BF16 = jnp.bfloat16
SLOTS = 16
CORNER = 80


def dot(a, b):
    return jnp.dot(a, b, preferred_element_type=F32)


def dot_nt(a, b):
    return lax.dot_general(a, b, NT, preferred_element_type=F32)


def iota2(shape, axis):
    return lax.broadcasted_iota(jnp.int32, shape, axis)


def hot(mask):
    return mask.astype(F32).astype(BF16)


def spread_heads(tile, cols, head_size):
    lane = iota2((cols, tile.shape[1]), 1) // head_size
    zero = jnp.zeros((cols, tile.shape[1]), tile.dtype)
    parts = []
    for i in range(TILE):
        rows = tile[i * cols : (i + 1) * cols]
        for h in range(GROUP):
            parts.append(jnp.where(lane == h, rows, zero))
    return jnp.concatenate(parts, 0)


def head_mask(cols, head_size):
    shape = (GROUP * head_size, TILE * GROUP * cols)
    return iota2(shape, 0) // head_size == (iota2(shape, 1) // cols) % GROUP


def picker(cols):
    shape = (TILE * cols, TILE * GROUP * cols)
    row = iota2(shape, 0)
    col = iota2(shape, 1)
    return hot((row // cols == col // (GROUP * cols)) & (row % cols == col % cols))


def row_keep(first_row, rows_all, win, lanes, cols_pad):
    row = first_row + iota2((win, lanes), 0) // cols_pad
    return (row >= 0) & (row < rows_all)


def take_cols(rows, cols, first):
    shape = (rows * RAD, rows * cols)
    n = iota2(shape, 0)
    return hot(iota2(shape, 1) == (n // RAD) * cols + first + n % RAD)


def put_cols(rows, cols, first):
    shape = (rows * cols, rows * RAD)
    n = iota2(shape, 1)
    return hot(iota2(shape, 0) == (n // RAD) * cols + first + n % RAD)


def put_corner(cols):
    shape = (RAD * cols, CORNER)
    n = iota2(shape, 1)
    half = RAD * RAD
    m = jnp.where(n < half, n, n - half)
    target = (m // RAD) * cols + m % RAD + jnp.where(n < half, 0, RAD)
    return hot((iota2(shape, 0) == target) & (n < 2 * half))


def pack_kernel(rows, cols, k_ref, v_ref, east_ref, west_ref, down_ref, up_ref):
    pick_east = take_cols(rows, cols, cols - RAD)
    pick_west = take_cols(rows, cols, 0)
    edge = RAD * cols
    for i, ref in enumerate((k_ref, v_ref)):
        x = ref[...]
        east_ref[i] = dot(pick_east, x).astype(BF16)
        west_ref[i] = dot(pick_west, x).astype(BF16)
        down_ref[i] = x[(rows - RAD) * cols :]
        up_ref[i] = x[:edge]


def corner_kernel(rows, w_ref, e_ref, down_ref, up_ref):
    half = RAD * RAD
    shape = (CORNER, rows * RAD)
    n = iota2(shape, 0)
    src = iota2(shape, 1)
    for ref, first in ((down_ref, (rows - RAD) * RAD), (up_ref, 0)):
        pick_w = hot((src == first + n) & (n < half))
        pick_e = hot((src == first + n - half) & (n >= half) & (n < 2 * half))
        for i in range(2):
            ref[i] = (dot(pick_w, w_ref[i]) + dot(pick_e, e_ref[i])).astype(BF16)


def table_kernel(cols, cols_pad, rel_ref, out_ref, c_ref, r_ref):
    lanes = rel_ref.shape[1]
    half = lanes // 2
    shape = (cols_pad, lanes)
    offset = slot_offset(shape, cols)
    inside = (offset >= 0) & (offset < SPAN)
    for a in range(SPAN):
        tile = jnp.full(shape, NEG, F32)
        for b in range(SPAN):
            n = a * SPAN + b
            tile = jnp.where(offset == b, rel_ref[n : n + 1, :], tile)
        tile = jnp.where(inside, tile, NEG)
        c_ref[a] = tile
        r_ref[a] = pltpu.roll(tile, half, 1)
    low = iota2(shape, 1) < half
    blank = jnp.full(shape, NEG, F32)
    for g in range(2):
        first, second = (c_ref, r_ref) if g == 0 else (r_ref, c_ref)
        for pair in range(TILE // 2):
            i = 2 * pair
            lo = (g * TILE // 2 + pair) * lanes
            for k in range(TILE + 2 * RAD):
                a = k - i
                one = first[a] if 0 <= a < SPAN else blank
                two = second[a - 1] if 0 <= a - 1 < SPAN else blank
                out_ref[k * cols_pad : (k + 1) * cols_pad, lo : lo + lanes] = jnp.where(
                    low, one, two
                )


def slot_offset(shape, cols):
    slot = iota2(shape, 0)
    pos = jnp.where(slot < cols, slot + RAD, jnp.where(slot < cols + RAD, slot - cols, slot))
    pos = jnp.where(slot < cols + 2 * RAD, pos, -1000)
    return pos - iota2(shape, 1) % cols


def assemble(out_ref, i, rows, cols, cols_pad, own, refs):
    w_ref, e_ref, ao_ref, ac_ref, bo_ref, bc_ref = refs
    side = dot(put_cols(rows, SLOTS, 0), w_ref[i]) + dot(put_cols(rows, SLOTS, RAD), e_ref[i])
    side = side.astype(BF16)
    for r in range(rows):
        lo = (RAD + r) * cols_pad
        out_ref[lo : lo + cols, :] = own[r * cols : (r + 1) * cols, :]
        out_ref[lo + cols : lo + cols + SLOTS, :] = side[r * SLOTS : (r + 1) * SLOTS]
    put = put_corner(SLOTS)
    for first, o_ref, c_ref in ((0, ao_ref, ac_ref), (RAD + rows, bo_ref, bc_ref)):
        side = dot(put, c_ref[i]).astype(BF16)
        for r in range(RAD):
            lo = (first + r) * cols_pad
            out_ref[lo : lo + cols, :] = o_ref[i, r * cols : (r + 1) * cols, :]
            out_ref[lo + cols : lo + cols + SLOTS, :] = side[r * SLOTS : (r + 1) * SLOTS]


def fwd_kernel(
    sizes, info_ref, q_ref, k_ref, v_ref, w_ref, e_ref, ao_ref, ac_ref, bo_ref, bc_ref,
    bias_ref, cot_ref, out_ref, m_ref, l_ref, weight_ref, ko_ref, vo_ref, vt_ref, at_ref,
):
    lat_dev, cols, cols_pad, head_size, rows_all = sizes
    scale = head_size ** (-0.5)
    refs = (w_ref, e_ref, ao_ref, ac_ref, bo_ref, bc_ref)
    assemble(ko_ref, 0, lat_dev, cols, cols_pad, k_ref, refs)
    assemble(vo_ref, 1, lat_dev, cols, cols_pad, v_ref, refs)
    vt_ref[...] = vo_ref[...].T
    mask = head_mask(cols, head_size)
    pick = picker(cols)
    win = (TILE + 2 * RAD) * cols_pad
    for t in range(lat_dev // TILE):
        lo = t * TILE * cols_pad
        qs = pl.ds(t * TILE * cols, TILE * cols)
        q_bd = spread_heads(q_ref[qs, :] * jnp.asarray(scale, BF16), cols, head_size)
        first = info_ref[1] * lat_dev + t * TILE - RAD
        keep = row_keep(first, rows_all, win, q_bd.shape[0], cols_pad)
        st = jnp.where(keep, dot_nt(ko_ref[pl.ds(lo, win), :], q_bd) + bias_ref[...], NEG)
        m = jnp.max(st, 0, keepdims=True)
        e = jnp.exp(st - m)
        inv = 1.0 / jnp.sum(e, 0, keepdims=True)
        p = (e * inv).astype(BF16)
        ot = dot(vt_ref[:, pl.ds(lo, win)], p)
        ot = jnp.where(mask, ot, 0.0).astype(BF16)
        out_ref[qs, :] = dot_nt(pick, ot).astype(BF16)
        m_ref[t : t + 1, :] = m
        l_ref[t : t + 1, :] = inv
    at_ref[...] = out_ref[...].T
    weight_ref[...] = dot(at_ref[...], cot_ref[...]).astype(weight_ref.dtype)


def bwd_kernel(
    sizes, info_ref, q_ref, g_ref, k_ref, v_ref, w_ref, e_ref, ao_ref, ac_ref, bo_ref, bc_ref,
    bias_ref, ms_ref, ls_ref, mk_ref, lk_ref,
    dq_ref, top_ref, bot_ref, mid_ref, side_ref, x_ref,
    ko_ref, vo_ref, kt_ref, dk_ref, dv_ref, db_ref,
):
    lat_dev, cols, cols_pad, head_size, rows_all = sizes
    scale = head_size ** (-0.5)
    refs = (w_ref, e_ref, ao_ref, ac_ref, bo_ref, bc_ref)
    assemble(ko_ref, 0, lat_dev, cols, cols_pad, k_ref, refs)
    assemble(vo_ref, 1, lat_dev, cols, cols_pad, v_ref, refs)
    kt_ref[...] = ko_ref[...].T
    mask = head_mask(cols, head_size)
    pick = picker(cols)
    win = (TILE + 2 * RAD) * cols_pad
    sent = pl.program_id(0) == info_ref[0]
    dk_ref[...] = jnp.zeros_like(dk_ref)
    dv_ref[...] = jnp.zeros_like(dv_ref)
    for t in range(lat_dev // TILE):
        lo = t * TILE * cols_pad
        qs = pl.ds(t * TILE * cols, TILE * cols)
        ws = pl.ds(lo, win)
        q_bd = spread_heads(q_ref[qs, :] * jnp.asarray(scale, BF16), cols, head_size)
        g_bd = spread_heads(g_ref[qs, :], cols, head_size)
        first = info_ref[1] * lat_dev + t * TILE - RAD
        keep = row_keep(first, rows_all, win, q_bd.shape[0], cols_pad)
        st = jnp.where(keep, dot_nt(ko_ref[ws, :], q_bd) + bias_ref[...], NEG)
        m = jnp.where(sent, ms_ref[t : t + 1, :], mk_ref[t : t + 1, :])
        inv = jnp.where(sent, ls_ref[t : t + 1, :], lk_ref[t : t + 1, :])
        p = jnp.exp(st - m) * inv
        slope = dot_nt(vo_ref[ws, :], g_bd)
        inner = jnp.sum(p * slope, 0, keepdims=True)
        sg = p * (slope - inner)
        if t == 0:
            db_ref[...] = sg
        else:
            db_ref[...] += sg
        sgb = sg.astype(BF16)
        dqt = jnp.where(mask, dot(kt_ref[:, ws], sgb) * scale, 0.0).astype(BF16)
        dq_ref[qs, :] = dot_nt(pick, dqt).astype(BF16)
        dk_ref[ws, :] += dot(sgb, q_bd)
        dv_ref[ws, :] += dot(p.astype(BF16), g_bd)
    edge = RAD * cols_pad
    for i, ref in enumerate((dk_ref, dv_ref)):
        top_ref[i] = ref[:edge, :].astype(BF16)
        bot_ref[i] = ref[edge + lat_dev * cols_pad :, :].astype(BF16)
        for r in range(lat_dev):
            lo = (RAD + r) * cols_pad
            mid_ref[i, r * cols : (r + 1) * cols, :] = ref[lo : lo + cols, :]
            side_ref[i, r * SLOTS : (r + 1) * SLOTS, :] = ref[lo + cols : lo + cols_pad, :]
    half = GROUP * cols
    low = iota2((cols_pad, 2 * half), 1) < half
    for a in range(SPAN):
        total = jnp.zeros((cols_pad, 2 * half), F32)
        for pair in range(TILE // 2):
            i = 2 * pair
            lanes = slice(pair * 2 * half, (pair + 1) * 2 * half)
            one = db_ref[(a + i) * cols_pad : (a + i + 1) * cols_pad, lanes]
            two = db_ref[(a + i + 1) * cols_pad : (a + i + 2) * cols_pad, lanes]
            total = total + jnp.where(low, one, two)
        x_ref[0, a * cols_pad : (a + 1) * cols_pad, :] = total


def bias_kernel(cols, cols_pad, x_ref, out_ref, z_ref):
    lanes = x_ref.shape[2]
    half = lanes // 2
    shape = (cols_pad, lanes)
    low = iota2(shape, 1) < half
    offset = slot_offset(shape, cols)
    z_ref[...] = jnp.zeros_like(z_ref)
    for a in range(SPAN):
        rows = slice(a * cols_pad, (a + 1) * cols_pad)
        one = x_ref[0, rows, :]
        two = x_ref[1, rows, :]
        both = jnp.where(low, one + pltpu.roll(one, half, 1), two + pltpu.roll(two, half, 1))
        for b in range(SPAN):
            n = a * SPAN + b
            z_ref[n : n + 1, :] = jnp.sum(jnp.where(offset == b, both, 0.0), 0, keepdims=True)
    heads = out_ref.shape[0]
    pick = (iota2((heads, lanes), 1) // cols == iota2((heads, lanes), 0)).astype(F32)
    out_ref[...] = lax.dot_general(
        pick, z_ref[...], NT, precision=lax.Precision.HIGHEST, preferred_element_type=F32
    )


def lat_terms(ref, i, rows, cols, cols_pad, first):
    parts = []
    for r in range(RAD):
        lo = r * cols_pad + first
        parts.append(ref[i, lo : lo + cols, :])
    return jnp.concatenate(parts, 0).astype(F32)


def side_kernel(rows, cols, cols_pad, side_ref, a_ref, b_ref, west_ref, east_ref, s_ref):
    edge = RAD * SLOTS
    pick_west = take_cols(rows, SLOTS, 0)
    pick_east = take_cols(rows, SLOTS, RAD)
    for i in range(2):
        s_ref[...] = side_ref[i]
        s_ref[:edge, :] += lat_terms(a_ref, i, rows, SLOTS, cols_pad, cols)
        s_ref[(rows - RAD) * SLOTS :, :] += lat_terms(b_ref, i, rows, SLOTS, cols_pad, cols)
        x = s_ref[...].astype(BF16)
        west_ref[i] = dot(pick_west, x).astype(BF16)
        east_ref[i] = dot(pick_east, x).astype(BF16)


def join_kernel(rows, cols, cols_pad, mid_ref, a_ref, b_ref, w_ref, e_ref, k_ref, v_ref, s_ref):
    edge = RAD * cols
    put_west = put_cols(rows, cols, 0)
    put_east = put_cols(rows, cols, cols - RAD)
    for i, out_ref in enumerate((k_ref, v_ref)):
        s_ref[...] = mid_ref[i] + dot(put_west, w_ref[i]) + dot(put_east, e_ref[i])
        s_ref[:edge, :] += lat_terms(a_ref, i, rows, cols, cols_pad, 0)
        s_ref[(rows - RAD) * cols :, :] += lat_terms(b_ref, i, rows, cols, cols_pad, 0)
        out_ref[...] = s_ref[...].astype(BF16)


def bits_of(mesh_shape):
    order = []
    for axis in ("lat", "lon"):
        n = mesh_shape[axis]
        bit = 1
        while bit < n:
            order.append((axis, bit, n))
            bit *= 2
    return order


def swap(x, axis, bit, n):
    return lax.ppermute(x, axis, [(i, i ^ bit) for i in range(n)])


def split_f32(x):
    hi = lax.reduce_precision(x, 8, 7)
    return hi.astype(BF16), lax.reduce_precision(x - hi, 8, 7).astype(BF16)


def place_kernel(info_ref, own_ref, got_ref, out_ref):
    first = pl.program_id(0) == 0

    @pl.when(first)
    def _():
        out_ref[...] = own_ref[...]

    @pl.when(jnp.logical_not(first))
    def _():
        out_ref[...] = got_ref[...]


def reduce_all(send, keep, bias, mesh_shape, norm):
    order = bits_of(mesh_shape)
    axis, bit, n = order[0]
    part = keep + swap(send, axis, bit, n).astype(F32)
    for axis, bit, n in order[1:-1]:
        mine = (lax.axis_index(axis) // bit) % 2
        half = part.shape[0] // 2
        send = lax.dynamic_slice_in_dim(part, (1 - mine) * half, half, 0).astype(BF16)
        keep = lax.dynamic_slice_in_dim(part, mine * half, half, 0)
        part = keep + swap(send, axis, bit, n).astype(F32)
    heads, count = bias.shape
    width = part.shape[1]
    part = part.astype(BF16)
    for step, (axis, bit, n) in enumerate(order[::-1]):
        rows = part.shape[0]
        hi, lo = split_f32(bias)
        small = jnp.pad(jnp.concatenate([hi, lo], 1), ((0, 0), (0, width - 2 * count)))
        got = swap(jnp.concatenate([part, small], 0), axis, bit, n)
        near = hi.astype(F32) + lo.astype(F32)
        far = got[rows:, :count].astype(F32) + got[rows:, count : 2 * count].astype(F32)
        bias = near + far
        if step == 0:
            part = ((part.astype(F32) + got[:rows].astype(F32)) * norm).astype(BF16)
            continue
        mine = (lax.axis_index(axis) // bit) % 2
        if step < len(order) - 1:
            other = got[:rows]
            part = jnp.where(
                mine == 0,
                jnp.concatenate([part, other], 0),
                jnp.concatenate([other, part], 0),
            )
            continue
        whole = pl.BlockSpec((rows, width), lambda i, s: (0, 0))
        part = pl.pallas_call(
            place_kernel,
            grid_spec=pltpu.PrefetchScalarGridSpec(
                num_scalar_prefetch=1,
                grid=(2,),
                in_specs=[whole, whole],
                out_specs=pl.BlockSpec((rows, width), lambda i, s: (i ^ s[0], 0)),
            ),
            out_shape=jax.ShapeDtypeStruct((2 * rows, width), BF16),
            name="place",
        )(mine.astype(jnp.int32).reshape(1), part, got)
    return part, bias * norm


def shards(mesh_shape, queries, keys, values, rel_bias, out_weight, cotangent):
    lat_dev, lon_dev, width = queries.shape
    heads = rel_bias.shape[0]
    head_size = width // heads
    groups = heads // GROUP
    lanes = GROUP * head_size
    model = out_weight.shape[1]
    n_lat, n_lon = mesh_shape["lat"], mesh_shape["lon"]
    cols_pad = lon_dev + SLOTS
    outer_lat = lat_dev + 2 * RAD
    tokens = lat_dev * lon_dev
    norm = (tokens * n_lat * n_lon) ** (-0.5)
    east = [(i, (i + 1) % n_lon) for i in range(n_lon)]
    west = [(i, (i - 1) % n_lon) for i in range(n_lon)]
    down = [(i, i + 1) for i in range(n_lat - 1)]
    up = [(i + 1, i) for i in range(n_lat - 1)]
    win = (TILE + 2 * RAD) * cols_pad
    tiles = lat_dev // TILE
    lanes_q = TILE * GROUP * lon_dev
    n_keys = outer_lat * cols_pad
    n_side = lat_dev * RAD
    n_edge = RAD * lon_dev
    n_strip = RAD * cols_pad

    def shape(dims, dtype=BF16):
        return jax.ShapeDtypeStruct(dims, dtype)

    q_flat = queries.reshape(tokens, width)
    k_flat = keys.reshape(tokens, width)
    v_flat = values.reshape(tokens, width)
    cot = cotangent.reshape(tokens, model)

    to_east, to_west, to_down, to_up = pl.pallas_call(
        functools.partial(pack_kernel, lat_dev, lon_dev),
        out_shape=[shape((2, n_side, width))] * 2 + [shape((2, n_edge, width))] * 2,
        name="pack",
    )(k_flat, v_flat)
    from_west = lax.ppermute(to_east, "lon", east)
    from_east = lax.ppermute(to_west, "lon", west)
    above_own = lax.ppermute(to_down, "lat", down)
    below_own = lax.ppermute(to_up, "lat", up)
    corner_down, corner_up = pl.pallas_call(
        functools.partial(corner_kernel, lat_dev),
        out_shape=[shape((2, CORNER, width))] * 2,
        name="corner",
    )(from_west, from_east)
    above_corner = lax.ppermute(corner_down, "lat", down)
    below_corner = lax.ppermute(corner_up, "lat", up)

    rel = jnp.repeat(rel_bias.reshape(heads, SPAN * SPAN).T, lon_dev, axis=1)
    table = pl.pallas_call(
        functools.partial(table_kernel, lon_dev, cols_pad),
        out_shape=shape((win, groups * lanes_q), F32),
        scratch_shapes=[pltpu.VMEM((SPAN, cols_pad, heads * lon_dev), F32)] * 2,
        name="table",
    )(rel)
    attended_grad = dot_nt(cot, out_weight).astype(BF16)

    lat_index = lax.axis_index("lat").astype(jnp.int32)
    core = lat_index % 2
    sizes = (lat_dev, lon_dev, cols_pad, head_size, lat_dev * n_lat)
    params = pltpu.CompilerParams(vmem_limit_bytes=48 << 20)

    def forward(group, dtype):
        def part(rows):
            return pl.BlockSpec((2, rows, lanes), lambda i, s: (0, 0, s[0]))

        tok = pl.BlockSpec((tokens, lanes), lambda i, s: (0, s[0]))
        whole = pl.BlockSpec((tokens, lanes), lambda i, s: (0, 0))
        stat = pl.BlockSpec((tiles, lanes_q), lambda i, s: (0, 0))
        return pl.pallas_call(
            functools.partial(fwd_kernel, sizes),
            grid_spec=pltpu.PrefetchScalarGridSpec(
                num_scalar_prefetch=1,
                grid=(1,),
                in_specs=[tok, tok, tok, part(n_side), part(n_side), part(n_edge), part(CORNER)]
                + [part(n_edge), part(CORNER), pl.BlockSpec((win, lanes_q), lambda i, s: (0, s[0]))]
                + [pl.BlockSpec((tokens, model), lambda i, s: (0, 0))],
                out_specs=[whole, stat, stat, pl.BlockSpec((lanes, model), lambda i, s: (0, 0))],
                scratch_shapes=[pltpu.VMEM((n_keys, lanes), BF16)] * 2
                + [pltpu.VMEM((lanes, n_keys), BF16), pltpu.VMEM((lanes, tokens), BF16)],
            ),
            out_shape=[shape((tokens, lanes))]
            + [shape((tiles, lanes_q), F32)] * 2
            + [shape((lanes, model), dtype)],
            compiler_params=params,
            name="attend_fwd",
        )(
            jnp.stack([group, lat_index]), q_flat, k_flat, v_flat, from_west, from_east,
            above_own, above_corner, below_own, below_corner, table, cot,
        )

    att_s, m_s, l_s, weight_s = forward(1 - core, BF16)
    att_k, m_k, l_k, weight_k = forward(core, F32)

    low = jnp.where(core == 0, att_k, att_s)
    high = jnp.where(core == 0, att_s, att_k)
    attended = jnp.concatenate([low, high], 1)
    block_out = dot(attended, out_weight).astype(BF16)

    smem = pl.BlockSpec(memory_space=pltpu.SMEM)
    tok = pl.BlockSpec((tokens, lanes), lambda g: (0, g))
    stat = pl.BlockSpec((tiles, lanes_q), lambda g: (0, 0))

    def part(rows):
        return pl.BlockSpec((2, rows, lanes), lambda g: (0, 0, g))

    query_grad, top, bottom, mid, side, folded = pl.pallas_call(
        functools.partial(bwd_kernel, sizes),
        grid=(groups,),
        in_specs=[smem, tok, tok, tok, tok, part(n_side), part(n_side), part(n_edge)]
        + [part(CORNER), part(n_edge), part(CORNER)]
        + [pl.BlockSpec((win, lanes_q), lambda g: (0, g)), stat, stat, stat, stat],
        out_specs=[tok, part(n_strip), part(n_strip), part(tokens), part(tokens)]
        + [pl.BlockSpec((1, SPAN * cols_pad, 2 * GROUP * lon_dev), lambda g: (g, 0, 0))],
        out_shape=[shape((tokens, width))]
        + [shape((2, n_strip, width))] * 2
        + [shape((2, tokens, width), F32)] * 2
        + [shape((groups, SPAN * cols_pad, 2 * GROUP * lon_dev), F32)],
        scratch_shapes=[pltpu.VMEM((n_keys, lanes), BF16)] * 2
        + [pltpu.VMEM((lanes, n_keys), BF16)]
        + [pltpu.VMEM((n_keys, lanes), F32)] * 2
        + [pltpu.VMEM((win, lanes_q), F32)],
        compiler_params=params,
        name="attend_bwd",
    )(
        jnp.stack([1 - core, lat_index]), q_flat, attended_grad, k_flat, v_flat, from_west,
        from_east, above_own, above_corner, below_own, below_corner, table, m_s, l_s, m_k, l_k,
    )

    get_below = lax.ppermute(top, "lat", up)
    get_above = lax.ppermute(bottom, "lat", down)
    give_west, give_east = pl.pallas_call(
        functools.partial(side_kernel, lat_dev, lon_dev, cols_pad),
        out_shape=[shape((2, n_side, width))] * 2,
        scratch_shapes=[pltpu.VMEM((tokens, width), F32)],
        name="side",
    )(side, get_above, get_below)
    get_east = lax.ppermute(give_west, "lon", west)
    get_west = lax.ppermute(give_east, "lon", east)
    key_grad, value_grad = pl.pallas_call(
        functools.partial(join_kernel, lat_dev, lon_dev, cols_pad),
        out_shape=[shape((tokens, width))] * 2,
        scratch_shapes=[pltpu.VMEM((tokens, width), F32)],
        name="join",
    )(mid, get_above, get_below, get_west, get_east)

    count = SPAN * SPAN
    bias_local = pl.pallas_call(
        functools.partial(bias_kernel, lon_dev, cols_pad),
        out_shape=shape((heads, 256), F32),
        scratch_shapes=[pltpu.VMEM((256, heads * lon_dev), F32)],
        name="bias_fold",
    )(folded)
    weight_grad, bias_total = reduce_all(weight_s, weight_k, bias_local, mesh_shape, norm)
    bias_grad = bias_total[:, :count].reshape(rel_bias.shape)
    return (
        block_out.reshape(lat_dev, lon_dev, model),
        query_grad.reshape(queries.shape),
        key_grad.reshape(keys.shape),
        value_grad.reshape(values.shape),
        weight_grad,
        bias_grad,
    )


def solution(mesh):
    spec = P("lat", "lon", None)
    return jax.shard_map(
        functools.partial(shards, dict(mesh.shape)),
        mesh=mesh,
        in_specs=(spec, spec, spec, P(), P(), spec),
        out_specs=(spec, spec, spec, spec, P(), P()),
        check_vma=False,
    )
```

```python
import functools

import jax
import jax.numpy as jnp
from jax import lax
from jax.experimental import pallas as pl
from jax.experimental.pallas import tpu as pltpu
from jax.sharding import PartitionSpec as P

RAD = 6
SPAN = 2 * RAD + 1
TILE = 4
GROUP = 4
NEG = -1e30
NT = (((1,), (1,)), ((), ()))
F32 = jnp.float32
BF16 = jnp.bfloat16
SLOTS = 16
CORNER = 80
MIB = 1 << 20


def dot(a, b):
    return jnp.dot(a, b, preferred_element_type=F32)


def dot_nt(a, b):
    return lax.dot_general(a, b, NT, preferred_element_type=F32)


def room(mib):
    return pltpu.CompilerParams(vmem_limit_bytes=mib * MIB)


def iota2(shape, axis):
    return lax.broadcasted_iota(jnp.int32, shape, axis)


def hot(mask):
    return mask.astype(F32).astype(BF16)


def spread_heads(tile, cols, head_size):
    lane = iota2((cols, tile.shape[1]), 1) // head_size
    zero = jnp.zeros((cols, tile.shape[1]), tile.dtype)
    parts = []
    for i in range(TILE):
        rows = tile[i * cols : (i + 1) * cols]
        for h in range(GROUP):
            parts.append(jnp.where(lane == h, rows, zero))
    return jnp.concatenate(parts, 0)


def head_mask(cols, head_size):
    shape = (GROUP * head_size, TILE * GROUP * cols)
    return iota2(shape, 0) // head_size == (iota2(shape, 1) // cols) % GROUP


def picker(cols):
    shape = (TILE * cols, TILE * GROUP * cols)
    row = iota2(shape, 0)
    col = iota2(shape, 1)
    return hot((row // cols == col // (GROUP * cols)) & (row % cols == col % cols))


def row_keep(first_row, rows_all, win, lanes, cols_pad):
    row = first_row + iota2((win, lanes), 0) // cols_pad
    return (row >= 0) & (row < rows_all)


def take_cols(rows, cols, first):
    shape = (rows * RAD, rows * cols)
    n = iota2(shape, 0)
    return hot(iota2(shape, 1) == (n // RAD) * cols + first + n % RAD)


def put_cols(rows, cols, first):
    shape = (rows * cols, rows * RAD)
    n = iota2(shape, 1)
    return hot(iota2(shape, 0) == (n // RAD) * cols + first + n % RAD)


def put_corner(cols):
    shape = (RAD * cols, CORNER)
    n = iota2(shape, 1)
    half = RAD * RAD
    m = jnp.where(n < half, n, n - half)
    target = (m // RAD) * cols + m % RAD + jnp.where(n < half, 0, RAD)
    return hot((iota2(shape, 0) == target) & (n < 2 * half))


def pack_kernel(
    rows, cols, k_hbm, v_hbm, east_ref, west_ref, down_ref, up_ref, x_ref, sem_ref
):
    copies = [
        pltpu.make_async_copy(ref, x_ref.at[i], sem_ref.at[i])
        for i, ref in enumerate((k_hbm, v_hbm))
    ]
    for copy in copies:
        copy.start()
    pick_east = take_cols(rows, cols, cols - RAD)
    pick_west = take_cols(rows, cols, 0)
    edge = RAD * cols
    for i, copy in enumerate(copies):
        copy.wait()
        x = x_ref[i]
        east_ref[i] = dot(pick_east, x).astype(BF16)
        west_ref[i] = dot(pick_west, x).astype(BF16)
        down_ref[i] = x[(rows - RAD) * cols :]
        up_ref[i] = x[:edge]


def corner_kernel(rows, w_ref, e_ref, down_ref, up_ref):
    half = RAD * RAD
    shape = (CORNER, rows * RAD)
    n = iota2(shape, 0)
    src = iota2(shape, 1)
    for ref, first in ((down_ref, (rows - RAD) * RAD), (up_ref, 0)):
        pick_w = hot((src == first + n) & (n < half))
        pick_e = hot((src == first + n - half) & (n >= half) & (n < 2 * half))
        for i in range(2):
            ref[i] = (dot(pick_w, w_ref[i]) + dot(pick_e, e_ref[i])).astype(BF16)


def prepare_kernel(
    cols, cols_pad, rel_ref, cot_ref, w_ref, out_ref, grad_ref, c_ref, r_ref
):
    grad_ref[...] = dot_nt(cot_ref[...], w_ref[...]).astype(BF16)
    heads = rel_ref.shape[0]
    lanes = heads * cols
    half = lanes // 2
    shape = (cols_pad, lanes)
    offset = slot_offset(shape, cols)
    inside = (offset >= 0) & (offset < SPAN)
    head = iota2((1, lanes), 1) // cols
    for a in range(SPAN):
        tile = jnp.full(shape, NEG, F32)
        for b in range(SPAN):
            row = jnp.full((1, lanes), rel_ref[0, a, b], F32)
            for h in range(1, heads):
                row = jnp.where(head == h, rel_ref[h, a, b], row)
            tile = jnp.where(offset == b, row, tile)
        tile = jnp.where(inside, tile, NEG)
        c_ref[a] = tile
        r_ref[a] = pltpu.roll(tile, half, 1)
    low = iota2(shape, 1) < half
    blank = jnp.full(shape, NEG, F32)
    for g in range(2):
        first, second = (c_ref, r_ref) if g == 0 else (r_ref, c_ref)
        for pair in range(TILE // 2):
            i = 2 * pair
            lo = (g * TILE // 2 + pair) * lanes
            for k in range(TILE + 2 * RAD):
                a = k - i
                one = first[a] if 0 <= a < SPAN else blank
                two = second[a - 1] if 0 <= a - 1 < SPAN else blank
                out_ref[k * cols_pad : (k + 1) * cols_pad, lo : lo + lanes] = jnp.where(
                    low, one, two
                )


def slot_offset(shape, cols):
    slot = iota2(shape, 0)
    pos = jnp.where(slot < cols, slot + RAD, jnp.where(slot < cols + RAD, slot - cols, slot))
    pos = jnp.where(slot < cols + 2 * RAD, pos, -1000)
    return pos - iota2(shape, 1) % cols


def assemble(out_ref, i, rows, cols, cols_pad, own, refs, group):
    w_ref, e_ref, ao_ref, ac_ref, bo_ref, bc_ref = refs
    side = dot(put_cols(rows, SLOTS, 0), w_ref[i, :, group])
    side = (side + dot(put_cols(rows, SLOTS, RAD), e_ref[i, :, group])).astype(BF16)
    for r in range(rows):
        lo = (RAD + r) * cols_pad
        out_ref[lo : lo + cols, :] = own[r * cols : (r + 1) * cols, group]
        out_ref[lo + cols : lo + cols + SLOTS, :] = side[r * SLOTS : (r + 1) * SLOTS]
    put = put_corner(SLOTS)
    for first, o_ref, c_ref in ((0, ao_ref, ac_ref), (RAD + rows, bo_ref, bc_ref)):
        side = dot(put, c_ref[i, :, group]).astype(BF16)
        for r in range(RAD):
            lo = (first + r) * cols_pad
            out_ref[lo : lo + cols, :] = o_ref[i, r * cols : (r + 1) * cols, group]
            out_ref[lo + cols : lo + cols + SLOTS, :] = side[r * SLOTS : (r + 1) * SLOTS]


def group_lanes(group, lanes):
    return pl.ds(pl.multiple_of(group * lanes, lanes), lanes)


def fwd_kernel(
    sizes, n, info_ref, q_ref, k_ref, v_ref, w_ref, e_ref, ao_ref, ac_ref, bo_ref, bc_ref,
    bias_ref, cot_ref, out_ref, weight_ref, p_ref, ko_ref, vo_ref, vt_ref, at_ref,
):
    lat_dev, cols, cols_pad, head_size, rows_all = sizes
    scale = head_size ** (-0.5)
    group = group_lanes(info_ref[n], GROUP * head_size)
    refs = (w_ref, e_ref, ao_ref, ac_ref, bo_ref, bc_ref)
    assemble(ko_ref, 0, lat_dev, cols, cols_pad, k_ref, refs, group)
    assemble(vo_ref, 1, lat_dev, cols, cols_pad, v_ref, refs, group)
    vt_ref[...] = vo_ref[...].T
    mask = head_mask(cols, head_size)
    pick = picker(cols)
    win = (TILE + 2 * RAD) * cols_pad
    for t in range(lat_dev // TILE):
        lo = t * TILE * cols_pad
        qs = pl.ds(t * TILE * cols, TILE * cols)
        q_bd = spread_heads(q_ref[qs, group] * jnp.asarray(scale, BF16), cols, head_size)
        first = info_ref[1] * lat_dev + t * TILE - RAD
        keep = row_keep(first, rows_all, win, q_bd.shape[0], cols_pad)
        st = dot_nt(ko_ref[pl.ds(lo, win), :], q_bd) + bias_ref[:, group]
        st = jnp.where(keep, st, NEG)
        m = jnp.max(st, 0, keepdims=True)
        e = jnp.exp(st - m)
        p = e * (1.0 / jnp.sum(e, 0, keepdims=True))
        p_ref[t] = p
        ot = dot(vt_ref[:, pl.ds(lo, win)], p.astype(BF16))
        ot = jnp.where(mask, ot, 0.0).astype(BF16)
        out_ref[qs, :] = dot_nt(pick, ot).astype(BF16)
    at_ref[...] = out_ref[...].T
    weight_ref[...] = dot(at_ref[...], cot_ref[...]).astype(weight_ref.dtype)


def bwd_kernel(
    sizes, info_ref, q_ref, g_ref, ps_ref, ks_ref, vs_ref, pk_ref, kk_ref, vk_ref,
    dq_ref, top_ref, bot_ref, mid_ref, side_ref, x_ref,
    kt_ref, dk_ref, dv_ref, db_ref,
):
    lat_dev, cols, cols_pad, head_size, rows_all = sizes
    scale = head_size ** (-0.5)
    mask = head_mask(cols, head_size)
    pick = picker(cols)
    win = (TILE + 2 * RAD) * cols_pad
    half = GROUP * cols
    low = iota2((cols_pad, 2 * half), 1) < half
    for step, (p_ref, k_ref, v_ref) in enumerate(
        ((ps_ref, ks_ref, vs_ref), (pk_ref, kk_ref, vk_ref))
    ):
        which = info_ref[0] if step == 0 else 1 - info_ref[0]
        group = group_lanes(which, GROUP * head_size)
        kt_ref[...] = k_ref[...].T
        dk_ref[...] = jnp.zeros_like(dk_ref)
        dv_ref[...] = jnp.zeros_like(dv_ref)
        for t in range(lat_dev // TILE):
            lo = t * TILE * cols_pad
            qs = pl.ds(t * TILE * cols, TILE * cols)
            ws = pl.ds(lo, win)
            q_bd = spread_heads(q_ref[qs, group] * jnp.asarray(scale, BF16), cols, head_size)
            g_bd = spread_heads(g_ref[qs, group], cols, head_size)
            p = p_ref[t]
            slope = dot_nt(v_ref[ws, :], g_bd)
            inner = jnp.sum(p * slope, 0, keepdims=True)
            sg = p * (slope - inner)
            if t == 0:
                db_ref[...] = sg
            else:
                db_ref[...] += sg
            sgb = sg.astype(BF16)
            dqt = jnp.where(mask, dot(kt_ref[:, ws], sgb) * scale, 0.0).astype(BF16)
            dq_ref[qs, group] = dot_nt(pick, dqt).astype(BF16)
            dk_ref[ws, :] += dot(sgb, q_bd)
            dv_ref[ws, :] += dot(p.astype(BF16), g_bd)
        edge = RAD * cols_pad
        for i, ref in enumerate((dk_ref, dv_ref)):
            top_ref[i, :, group] = ref[:edge, :].astype(BF16)
            bot_ref[i, :, group] = ref[edge + lat_dev * cols_pad :, :].astype(BF16)
            for r in range(lat_dev):
                lo = (RAD + r) * cols_pad
                mid_ref[i, r * cols : (r + 1) * cols, group] = ref[lo : lo + cols, :]
                side_ref[i, r * SLOTS : (r + 1) * SLOTS, group] = ref[lo + cols : lo + cols_pad, :]
        for a in range(SPAN):
            total = jnp.zeros((cols_pad, 2 * half), F32)
            for pair in range(TILE // 2):
                i = 2 * pair
                lanes = slice(pair * 2 * half, (pair + 1) * 2 * half)
                one = db_ref[(a + i) * cols_pad : (a + i + 1) * cols_pad, lanes]
                two = db_ref[(a + i + 1) * cols_pad : (a + i + 2) * cols_pad, lanes]
                total = total + jnp.where(low, one, two)
            x_ref[which, a * cols_pad : (a + 1) * cols_pad, :] = total


def bias_kernel(cols, cols_pad, x_ref, out_ref, z_ref):
    lanes = x_ref.shape[2]
    half = lanes // 2
    shape = (cols_pad, lanes)
    low = iota2(shape, 1) < half
    offset = slot_offset(shape, cols)
    z_ref[...] = jnp.zeros_like(z_ref)
    for a in range(SPAN):
        rows = slice(a * cols_pad, (a + 1) * cols_pad)
        one = x_ref[0, rows, :]
        two = x_ref[1, rows, :]
        both = jnp.where(low, one + pltpu.roll(one, half, 1), two + pltpu.roll(two, half, 1))
        for b in range(SPAN):
            n = a * SPAN + b
            z_ref[n : n + 1, :] = jnp.sum(jnp.where(offset == b, both, 0.0), 0, keepdims=True)
    heads = out_ref.shape[0]
    pick = (iota2((heads, lanes), 1) // cols == iota2((heads, lanes), 0)).astype(F32)
    out_ref[...] = lax.dot_general(
        pick, z_ref[...], NT, precision=lax.Precision.HIGHEST, preferred_element_type=F32
    )


def lat_terms(ref, i, rows, cols, cols_pad, first):
    parts = []
    for r in range(RAD):
        lo = r * cols_pad + first
        parts.append(ref[i, lo : lo + cols, :])
    return jnp.concatenate(parts, 0).astype(F32)


def side_kernel(rows, cols, cols_pad, side_ref, a_ref, b_ref, west_ref, east_ref, s_ref):
    edge = RAD * SLOTS
    pick_west = take_cols(rows, SLOTS, 0)
    pick_east = take_cols(rows, SLOTS, RAD)
    for i in range(2):
        s_ref[...] = side_ref[i]
        s_ref[:edge, :] += lat_terms(a_ref, i, rows, SLOTS, cols_pad, cols)
        s_ref[(rows - RAD) * SLOTS :, :] += lat_terms(b_ref, i, rows, SLOTS, cols_pad, cols)
        x = s_ref[...].astype(BF16)
        west_ref[i] = dot(pick_west, x).astype(BF16)
        east_ref[i] = dot(pick_east, x).astype(BF16)


def join_kernel(rows, cols, cols_pad, mid_ref, a_ref, b_ref, w_ref, e_ref, k_ref, v_ref, s_ref):
    edge = RAD * cols
    put_west = put_cols(rows, cols, 0)
    put_east = put_cols(rows, cols, cols - RAD)
    for i, out_ref in enumerate((k_ref, v_ref)):
        s_ref[...] = mid_ref[i] + dot(put_west, w_ref[i]) + dot(put_east, e_ref[i])
        s_ref[:edge, :] += lat_terms(a_ref, i, rows, cols, cols_pad, 0)
        s_ref[(rows - RAD) * cols :, :] += lat_terms(b_ref, i, rows, cols, cols_pad, 0)
        out_ref[...] = s_ref[...].astype(BF16)


def bits_of(mesh_shape):
    order = []
    for axis in ("lat", "lon"):
        bit = 1
        while bit < mesh_shape[axis]:
            order.append((axis, bit))
            bit *= 2
    return order


def rounds_of(mesh_shape):
    first, *rest = bits_of(mesh_shape)
    *middle, last = rest
    turned = middle[1:] + middle[:1]
    return [(first, first)] + list(zip(middle, turned)) + [(last, last)]


def partner_pairs(mesh_shape, bits):
    n_lat, n_lon = mesh_shape["lat"], mesh_shape["lon"]
    pairs = []
    for i in range(n_lat):
        axis, bit = bits[i % 2]
        for j in range(n_lon):
            a, b = (i ^ bit, j) if axis == "lat" else (i, j ^ bit)
            pairs.append((i * n_lon + j, a * n_lon + b))
    return pairs


def swap(x, mesh_shape, bits):
    return lax.ppermute(x, ("lat", "lon"), partner_pairs(mesh_shape, bits))


def my_bit(bits):
    def of(axis, bit):
        return (lax.axis_index(axis) // bit) % 2

    odd = lax.axis_index("lat") % 2
    return jnp.where(odd == 0, of(*bits[0]), of(*bits[1]))


def put_bias(ref, rows, bias):
    heads, count = bias.shape
    high = bias.astype(BF16)
    ref[rows:, :count] = high
    ref[rows:, count : 2 * count] = (bias - high.astype(F32)).astype(BF16)
    ref[rows:, 2 * count :] = jnp.zeros((heads, ref.shape[1] - 2 * count), BF16)


def get_bias(ref, rows, count):
    return ref[rows:, :count].astype(F32) + ref[rows:, count : 2 * count].astype(F32)


def halve_kernel(n, info_ref, keep_ref, got_ref, send_ref, out_ref):
    half = send_ref.shape[0]
    low = keep_ref[:half, :] + got_ref[:half, :].astype(F32)
    high = keep_ref[half:, :] + got_ref[half:, :].astype(F32)
    lower = info_ref[n] == 0
    send_ref[...] = jnp.where(lower, high, low).astype(BF16)
    out_ref[...] = jnp.where(lower, low, high)


def meet_kernel(keep_ref, got_ref, bias_ref, out_ref):
    rows = keep_ref.shape[0]
    out_ref[:rows, :] = (keep_ref[...] + got_ref[...].astype(F32)).astype(BF16)
    put_bias(out_ref, rows, bias_ref[...])


def total_kernel(norm, count, heads, own_ref, got_ref, out_ref):
    rows = own_ref.shape[0] - heads
    total = own_ref[:rows, :].astype(F32) + got_ref[:rows, :].astype(F32)
    out_ref[:rows, :] = (total * norm).astype(BF16)
    put_bias(out_ref, rows, get_bias(own_ref, rows, count) + get_bias(got_ref, rows, count))


def grow_kernel(n, count, heads, info_ref, own_ref, got_ref, out_ref):
    rows = own_ref.shape[0] - heads
    lower = info_ref[n] == 0
    own = own_ref[:rows, :]
    got = got_ref[:rows, :]
    out_ref[:rows, :] = jnp.where(lower, own, got)
    out_ref[rows : 2 * rows, :] = jnp.where(lower, got, own)
    put_bias(out_ref, 2 * rows, get_bias(own_ref, rows, count) + get_bias(got_ref, rows, count))


def last_kernel(n, norm, count, info_ref, own_ref, got_ref, out_ref, bias_ref):
    rows = out_ref.shape[0] // 2
    lower = info_ref[n] == 0
    own = own_ref[:rows, :]
    got = got_ref[:rows, :]
    out_ref[:rows, :] = jnp.where(lower, own, got)
    out_ref[rows:, :] = jnp.where(lower, got, own)
    bias = (get_bias(own_ref, rows, count) + get_bias(got_ref, rows, count)) * norm
    for a in range(SPAN):
        bias_ref[:, a, :] = bias[:, a * SPAN : (a + 1) * SPAN]


def project_kernel(info_ref, s_ref, k_ref, w_ref, out_ref):
    rows = s_ref.shape[1]
    first = pl.ds(pl.multiple_of(info_ref[0] * rows, rows), rows)
    second = pl.ds(pl.multiple_of((1 - info_ref[0]) * rows, rows), rows)
    out = dot(s_ref[...], w_ref[first, :]) + dot(k_ref[...], w_ref[second, :])
    out_ref[...] = out.astype(BF16)


def shards(mesh_shape, queries, keys, values, rel_bias, out_weight, cotangent):
    lat_dev, lon_dev, width = queries.shape
    heads = rel_bias.shape[0]
    head_size = width // heads
    groups = heads // GROUP
    lanes = GROUP * head_size
    model = out_weight.shape[1]
    n_lat, n_lon = mesh_shape["lat"], mesh_shape["lon"]
    cols_pad = lon_dev + SLOTS
    outer_lat = lat_dev + 2 * RAD
    tokens = lat_dev * lon_dev
    norm = (tokens * n_lat * n_lon) ** (-0.5)
    east = [(i, (i + 1) % n_lon) for i in range(n_lon)]
    west = [(i, (i - 1) % n_lon) for i in range(n_lon)]
    down = [(i, i + 1) for i in range(n_lat - 1)]
    up = [(i + 1, i) for i in range(n_lat - 1)]
    win = (TILE + 2 * RAD) * cols_pad
    tiles = lat_dev // TILE
    lanes_q = TILE * GROUP * lon_dev
    n_keys = outer_lat * cols_pad
    n_side = lat_dev * RAD
    n_edge = RAD * lon_dev
    n_strip = RAD * cols_pad

    def shape(dims, dtype=BF16):
        return jax.ShapeDtypeStruct(dims, dtype)

    q_flat = queries.reshape(tokens, width)
    k_flat = keys.reshape(tokens, width)
    v_flat = values.reshape(tokens, width)
    cot = cotangent.reshape(tokens, model)

    lat_index = lax.axis_index("lat").astype(jnp.int32)
    core = lat_index % 2
    rounds = rounds_of(mesh_shape)
    facts = [1 - core, lat_index, core] + [my_bit(bits) for bits in rounds]
    info = jnp.stack([x.astype(jnp.int32) for x in facts])
    smem = pl.BlockSpec(memory_space=pltpu.SMEM)
    vmem = pl.BlockSpec(memory_space=pltpu.VMEM)
    hbm = pl.BlockSpec(memory_space=pltpu.HBM)

    to_east, to_west, to_down, to_up = pl.pallas_call(
        functools.partial(pack_kernel, lat_dev, lon_dev),
        in_specs=[hbm, hbm],
        out_shape=[shape((2, n_side, width))] * 2 + [shape((2, n_edge, width))] * 2,
        scratch_shapes=[pltpu.VMEM((2, tokens, width), BF16), pltpu.SemaphoreType.DMA((2,))],
        compiler_params=room(4),
        name="pack",
    )(k_flat, v_flat)
    from_west = lax.ppermute(to_east, "lon", east)
    from_east = lax.ppermute(to_west, "lon", west)
    above_own = lax.ppermute(to_down, "lat", down)
    below_own = lax.ppermute(to_up, "lat", up)
    sizes = (lat_dev, lon_dev, cols_pad, head_size, lat_dev * n_lat)
    table, attended_grad = pl.pallas_call(
        functools.partial(prepare_kernel, lon_dev, cols_pad),
        in_specs=[smem, vmem, vmem],
        out_shape=[shape((win, groups * lanes_q), F32), shape((tokens, width))],
        scratch_shapes=[pltpu.VMEM((SPAN, cols_pad, heads * lon_dev), F32)] * 2,
        compiler_params=room(6),
        name="prepare",
    )(rel_bias, cot, out_weight)
    from_west, from_east, table = lax.optimization_barrier((from_west, from_east, table))
    corner_down, corner_up = pl.pallas_call(
        functools.partial(corner_kernel, lat_dev),
        out_shape=[shape((2, CORNER, width))] * 2,
        compiler_params=room(4),
        name="corner",
    )(from_west, from_east)
    above_corner = lax.ppermute(corner_down, "lat", down)
    below_corner = lax.ppermute(corner_up, "lat", up)

    probs = (tiles, win, lanes_q)
    outer = (n_keys, lanes)

    def forward(n, dtype):
        return pl.pallas_call(
            functools.partial(fwd_kernel, sizes, n),
            in_specs=[smem] + [vmem] * 11,
            out_shape=[shape((tokens, lanes)), shape((lanes, model), dtype), shape(probs, F32)]
            + [shape(outer)] * 2,
            scratch_shapes=[pltpu.VMEM((lanes, n_keys), BF16), pltpu.VMEM((lanes, tokens), BF16)],
            compiler_params=room(8),
            name="attend_fwd",
        )(
            info, q_flat, k_flat, v_flat, from_west, from_east,
            above_own, above_corner, below_own, below_corner, table, cot,
        )

    def step_call(kernel, name, outs, *operands):
        scalars = [smem if x.dtype == jnp.int32 else vmem for x in operands]
        return pl.pallas_call(
            kernel, in_specs=scalars, out_shape=outs, compiler_params=room(4), name=name
        )(*operands)

    att_s, weight_s, p_s, k_s, v_s = forward(0, BF16)
    got = swap(weight_s, mesh_shape, rounds[0])
    att_k, keep, p_k, k_k, v_k = forward(2, F32)

    def halve(keep, got, number):
        half = (keep.shape[0] // 2, model)
        outs = [shape(half), shape(half, F32)]
        kernel = functools.partial(halve_kernel, 3 + number)
        return step_call(kernel, "halve", outs, info, keep, got)

    send, keep = halve(keep, got, 1)
    info_b, send = lax.optimization_barrier((info, send))
    got = swap(send, mesh_shape, rounds[1])

    query_grad, top, bottom, mid, side, folded = pl.pallas_call(
        functools.partial(bwd_kernel, sizes),
        in_specs=[smem] + [vmem] * 8,
        out_shape=[shape((tokens, width))]
        + [shape((2, n_strip, width))] * 2
        + [shape((2, tokens, width), F32)] * 2
        + [shape((groups, SPAN * cols_pad, 2 * GROUP * lon_dev), F32)],
        scratch_shapes=[pltpu.VMEM((lanes, n_keys), BF16)]
        + [pltpu.VMEM((n_keys, lanes), F32)] * 2
        + [pltpu.VMEM((win, lanes_q), F32)],
        compiler_params=room(10),
        name="attend_bwd",
    )(info_b, q_flat, attended_grad, p_s, k_s, v_s, p_k, k_k, v_k)

    get_below = lax.ppermute(top, "lat", up)
    get_above = lax.ppermute(bottom, "lat", down)
    for number in range(2, len(rounds) - 1):
        send, keep = halve(keep, got, number)
        if number == 3:
            send, get_below, get_above = lax.optimization_barrier((send, get_below, get_above))
        got = swap(send, mesh_shape, rounds[number])

    give_west, give_east = pl.pallas_call(
        functools.partial(side_kernel, lat_dev, lon_dev, cols_pad),
        out_shape=[shape((2, n_side, width))] * 2,
        scratch_shapes=[pltpu.VMEM((tokens, width), F32)],
        compiler_params=room(6),
        name="side",
    )(side, get_above, get_below)
    get_east = lax.ppermute(give_west, "lon", west)
    get_west = lax.ppermute(give_east, "lon", east)

    count = 256
    bias_local = pl.pallas_call(
        functools.partial(bias_kernel, lon_dev, cols_pad),
        out_shape=shape((heads, count), F32),
        scratch_shapes=[pltpu.VMEM((count, heads * lon_dev), F32)],
        compiler_params=room(4),
        name="bias_fold",
    )(folded)
    note = shape((keep.shape[0] + heads, model))
    message = step_call(meet_kernel, "meet", note, keep, got, bias_local)
    got = swap(message, mesh_shape, rounds[-1])
    kernel = functools.partial(total_kernel, norm, count, heads)
    message = step_call(kernel, "total", note, message, got)
    for number in range(len(rounds) - 2, 0, -1):
        if number == 2:
            message, get_east, get_west = lax.optimization_barrier((message, get_east, get_west))
        got = swap(message, mesh_shape, rounds[number])
        note = shape((2 * message.shape[0] - heads, model))
        kernel = functools.partial(grow_kernel, 3 + number, count, heads)
        message = step_call(kernel, "grow", note, info, message, got)

    key_grad, value_grad = pl.pallas_call(
        functools.partial(join_kernel, lat_dev, lon_dev, cols_pad),
        out_shape=[shape((tokens, width))] * 2,
        scratch_shapes=[pltpu.VMEM((tokens, width), F32)],
        compiler_params=room(6),
        name="join",
    )(mid, get_above, get_below, get_west, get_east)
    block_out = pl.pallas_call(
        project_kernel,
        in_specs=[smem] + [vmem] * 3,
        out_shape=shape((tokens, model)),
        compiler_params=room(6),
        name="project",
    )(info, att_s, att_k, out_weight)

    got = swap(message, mesh_shape, rounds[0])
    weight_grad, bias_grad = step_call(
        functools.partial(last_kernel, 3, norm, count),
        "last",
        [shape((width, model)), shape(rel_bias.shape, F32)],
        info, message, got,
    )
    return (
        block_out.reshape(lat_dev, lon_dev, model),
        query_grad.reshape(queries.shape),
        key_grad.reshape(keys.shape),
        value_grad.reshape(values.shape),
        weight_grad,
        bias_grad,
    )


def solution(mesh):
    spec = P("lat", "lon", None)
    return jax.shard_map(
        functools.partial(shards, dict(mesh.shape)),
        mesh=mesh,
        in_specs=(spec, spec, spec, P(), P(), spec),
        out_specs=(spec, spec, spec, spec, P(), P()),
        check_vma=False,
    )
```

```python
import functools

import jax
import jax.numpy as jnp
from jax import lax
from jax.experimental import pallas as pl
from jax.experimental.pallas import tpu as pltpu
from jax.sharding import PartitionSpec as P

RAD = 6
SPAN = 2 * RAD + 1
TILE = 4
GROUP = 4
NEG = -1e30
NT = (((1,), (1,)), ((), ()))
F32 = jnp.float32
BF16 = jnp.bfloat16
SLOTS = 16
CORNER = 80
MIB = 1 << 20


def dot(a, b):
    return jnp.dot(a, b, preferred_element_type=F32)


def dot_nt(a, b):
    return lax.dot_general(a, b, NT, preferred_element_type=F32)


def in_hbm(x):
    return pltpu.with_memory_space_constraint(x, pltpu.HBM)


def room(mib):
    return pltpu.CompilerParams(vmem_limit_bytes=mib * MIB)


def iota2(shape, axis):
    return lax.broadcasted_iota(jnp.int32, shape, axis)


def hot(mask):
    return mask.astype(F32).astype(BF16)


def over(x, n):
    if n & (n - 1) == 0:
        return x >> (n.bit_length() - 1), x & (n - 1)
    return x // n, x % n


def down_iota(n):
    return iota2((n, 1), 0)


def along_iota(n):
    return iota2((1, n), 1)


def spread_heads(tile, cols, head_size):
    lane = over(iota2((cols, tile.shape[1]), 1), head_size)[0]
    zero = jnp.zeros((cols, tile.shape[1]), tile.dtype)
    parts = []
    for i in range(TILE):
        rows = tile[i * cols : (i + 1) * cols]
        for h in range(GROUP):
            parts.append(jnp.where(lane == h, rows, zero))
    return jnp.concatenate(parts, 0)


def head_mask(cols, head_size):
    shape = (GROUP * head_size, TILE * GROUP * cols)
    column = over(over(iota2(shape, 1), cols)[0], GROUP)[1]
    return over(iota2(shape, 0), head_size)[0] == column


def picker(cols):
    row_i, row_j = over(down_iota(TILE * cols), cols)
    high, col_j = over(along_iota(TILE * GROUP * cols), cols)
    return hot((row_i == over(high, GROUP)[0]) & (row_j == col_j))


def keep_rows(st, first_row, rows_all, cols_pad):
    parts = []
    for k in range(TILE + 2 * RAD):
        row = first_row + k
        inside = (row >= 0) & (row < rows_all)
        parts.append(jnp.where(inside, st[k * cols_pad : (k + 1) * cols_pad], NEG))
    return jnp.concatenate(parts, 0)


def take_cols(rows, cols, first):
    r, c = over(down_iota(rows * RAD), RAD)
    return hot(along_iota(rows * cols) == r * cols + first + c)


def put_cols(rows, cols, first):
    r, c = over(along_iota(rows * RAD), RAD)
    return hot(down_iota(rows * cols) == r * cols + first + c)


def put_corner(cols):
    n = along_iota(CORNER)
    half = RAD * RAD
    r, c = over(jnp.where(n < half, n, n - half), RAD)
    target = r * cols + c + jnp.where(n < half, 0, RAD)
    return hot((down_iota(RAD * cols) == target) & (n < 2 * half))


def pack_kernel(
    rows, cols, k_hbm, v_hbm, east_ref, west_ref, down_ref, up_ref, x_ref, sem_ref
):
    copies = [
        pltpu.make_async_copy(ref, x_ref.at[i], sem_ref.at[i])
        for i, ref in enumerate((k_hbm, v_hbm))
    ]
    for copy in copies:
        copy.start()
    pick_east = take_cols(rows, cols, cols - RAD)
    pick_west = take_cols(rows, cols, 0)
    edge = RAD * cols
    for i, copy in enumerate(copies):
        copy.wait()
        x = x_ref[i]
        east_ref[i] = dot(pick_east, x).astype(BF16)
        west_ref[i] = dot(pick_west, x).astype(BF16)
        down_ref[i] = x[(rows - RAD) * cols :]
        up_ref[i] = x[:edge]


def corner_kernel(rows, cols, w_ref, e_ref, own_down_ref, own_up_ref, down_ref, up_ref):
    half = RAD * RAD
    edge = RAD * cols
    n = down_iota(CORNER)
    src = along_iota(rows * RAD)
    for ref, own_ref, first in (
        (down_ref, own_down_ref, (rows - RAD) * RAD), (up_ref, own_up_ref, 0)
    ):
        pick_w = hot((src == first + n) & (n < half))
        pick_e = hot((src == first + n - half) & (n >= half) & (n < 2 * half))
        for i in range(2):
            side = dot(pick_w, w_ref[i]) + dot(pick_e, e_ref[i])
            ref[i, :edge, :] = own_ref[i]
            ref[i, edge:, :] = side.astype(BF16)


def prepare_kernel(
    cols, cols_pad, rel_ref, cot_hbm, w_hbm, out_ref, grad_ref, c_ref, r_ref, cot_ref, w_ref,
    sem_ref,
):
    copies = [
        pltpu.make_async_copy(cot_hbm, cot_ref, sem_ref.at[0]),
        pltpu.make_async_copy(w_hbm, w_ref, sem_ref.at[1]),
    ]
    for copy in copies:
        copy.start()
    heads = rel_ref.shape[1]
    lanes = heads * cols
    half = lanes // 2
    shape = (cols_pad, lanes)
    offset = slot_offset(shape, cols)
    inside = (offset >= 0) & (offset < SPAN)
    head = over(iota2((1, lanes), 1), cols)[0]
    for a in range(SPAN):
        tile = jnp.full(shape, NEG, F32)
        for b in range(SPAN):
            row = jnp.full((1, lanes), rel_ref[a, 0, b], F32)
            for h in range(1, heads):
                row = jnp.where(head == h, rel_ref[a, h, b], row)
            tile = jnp.where(offset == b, row, tile)
        tile = jnp.where(inside, tile, NEG)
        c_ref[a] = tile
        r_ref[a] = pltpu.roll(tile, half, 1)
    low = iota2(shape, 1) < half
    blank = jnp.full(shape, NEG, F32)
    for g in range(2):
        first, second = (c_ref, r_ref) if g == 0 else (r_ref, c_ref)
        for pair in range(TILE // 2):
            i = 2 * pair
            lo = (g * TILE // 2 + pair) * lanes
            for k in range(TILE + 2 * RAD):
                a = k - i
                one = first[a] if 0 <= a < SPAN else blank
                two = second[a - 1] if 0 <= a - 1 < SPAN else blank
                out_ref[k * cols_pad : (k + 1) * cols_pad, lo : lo + lanes] = jnp.where(
                    low, one, two
                )
    for copy in copies:
        copy.wait()
    grad_ref[...] = dot_nt(cot_ref[...], w_ref[...]).astype(BF16)


def slot_offset(shape, cols):
    slot = iota2(shape, 0)
    pos = jnp.where(slot < cols, slot + RAD, jnp.where(slot < cols + RAD, slot - cols, slot))
    pos = jnp.where(slot < cols + 2 * RAD, pos, -1000)
    return pos - over(iota2(shape, 1), cols)[1]


def assemble(out_ref, i, rows, cols, cols_pad, own, refs, group):
    w_ref, e_ref, a_ref, b_ref = refs
    edge = RAD * cols
    side = dot(put_cols(rows, SLOTS, 0), w_ref[i, :, group])
    side = (side + dot(put_cols(rows, SLOTS, RAD), e_ref[i, :, group])).astype(BF16)
    for r in range(rows):
        lo = (RAD + r) * cols_pad
        out_ref[lo : lo + cols, :] = own[r * cols : (r + 1) * cols, group]
        out_ref[lo + cols : lo + cols + SLOTS, :] = side[r * SLOTS : (r + 1) * SLOTS]
    put = put_corner(SLOTS)
    for first, o_ref in ((0, a_ref), (RAD + rows, b_ref)):
        side = dot(put, o_ref[i, edge:, group]).astype(BF16)
        for r in range(RAD):
            lo = (first + r) * cols_pad
            out_ref[lo : lo + cols, :] = o_ref[i, r * cols : (r + 1) * cols, group]
            out_ref[lo + cols : lo + cols + SLOTS, :] = side[r * SLOTS : (r + 1) * SLOTS]


def group_lanes(group, lanes):
    return pl.ds(pl.multiple_of(group * lanes, lanes), lanes)


def fwd_kernel(
    sizes, n, info_ref, q_ref, k_ref, v_ref, w_ref, e_ref, a_ref, b_ref,
    bias_ref, cot_ref, out_ref, weight_ref, p_ref, ko_ref, vo_ref, vt_ref, at_ref,
):
    lat_dev, cols, cols_pad, head_size, rows_all = sizes
    scale = head_size ** (-0.5)
    group = group_lanes(info_ref[n], GROUP * head_size)
    refs = (w_ref, e_ref, a_ref, b_ref)
    assemble(ko_ref, 0, lat_dev, cols, cols_pad, k_ref, refs, group)
    assemble(vo_ref, 1, lat_dev, cols, cols_pad, v_ref, refs, group)
    vt_ref[...] = vo_ref[...].T
    mask = head_mask(cols, head_size)
    pick = picker(cols)
    win = (TILE + 2 * RAD) * cols_pad
    for t in range(lat_dev // TILE):
        lo = t * TILE * cols_pad
        qs = pl.ds(t * TILE * cols, TILE * cols)
        q_bd = spread_heads(q_ref[qs, group] * jnp.asarray(scale, BF16), cols, head_size)
        first = info_ref[1] * lat_dev + t * TILE - RAD
        st = dot_nt(ko_ref[pl.ds(lo, win), :], q_bd) + bias_ref[:, group]
        st = keep_rows(st, first, rows_all, cols_pad)
        m = jnp.max(st, 0, keepdims=True)
        e = jnp.exp(st - m)
        p = e * (1.0 / jnp.sum(e, 0, keepdims=True))
        p_ref[t] = p
        ot = dot(vt_ref[:, pl.ds(lo, win)], p.astype(BF16))
        ot = jnp.where(mask, ot, 0.0).astype(BF16)
        out_ref[qs, :] = dot_nt(pick, ot).astype(BF16)
    at_ref[...] = out_ref[...].T
    weight_ref[...] = dot(at_ref[...], cot_ref[...]).astype(weight_ref.dtype)


def bwd_kernel(sizes, n, info_ref, q_ref, g_ref, p_ref, k_ref, v_ref, *refs):
    dq_ref, top_ref, bot_ref, mid_ref, side_ref, x_ref, kt_ref, dk_ref, dv_ref, db_ref = refs[-10:]
    before = refs[:-10]
    lat_dev, cols, cols_pad, head_size, rows_all = sizes
    scale = head_size ** (-0.5)
    mask = head_mask(cols, head_size)
    pick = picker(cols)
    win = (TILE + 2 * RAD) * cols_pad
    half = GROUP * cols
    low = iota2((cols_pad, 2 * half), 1) < half
    which = info_ref[n]
    group = group_lanes(which, GROUP * head_size)
    mine = group if before else slice(None)
    if before:
        other = group_lanes(1 - which, GROUP * head_size)
        dq_ref[:, other] = before[0][...]
        top_ref[:, :, other] = before[1][...]
        bot_ref[:, :, other] = before[2][...]
    kt_ref[...] = k_ref[...].T
    dk_ref[...] = jnp.zeros_like(dk_ref)
    dv_ref[...] = jnp.zeros_like(dv_ref)
    for t in range(lat_dev // TILE):
        lo = t * TILE * cols_pad
        qs = pl.ds(t * TILE * cols, TILE * cols)
        ws = pl.ds(lo, win)
        q_bd = spread_heads(q_ref[qs, group] * jnp.asarray(scale, BF16), cols, head_size)
        g_bd = spread_heads(g_ref[qs, group], cols, head_size)
        p = p_ref[t]
        slope = dot_nt(v_ref[ws, :], g_bd)
        inner = jnp.sum(p * slope, 0, keepdims=True)
        sg = p * (slope - inner)
        if t == 0:
            db_ref[...] = sg
        else:
            db_ref[...] += sg
        sgb = sg.astype(BF16)
        dqt = jnp.where(mask, dot(kt_ref[:, ws], sgb) * scale, 0.0).astype(BF16)
        dq_ref[qs, mine] = dot_nt(pick, dqt).astype(BF16)
        dk_ref[ws, :] += dot(sgb, q_bd)
        dv_ref[ws, :] += dot(p.astype(BF16), g_bd)
    edge = RAD * cols_pad
    for i, ref in enumerate((dk_ref, dv_ref)):
        top_ref[i, :, mine] = ref[:edge, :].astype(BF16)
        bot_ref[i, :, mine] = ref[edge + lat_dev * cols_pad :, :].astype(BF16)
        for r in range(lat_dev):
            lo = (RAD + r) * cols_pad
            mid_ref[i, r * cols : (r + 1) * cols, :] = ref[lo : lo + cols, :]
            side_ref[i, r * SLOTS : (r + 1) * SLOTS, :] = ref[lo + cols : lo + cols_pad, :]
    for a in range(SPAN):
        total = jnp.zeros((cols_pad, 2 * half), F32)
        for pair in range(TILE // 2):
            i = 2 * pair
            lanes = slice(pair * 2 * half, (pair + 1) * 2 * half)
            one = db_ref[(a + i) * cols_pad : (a + i + 1) * cols_pad, lanes]
            two = db_ref[(a + i + 1) * cols_pad : (a + i + 2) * cols_pad, lanes]
            total = total + jnp.where(low, one, two)
        x_ref[a * cols_pad : (a + 1) * cols_pad, :] = total


def bias_kernel(cols, cols_pad, info_ref, xs_ref, xk_ref, out_ref, z_ref):
    lanes = xs_ref.shape[1]
    half = lanes // 2
    shape = (cols_pad, lanes)
    low = (over(iota2(shape, 1), half)[0] == info_ref[0])
    offset = slot_offset(shape, cols)
    z_ref[...] = jnp.zeros_like(z_ref)
    for a in range(SPAN):
        rows = slice(a * cols_pad, (a + 1) * cols_pad)
        one = xs_ref[rows, :]
        two = xk_ref[rows, :]
        both = jnp.where(low, one + pltpu.roll(one, half, 1), two + pltpu.roll(two, half, 1))
        for b in range(SPAN):
            n = a * SPAN + b
            z_ref[n : n + 1, :] = jnp.sum(jnp.where(offset == b, both, 0.0), 0, keepdims=True)
    heads = out_ref.shape[0]
    pick = (over(iota2((heads, lanes), 1), cols)[0] == iota2((heads, lanes), 0)).astype(F32)
    out_ref[...] = lax.dot_general(
        pick, z_ref[...], NT, precision=lax.Precision.HIGHEST, preferred_element_type=F32
    )


def lat_terms(ref, i, rows, cols, cols_pad, first):
    parts = []
    for r in range(RAD):
        lo = r * cols_pad + first
        parts.append(ref[i, lo : lo + cols, :])
    return jnp.concatenate(parts, 0).astype(F32)


def both_groups(info_ref, dst_ref, i, s_ref, k_ref):
    lanes = s_ref.shape[2]
    dst_ref[:, group_lanes(info_ref[0], lanes)] = s_ref[i]
    dst_ref[:, group_lanes(1 - info_ref[0], lanes)] = k_ref[i]


def side_kernel(
    rows, cols, cols_pad, info_ref, ss_ref, sk_ref, a_ref, b_ref, west_ref, east_ref, s_ref
):
    edge = RAD * SLOTS
    pick_west = take_cols(rows, SLOTS, 0)
    pick_east = take_cols(rows, SLOTS, RAD)
    for i in range(2):
        both_groups(info_ref, s_ref, i, ss_ref, sk_ref)
        s_ref[:edge, :] += lat_terms(a_ref, i, rows, SLOTS, cols_pad, cols)
        s_ref[(rows - RAD) * SLOTS :, :] += lat_terms(b_ref, i, rows, SLOTS, cols_pad, cols)
        x = s_ref[...].astype(BF16)
        west_ref[i] = dot(pick_west, x).astype(BF16)
        east_ref[i] = dot(pick_east, x).astype(BF16)


def join_kernel(
    rows, cols, cols_pad, info_ref, ms_ref, mk_ref, a_ref, b_ref, w_ref, e_ref,
    k_ref, v_ref, s_ref,
):
    edge = RAD * cols
    put_west = put_cols(rows, cols, 0)
    put_east = put_cols(rows, cols, cols - RAD)
    for i, out_ref in enumerate((k_ref, v_ref)):
        both_groups(info_ref, s_ref, i, ms_ref, mk_ref)
        s_ref[...] += dot(put_west, w_ref[i]) + dot(put_east, e_ref[i])
        s_ref[:edge, :] += lat_terms(a_ref, i, rows, cols, cols_pad, 0)
        s_ref[(rows - RAD) * cols :, :] += lat_terms(b_ref, i, rows, cols, cols_pad, 0)
        out_ref[...] = s_ref[...].astype(BF16)


def bits_of(mesh_shape):
    order = []
    for axis in ("lat", "lon"):
        bit = 1
        while bit < mesh_shape[axis]:
            order.append((axis, bit))
            bit *= 2
    return order


def rounds_of(mesh_shape):
    first, *rest = bits_of(mesh_shape)
    middle, ends = rest[:-2], rest[-2:]
    turned = middle[1:] + middle[:1]
    return [(first, first)] + list(zip(middle, turned)), list(zip(ends, ends[::-1]))


def partner_pairs(mesh_shape, bits):
    n_lat, n_lon = mesh_shape["lat"], mesh_shape["lon"]
    pairs = []
    for i in range(n_lat):
        axis, bit = bits[i % 2]
        for j in range(n_lon):
            a, b = (i ^ bit, j) if axis == "lat" else (i, j ^ bit)
            pairs.append((i * n_lon + j, a * n_lon + b))
    return pairs


def swap(x, mesh_shape, bits):
    return lax.ppermute(x, ("lat", "lon"), partner_pairs(mesh_shape, bits))


def my_bit(bits):
    def of(axis, bit):
        return (lax.axis_index(axis) // bit) % 2

    odd = lax.axis_index("lat") % 2
    return jnp.where(odd == 0, of(*bits[0]), of(*bits[1]))


def put_bias(ref, rows, bias):
    heads, count = bias.shape
    high = bias.astype(BF16)
    ref[rows:, :count] = high
    ref[rows:, count : 2 * count] = (bias - high.astype(F32)).astype(BF16)
    ref[rows:, 2 * count :] = jnp.zeros((heads, ref.shape[1] - 2 * count), BF16)


def get_bias(ref, rows, count):
    return ref[rows:, :count].astype(F32) + ref[rows:, count : 2 * count].astype(F32)


def halve_kernel(n, info_ref, keep_ref, got_ref, send_ref, out_ref):
    half = send_ref.shape[0]
    low = keep_ref[:half, :] + got_ref[:half, :].astype(F32)
    high = keep_ref[half:, :] + got_ref[half:, :].astype(F32)
    lower = info_ref[n] == 0
    send_ref[...] = jnp.where(lower, high, low).astype(BF16)
    out_ref[...] = jnp.where(lower, low, high)


def meet_kernel(keep_ref, got_ref, bias_ref, out_ref):
    rows = keep_ref.shape[0]
    out_ref[:rows, :] = (keep_ref[...] + got_ref[...].astype(F32)).astype(BF16)
    put_bias(out_ref, rows, bias_ref[...])


def total_kernel(norm, count, heads, own_ref, got_ref, out_ref):
    rows = own_ref.shape[0] - heads
    total = own_ref[:rows, :].astype(F32) + got_ref[:rows, :].astype(F32)
    out_ref[:rows, :] = (total if norm is None else total * norm).astype(BF16)
    put_bias(out_ref, rows, get_bias(own_ref, rows, count) + get_bias(got_ref, rows, count))


def grow_kernel(n, count, heads, info_ref, own_ref, got_ref, out_ref):
    rows = own_ref.shape[0] - heads
    lower = info_ref[n] == 0
    own = own_ref[:rows, :]
    got = got_ref[:rows, :]
    out_ref[:rows, :] = jnp.where(lower, own, got)
    out_ref[rows : 2 * rows, :] = jnp.where(lower, got, own)
    put_bias(out_ref, 2 * rows, get_bias(own_ref, rows, count) + get_bias(got_ref, rows, count))


def last_kernel(n, norm, count, info_ref, own_ref, got_ref, out_ref, bias_ref):
    rows = out_ref.shape[0] // 2
    lower = info_ref[n] == 0
    own = own_ref[:rows, :]
    got = got_ref[:rows, :]
    out_ref[:rows, :] = jnp.where(lower, own, got)
    out_ref[rows:, :] = jnp.where(lower, got, own)
    bias = (get_bias(own_ref, rows, count) + get_bias(got_ref, rows, count)) * norm
    for a in range(SPAN):
        bias_ref[a] = bias[:, a * SPAN : (a + 1) * SPAN]


def project_kernel(info_ref, s_ref, k_ref, w_ref, out_ref):
    rows = s_ref.shape[1]
    first = pl.ds(pl.multiple_of(info_ref[0] * rows, rows), rows)
    second = pl.ds(pl.multiple_of((1 - info_ref[0]) * rows, rows), rows)
    out = dot(s_ref[...], w_ref[first, :]) + dot(k_ref[...], w_ref[second, :])
    out_ref[...] = out.astype(BF16)


def shards(mesh_shape, queries, keys, values, rel_bias, out_weight, cotangent):
    lat_dev, lon_dev, width = queries.shape
    heads = rel_bias.shape[0]
    head_size = width // heads
    groups = heads // GROUP
    lanes = GROUP * head_size
    model = out_weight.shape[1]
    n_lat, n_lon = mesh_shape["lat"], mesh_shape["lon"]
    cols_pad = lon_dev + SLOTS
    outer_lat = lat_dev + 2 * RAD
    tokens = lat_dev * lon_dev
    norm = (tokens * n_lat * n_lon) ** (-0.5)
    east = [(i, (i + 1) % n_lon) for i in range(n_lon)]
    west = [(i, (i - 1) % n_lon) for i in range(n_lon)]
    down = [(i, i + 1) for i in range(n_lat - 1)]
    up = [(i + 1, i) for i in range(n_lat - 1)]
    win = (TILE + 2 * RAD) * cols_pad
    tiles = lat_dev // TILE
    lanes_q = TILE * GROUP * lon_dev
    n_keys = outer_lat * cols_pad
    n_side = lat_dev * RAD
    n_edge = RAD * lon_dev
    n_strip = RAD * cols_pad

    def shape(dims, dtype=BF16):
        return jax.ShapeDtypeStruct(dims, dtype)

    q_flat = queries.reshape(tokens, width)
    k_flat = keys.reshape(tokens, width)
    v_flat = values.reshape(tokens, width)
    cot = cotangent.reshape(tokens, model)

    lat_index = lax.axis_index("lat").astype(jnp.int32)
    core = lat_index % 2
    rounds, ends = rounds_of(mesh_shape)
    facts = [1 - core, lat_index, core] + [my_bit(bits) for bits in rounds]
    info = jnp.stack([x.astype(jnp.int32) for x in facts])
    smem = pl.BlockSpec(memory_space=pltpu.SMEM)
    vmem = pl.BlockSpec(memory_space=pltpu.VMEM)
    hbm = pl.BlockSpec(memory_space=pltpu.HBM)

    to_east, to_west, to_down, to_up = pl.pallas_call(
        functools.partial(pack_kernel, lat_dev, lon_dev),
        in_specs=[hbm, hbm],
        out_shape=[shape((2, n_side, width))] * 2 + [shape((2, n_edge, width))] * 2,
        scratch_shapes=[pltpu.VMEM((2, tokens, width), BF16), pltpu.SemaphoreType.DMA((2,))],
        compiler_params=room(4),
        name="pack",
    )(in_hbm(k_flat), in_hbm(v_flat))
    from_west = lax.ppermute(to_east, "lon", east)
    from_east = lax.ppermute(to_west, "lon", west)
    sizes = (lat_dev, lon_dev, cols_pad, head_size, lat_dev * n_lat)
    table, attended_grad = pl.pallas_call(
        functools.partial(prepare_kernel, lon_dev, cols_pad),
        in_specs=[smem, hbm, hbm],
        out_shape=[shape((win, groups * lanes_q), F32), shape((tokens, width))],
        scratch_shapes=[pltpu.VMEM((SPAN, cols_pad, heads * lon_dev), F32)] * 2
        + [pltpu.VMEM((tokens, model), BF16), pltpu.VMEM((width, model), BF16)]
        + [pltpu.SemaphoreType.DMA((2,))],
        compiler_params=room(6),
        name="prepare",
    )(rel_bias.transpose(1, 0, 2), in_hbm(cot), in_hbm(out_weight))
    from_west, from_east, table = lax.optimization_barrier((from_west, from_east, table))
    corner_down, corner_up = pl.pallas_call(
        functools.partial(corner_kernel, lat_dev, lon_dev),
        out_shape=[shape((2, n_edge + CORNER, width))] * 2,
        compiler_params=room(4),
        name="corner",
    )(from_west, from_east, to_down, to_up)
    from_above = lax.ppermute(corner_down, "lat", down)
    from_below = lax.ppermute(corner_up, "lat", up)

    probs = (tiles, win, lanes_q)
    outer = (n_keys, lanes)

    def forward(n, dtype):
        return pl.pallas_call(
            functools.partial(fwd_kernel, sizes, n),
            in_specs=[smem] + [vmem] * 9,
            out_shape=[shape((tokens, lanes)), shape((lanes, model), dtype), shape(probs, F32)]
            + [shape(outer)] * 2,
            scratch_shapes=[pltpu.VMEM((lanes, n_keys), BF16), pltpu.VMEM((lanes, tokens), BF16)],
            compiler_params=room(8),
            name="attend_fwd",
        )(
            info, q_flat, k_flat, v_flat, from_west, from_east,
            from_above, from_below, table, cot,
        )

    def step_call(kernel, name, outs, *operands):
        scalars = [smem if x.dtype == jnp.int32 else vmem for x in operands]
        return pl.pallas_call(
            kernel, in_specs=scalars, out_shape=outs, compiler_params=room(4), name=name
        )(*operands)

    att_s, weight_s, p_s, k_s, v_s = forward(0, BF16)
    got = swap(weight_s, mesh_shape, rounds[0])
    att_k, keep, p_k, k_k, v_k = forward(2, F32)

    def halve(keep, got, number):
        half = (keep.shape[0] // 2, model)
        outs = [shape(half), shape(half, F32)]
        kernel = functools.partial(halve_kernel, 3 + number)
        return step_call(kernel, "halve", outs, info, keep, got)

    send, keep = halve(keep, got, 1)
    def backward(n, info, p, k, v, *before):
        size = width if before else lanes
        return pl.pallas_call(
            functools.partial(bwd_kernel, sizes, n),
            in_specs=[smem] + [vmem] * (5 + len(before)),
            out_shape=[shape((tokens, size))]
            + [shape((2, n_strip, size))] * 2
            + [shape((2, tokens, lanes), F32)] * 2
            + [shape((SPAN * cols_pad, 2 * GROUP * lon_dev), F32)],
            scratch_shapes=[pltpu.VMEM((lanes, n_keys), BF16)]
            + [pltpu.VMEM((n_keys, lanes), F32)] * 2
            + [pltpu.VMEM((win, lanes_q), F32)],
            compiler_params=room(10),
            name="attend_bwd",
        )(info, q_flat, attended_grad, p, k, v, *before)

    info_b, send = lax.optimization_barrier((info, send))
    got = swap(send, mesh_shape, rounds[1])
    *before, mid_s, side_s, fold_s = backward(0, info_b, p_s, k_s, v_s)
    for number in range(2, len(rounds)):
        send, keep = halve(keep, got, number)
        if number == 2:
            info_b, send = lax.optimization_barrier((info, send))
        got = swap(send, mesh_shape, rounds[number])
    after = backward(2, info_b, p_k, k_k, v_k, *before)
    query_grad, top, bottom, mid_k, side_k, fold_k = after
    get_below = lax.ppermute(top, "lat", up)
    get_above = lax.ppermute(bottom, "lat", down)

    count = 256
    bias_local = pl.pallas_call(
        functools.partial(bias_kernel, lon_dev, cols_pad),
        in_specs=[smem, vmem, vmem],
        out_shape=shape((heads, count), F32),
        scratch_shapes=[pltpu.VMEM((count, heads * lon_dev), F32)],
        compiler_params=room(4),
        name="bias_fold",
    )(info, fold_s, fold_k)
    block_out = pl.pallas_call(
        project_kernel,
        in_specs=[smem] + [vmem] * 3,
        out_shape=shape((tokens, model)),
        compiler_params=room(6),
        name="project",
    )(info, att_s, att_k, out_weight)
    note = shape((keep.shape[0] + heads, model))
    message = step_call(meet_kernel, "meet", note, keep, got, bias_local)
    got = swap(message, mesh_shape, ends[0])
    kernel = functools.partial(total_kernel, None, count, heads)
    message = step_call(kernel, "total", note, message, got)
    message, get_below, get_above, block_out = lax.optimization_barrier(
        (message, get_below, get_above, block_out)
    )
    got = swap(message, mesh_shape, ends[1])
    give_west, give_east = pl.pallas_call(
        functools.partial(side_kernel, lat_dev, lon_dev, cols_pad),
        in_specs=[smem] + [vmem] * 4,
        out_shape=[shape((2, n_side, width))] * 2,
        scratch_shapes=[pltpu.VMEM((tokens, width), F32)],
        compiler_params=room(6),
        name="side",
    )(info, side_s, side_k, get_above, get_below)
    get_east = lax.ppermute(give_west, "lon", west)
    get_west = lax.ppermute(give_east, "lon", east)
    kernel = functools.partial(total_kernel, norm, count, heads)
    message = step_call(kernel, "total", note, message, got)
    message, give_west, give_east = lax.optimization_barrier((message, give_west, give_east))

    for number in range(len(rounds) - 1, 0, -1):
        if number == 1:
            message, get_east, get_west = lax.optimization_barrier((message, get_east, get_west))
        got = swap(message, mesh_shape, rounds[number])
        note = shape((2 * message.shape[0] - heads, model))
        kernel = functools.partial(grow_kernel, 3 + number, count, heads)
        message = step_call(kernel, "grow", note, info, message, got)
    key_grad, value_grad = pl.pallas_call(
        functools.partial(join_kernel, lat_dev, lon_dev, cols_pad),
        in_specs=[smem] + [vmem] * 6,
        out_shape=[shape((tokens, width))] * 2,
        scratch_shapes=[pltpu.VMEM((tokens, width), F32)],
        compiler_params=room(6),
        name="join",
    )(info, mid_s, mid_k, get_above, get_below, get_west, get_east)
    got = swap(message, mesh_shape, rounds[0])
    weight_grad, bias_grad = step_call(
        functools.partial(last_kernel, 3, norm, count),
        "last",
        [shape((width, model)), shape((SPAN, heads, SPAN), F32)],
        info, message, got,
    )
    return (
        block_out.reshape(lat_dev, lon_dev, model),
        query_grad.reshape(queries.shape),
        key_grad.reshape(keys.shape),
        value_grad.reshape(values.shape),
        weight_grad,
        bias_grad.transpose(1, 0, 2),
    )


def solution(mesh):
    spec = P("lat", "lon", None)
    return jax.shard_map(
        functools.partial(shards, dict(mesh.shape)),
        mesh=mesh,
        in_specs=(spec, spec, spec, P(), P(), spec),
        out_specs=(spec, spec, spec, spec, P(), P()),
        check_vma=False,
    )
```

```python
import functools

import jax
import jax.numpy as jnp
from jax import lax
from jax.experimental import pallas as pl
from jax.experimental.pallas import tpu as pltpu
from jax.sharding import PartitionSpec as P

RAD = 6
SPAN = 2 * RAD + 1
TILE = 4
GROUP = 4
NEG = -1e30
NT = (((1,), (1,)), ((), ()))
F32 = jnp.float32
BF16 = jnp.bfloat16
SLOTS = 16
CORNER = 80
MIB = 1 << 20


def dot(a, b):
    return jnp.dot(a, b, preferred_element_type=F32)


def dot_nt(a, b):
    return lax.dot_general(a, b, NT, preferred_element_type=F32)


def in_hbm(x):
    return pltpu.with_memory_space_constraint(x, pltpu.HBM)


def room(mib):
    return pltpu.CompilerParams(vmem_limit_bytes=mib * MIB)


def iota2(shape, axis):
    return lax.broadcasted_iota(jnp.int32, shape, axis)


def hot(mask):
    return mask.astype(F32).astype(BF16)


def over(x, n):
    if n & (n - 1) == 0:
        return x >> (n.bit_length() - 1), x & (n - 1)
    return x // n, x % n


def down_iota(n):
    return iota2((n, 1), 0)


def along_iota(n):
    return iota2((1, n), 1)


def spread_heads(tile, cols, head_size):
    lane = over(iota2((cols, tile.shape[1]), 1), head_size)[0]
    zero = jnp.zeros((cols, tile.shape[1]), tile.dtype)
    parts = []
    for i in range(TILE):
        rows = tile[i * cols : (i + 1) * cols]
        for h in range(GROUP):
            parts.append(jnp.where(lane == h, rows, zero))
    return jnp.concatenate(parts, 0)


def head_mask(cols, head_size):
    shape = (GROUP * head_size, TILE * GROUP * cols)
    column = over(over(iota2(shape, 1), cols)[0], GROUP)[1]
    return over(iota2(shape, 0), head_size)[0] == column


def picker(cols):
    row_i, row_j = over(down_iota(TILE * cols), cols)
    high, col_j = over(along_iota(TILE * GROUP * cols), cols)
    return hot((row_i == over(high, GROUP)[0]) & (row_j == col_j))


def keep_rows(st, first_row, rows_all, cols_pad):
    parts = []
    for k in range(TILE + 2 * RAD):
        row = first_row + k
        inside = (row >= 0) & (row < rows_all)
        parts.append(jnp.where(inside, st[k * cols_pad : (k + 1) * cols_pad], NEG))
    return jnp.concatenate(parts, 0)


def take_cols(rows, cols, first):
    r, c = over(down_iota(rows * RAD), RAD)
    return hot(along_iota(rows * cols) == r * cols + first + c)


def put_cols(rows, cols, first):
    r, c = over(along_iota(rows * RAD), RAD)
    return hot(down_iota(rows * cols) == r * cols + first + c)


def put_corner(cols):
    n = along_iota(CORNER)
    half = RAD * RAD
    r, c = over(jnp.where(n < half, n, n - half), RAD)
    target = r * cols + c + jnp.where(n < half, 0, RAD)
    return hot((down_iota(RAD * cols) == target) & (n < 2 * half))


def pack_kernel(
    rows, cols, info_ref, k_hbm, v_hbm, east_ref, west_ref, a_ref, b_ref, x_ref, sem_ref
):
    copies = [
        pltpu.make_async_copy(ref, x_ref.at[i], sem_ref.at[i])
        for i, ref in enumerate((k_hbm, v_hbm))
    ]
    for copy in copies:
        copy.start()
    pick_east = take_cols(rows, cols, cols - RAD)
    pick_west = take_cols(rows, cols, 0)
    edge = RAD * cols
    odd = info_ref[2] == 1
    for i, copy in enumerate(copies):
        copy.wait()
        x = x_ref[i]
        east_ref[i] = dot(pick_east, x).astype(BF16)
        west_ref[i] = dot(pick_west, x).astype(BF16)
        down = x[(rows - RAD) * cols :]
        up = x[:edge]
        a_ref[i] = jnp.where(odd, up, down)
        b_ref[i] = jnp.where(odd, down, up)


def corner_kernel(rows, own, info_ref, w_ref, e_ref, *refs):
    out_ref = refs[-1]
    half = RAD * RAD
    n = down_iota(CORNER)
    src = along_iota(rows * RAD)
    odd = info_ref[2] == 1
    up = odd if own else jnp.logical_not(odd)
    first = jnp.where(up, 0, (rows - RAD) * RAD)
    pick_w = hot((src == first + n) & (n < half))
    pick_e = hot((src == first + n - half) & (n >= half) & (n < 2 * half))
    for i in range(2):
        side = dot(pick_w, w_ref[i]) + dot(pick_e, e_ref[i])
        edge = out_ref.shape[1] - CORNER
        if own:
            out_ref[i, :edge, :] = refs[0][i]
        out_ref[i, edge:, :] = side.astype(BF16)


def prepare_kernel(
    cols, cols_pad, rel_ref, cot_hbm, w_hbm, out_ref, grad_ref, c_ref, r_ref, cot_ref, w_ref,
    sem_ref,
):
    copies = [
        pltpu.make_async_copy(cot_hbm, cot_ref, sem_ref.at[0]),
        pltpu.make_async_copy(w_hbm, w_ref, sem_ref.at[1]),
    ]
    for copy in copies:
        copy.start()
    heads = rel_ref.shape[1]
    lanes = heads * cols
    half = lanes // 2
    shape = (cols_pad, lanes)
    offset = slot_offset(shape, cols)
    inside = (offset >= 0) & (offset < SPAN)
    head = over(iota2((1, lanes), 1), cols)[0]
    for a in range(SPAN):
        tile = jnp.full(shape, NEG, F32)
        for b in range(SPAN):
            row = jnp.full((1, lanes), rel_ref[a, 0, b], F32)
            for h in range(1, heads):
                row = jnp.where(head == h, rel_ref[a, h, b], row)
            tile = jnp.where(offset == b, row, tile)
        tile = jnp.where(inside, tile, NEG)
        c_ref[a] = tile
        r_ref[a] = pltpu.roll(tile, half, 1)
    low = iota2(shape, 1) < half
    blank = jnp.full(shape, NEG, F32)
    for g in range(2):
        first, second = (c_ref, r_ref) if g == 0 else (r_ref, c_ref)
        for pair in range(TILE // 2):
            i = 2 * pair
            lo = (g * TILE // 2 + pair) * lanes
            for k in range(TILE + 2 * RAD):
                a = k - i
                one = first[a] if 0 <= a < SPAN else blank
                two = second[a - 1] if 0 <= a - 1 < SPAN else blank
                out_ref[k * cols_pad : (k + 1) * cols_pad, lo : lo + lanes] = jnp.where(
                    low, one, two
                )
    for copy in copies:
        copy.wait()
    grad_ref[...] = dot_nt(cot_ref[...], w_ref[...]).astype(BF16)


def slot_offset(shape, cols):
    slot = iota2(shape, 0)
    pos = jnp.where(slot < cols, slot + RAD, jnp.where(slot < cols + RAD, slot - cols, slot))
    pos = jnp.where(slot < cols + 2 * RAD, pos, -1000)
    return pos - over(iota2(shape, 1), cols)[1]


def assemble(out_ref, i, rows, cols, cols_pad, own, refs, group, odd):
    w_ref, e_ref, a_ref, b_ref, c_ref = refs
    edge = RAD * cols
    side = dot(put_cols(rows, SLOTS, 0), w_ref[i, :, group])
    side = (side + dot(put_cols(rows, SLOTS, RAD), e_ref[i, :, group])).astype(BF16)
    for r in range(rows):
        lo = (RAD + r) * cols_pad
        out_ref[lo : lo + cols, :] = own[r * cols : (r + 1) * cols, group]
        out_ref[lo + cols : lo + cols + SLOTS, :] = side[r * SLOTS : (r + 1) * SLOTS]
    put = put_corner(SLOTS)
    below = (RAD + rows) * cols_pad
    corner_a = a_ref[i, edge:, group]
    for first, o_ref, corner in (
        (jnp.where(odd, 0, below), a_ref, corner_a),
        (jnp.where(odd, below, 0), b_ref, c_ref[i, :, group]),
    ):
        side = dot(put, corner).astype(BF16)
        for r in range(RAD):
            lo = pl.multiple_of(first + r * cols_pad, cols_pad)
            out_ref[pl.ds(lo, cols), :] = o_ref[i, r * cols : (r + 1) * cols, group]
            lo = pl.multiple_of(first + r * cols_pad + cols, cols)
            out_ref[pl.ds(lo, SLOTS), :] = side[r * SLOTS : (r + 1) * SLOTS]


def group_lanes(group, lanes):
    return pl.ds(pl.multiple_of(group * lanes, lanes), lanes)


def fwd_kernel(
    sizes, n, info_ref, q_ref, k_ref, v_ref, w_ref, e_ref, a_ref, b_ref, c_ref,
    bias_ref, cot_ref, out_ref, weight_ref, p_ref, ko_ref, vo_ref, vt_ref, at_ref,
):
    lat_dev, cols, cols_pad, head_size, rows_all = sizes
    scale = head_size ** (-0.5)
    group = group_lanes(info_ref[n], GROUP * head_size)
    refs = (w_ref, e_ref, a_ref, b_ref, c_ref)
    odd = info_ref[2] == 1
    assemble(ko_ref, 0, lat_dev, cols, cols_pad, k_ref, refs, group, odd)
    assemble(vo_ref, 1, lat_dev, cols, cols_pad, v_ref, refs, group, odd)
    vt_ref[...] = vo_ref[...].T
    mask = head_mask(cols, head_size)
    pick = picker(cols)
    win = (TILE + 2 * RAD) * cols_pad
    for t in range(lat_dev // TILE):
        lo = t * TILE * cols_pad
        qs = pl.ds(t * TILE * cols, TILE * cols)
        q_bd = spread_heads(q_ref[qs, group] * jnp.asarray(scale, BF16), cols, head_size)
        first = info_ref[1] * lat_dev + t * TILE - RAD
        st = dot_nt(ko_ref[pl.ds(lo, win), :], q_bd) + bias_ref[:, group]
        st = keep_rows(st, first, rows_all, cols_pad)
        m = jnp.max(st, 0, keepdims=True)
        e = jnp.exp(st - m)
        p = e * (1.0 / jnp.sum(e, 0, keepdims=True))
        p_ref[t] = p
        ot = dot(vt_ref[:, pl.ds(lo, win)], p.astype(BF16))
        ot = jnp.where(mask, ot, 0.0).astype(BF16)
        out_ref[qs, :] = dot_nt(pick, ot).astype(BF16)
    at_ref[...] = out_ref[...].T
    weight_ref[...] = dot(at_ref[...], cot_ref[...]).astype(weight_ref.dtype)


def bwd_kernel(sizes, n, info_ref, q_ref, g_ref, p_ref, k_ref, v_ref, *refs):
    dq_ref, sa_ref, sb_ref, mid_ref, side_ref, x_ref, kt_ref, dk_ref, dv_ref, db_ref = refs[-10:]
    before = refs[:-10]
    lat_dev, cols, cols_pad, head_size, rows_all = sizes
    scale = head_size ** (-0.5)
    mask = head_mask(cols, head_size)
    pick = picker(cols)
    win = (TILE + 2 * RAD) * cols_pad
    half = GROUP * cols
    low = iota2((cols_pad, 2 * half), 1) < half
    which = info_ref[n]
    group = group_lanes(which, GROUP * head_size)
    mine = group if before else slice(None)
    if before:
        other = group_lanes(1 - which, GROUP * head_size)
        dq_ref[:, other] = before[0][...]
        sa_ref[:, :, other] = before[1][...]
        sb_ref[:, :, other] = before[2][...]
    kt_ref[...] = k_ref[...].T
    dk_ref[...] = jnp.zeros_like(dk_ref)
    dv_ref[...] = jnp.zeros_like(dv_ref)
    for t in range(lat_dev // TILE):
        lo = t * TILE * cols_pad
        qs = pl.ds(t * TILE * cols, TILE * cols)
        ws = pl.ds(lo, win)
        q_bd = spread_heads(q_ref[qs, group] * jnp.asarray(scale, BF16), cols, head_size)
        g_bd = spread_heads(g_ref[qs, group], cols, head_size)
        p = p_ref[t]
        slope = dot_nt(v_ref[ws, :], g_bd)
        inner = jnp.sum(p * slope, 0, keepdims=True)
        sg = p * (slope - inner)
        if t == 0:
            db_ref[...] = sg
        else:
            db_ref[...] += sg
        sgb = sg.astype(BF16)
        dqt = jnp.where(mask, dot(kt_ref[:, ws], sgb) * scale, 0.0).astype(BF16)
        dq_ref[qs, mine] = dot_nt(pick, dqt).astype(BF16)
        dk_ref[ws, :] += dot(sgb, q_bd)
        dv_ref[ws, :] += dot(p.astype(BF16), g_bd)
    edge = RAD * cols_pad
    odd = info_ref[2] == 1
    low_rows = edge + lat_dev * cols_pad
    first_a = pl.multiple_of(jnp.where(odd, 0, low_rows), cols_pad)
    first_b = pl.multiple_of(jnp.where(odd, low_rows, 0), cols_pad)
    for i, ref in enumerate((dk_ref, dv_ref)):
        sa_ref[i, :, mine] = ref[pl.ds(first_a, edge), :].astype(BF16)
        sb_ref[i, :, mine] = ref[pl.ds(first_b, edge), :].astype(BF16)
        for r in range(lat_dev):
            lo = (RAD + r) * cols_pad
            mid_ref[i, r * cols : (r + 1) * cols, :] = ref[lo : lo + cols, :]
            side_ref[i, r * SLOTS : (r + 1) * SLOTS, :] = ref[lo + cols : lo + cols_pad, :]
    for a in range(SPAN):
        total = jnp.zeros((cols_pad, 2 * half), F32)
        for pair in range(TILE // 2):
            i = 2 * pair
            lanes = slice(pair * 2 * half, (pair + 1) * 2 * half)
            one = db_ref[(a + i) * cols_pad : (a + i + 1) * cols_pad, lanes]
            two = db_ref[(a + i + 1) * cols_pad : (a + i + 2) * cols_pad, lanes]
            total = total + jnp.where(low, one, two)
        x_ref[a * cols_pad : (a + 1) * cols_pad, :] = total


def bias_kernel(cols, cols_pad, info_ref, xs_ref, xk_ref, out_ref, z_ref):
    lanes = xs_ref.shape[1]
    half = lanes // 2
    shape = (cols_pad, lanes)
    low = (over(iota2(shape, 1), half)[0] == info_ref[0])
    offset = slot_offset(shape, cols)
    z_ref[...] = jnp.zeros_like(z_ref)
    for a in range(SPAN):
        rows = slice(a * cols_pad, (a + 1) * cols_pad)
        one = xs_ref[rows, :]
        two = xk_ref[rows, :]
        both = jnp.where(low, one + pltpu.roll(one, half, 1), two + pltpu.roll(two, half, 1))
        for b in range(SPAN):
            n = a * SPAN + b
            z_ref[n : n + 1, :] = jnp.sum(jnp.where(offset == b, both, 0.0), 0, keepdims=True)
    heads = out_ref.shape[0]
    pick = (over(iota2((heads, lanes), 1), cols)[0] == iota2((heads, lanes), 0)).astype(F32)
    out_ref[...] = lax.dot_general(
        pick, z_ref[...], NT, precision=lax.Precision.HIGHEST, preferred_element_type=F32
    )


def lat_terms(ref, i, rows, cols, cols_pad, first):
    parts = []
    for r in range(RAD):
        lo = r * cols_pad + first
        parts.append(ref[i, lo : lo + cols, :])
    return jnp.concatenate(parts, 0).astype(F32)


def strips(info_ref, rows, cols):
    odd = info_ref[2] == 1
    last = (rows - RAD) * cols
    return [pl.multiple_of(jnp.where(odd, x, last - x), cols) for x in (0, last)]


def both_groups(info_ref, dst_ref, i, s_ref, k_ref):
    lanes = s_ref.shape[2]
    dst_ref[:, group_lanes(info_ref[0], lanes)] = s_ref[i]
    dst_ref[:, group_lanes(1 - info_ref[0], lanes)] = k_ref[i]


def side_kernel(
    rows, cols, cols_pad, info_ref, ss_ref, sk_ref, a_ref, b_ref, west_ref, east_ref, s_ref
):
    edge = RAD * SLOTS
    pick_west = take_cols(rows, SLOTS, 0)
    pick_east = take_cols(rows, SLOTS, RAD)
    for i in range(2):
        both_groups(info_ref, s_ref, i, ss_ref, sk_ref)
        for ref, first in zip((a_ref, b_ref), strips(info_ref, rows, SLOTS)):
            s_ref[pl.ds(first, edge), :] += lat_terms(ref, i, rows, SLOTS, cols_pad, cols)
        x = s_ref[...].astype(BF16)
        west_ref[i] = dot(pick_west, x).astype(BF16)
        east_ref[i] = dot(pick_east, x).astype(BF16)


def join_kernel(
    rows, cols, cols_pad, info_ref, ms_ref, mk_ref, a_ref, b_ref, w_ref, e_ref,
    k_ref, v_ref, s_ref,
):
    edge = RAD * cols
    put_west = put_cols(rows, cols, 0)
    put_east = put_cols(rows, cols, cols - RAD)
    for i, out_ref in enumerate((k_ref, v_ref)):
        both_groups(info_ref, s_ref, i, ms_ref, mk_ref)
        s_ref[...] += dot(put_west, w_ref[i]) + dot(put_east, e_ref[i])
        for ref, first in zip((a_ref, b_ref), strips(info_ref, rows, cols)):
            s_ref[pl.ds(first, edge), :] += lat_terms(ref, i, rows, cols, cols_pad, 0)
        out_ref[...] = s_ref[...].astype(BF16)


def bits_of(mesh_shape):
    order = []
    for axis in ("lat", "lon"):
        bit = 1
        while bit < mesh_shape[axis]:
            order.append((axis, bit))
            bit *= 2
    return order


def rounds_of(mesh_shape):
    first, *rest = bits_of(mesh_shape)
    middle, ends = rest[:-2], rest[-2:]
    turned = middle[1:] + middle[:1]
    return [(first, first)] + list(zip(middle, turned)), list(zip(ends, ends[::-1]))


def partner_pairs(mesh_shape, bits):
    n_lat, n_lon = mesh_shape["lat"], mesh_shape["lon"]
    pairs = []
    for i in range(n_lat):
        axis, bit = bits[i % 2]
        for j in range(n_lon):
            a, b = (i ^ bit, j) if axis == "lat" else (i, j ^ bit)
            pairs.append((i * n_lon + j, a * n_lon + b))
    return pairs


def swap(x, mesh_shape, bits):
    return lax.ppermute(x, ("lat", "lon"), partner_pairs(mesh_shape, bits))


def my_bit(bits):
    def of(axis, bit):
        return (lax.axis_index(axis) // bit) % 2

    odd = lax.axis_index("lat") % 2
    return jnp.where(odd == 0, of(*bits[0]), of(*bits[1]))


def put_bias(ref, rows, bias):
    heads, count = bias.shape
    high = bias.astype(BF16)
    ref[rows:, :count] = high
    ref[rows:, count : 2 * count] = (bias - high.astype(F32)).astype(BF16)
    ref[rows:, 2 * count :] = jnp.zeros((heads, ref.shape[1] - 2 * count), BF16)


def get_bias(ref, rows, count):
    return ref[rows:, :count].astype(F32) + ref[rows:, count : 2 * count].astype(F32)


def halve_kernel(n, info_ref, keep_ref, got_ref, send_ref, out_ref):
    half = send_ref.shape[0]
    low = keep_ref[:half, :] + got_ref[:half, :].astype(F32)
    high = keep_ref[half:, :] + got_ref[half:, :].astype(F32)
    lower = info_ref[n] == 0
    send_ref[...] = jnp.where(lower, high, low).astype(BF16)
    out_ref[...] = jnp.where(lower, low, high)


def meet_kernel(keep_ref, got_ref, bias_ref, out_ref):
    rows = keep_ref.shape[0]
    out_ref[:rows, :] = (keep_ref[...] + got_ref[...].astype(F32)).astype(BF16)
    put_bias(out_ref, rows, bias_ref[...])


def total_kernel(norm, count, heads, own_ref, got_ref, out_ref):
    rows = own_ref.shape[0] - heads
    total = own_ref[:rows, :].astype(F32) + got_ref[:rows, :].astype(F32)
    out_ref[:rows, :] = (total if norm is None else total * norm).astype(BF16)
    put_bias(out_ref, rows, get_bias(own_ref, rows, count) + get_bias(got_ref, rows, count))


def grow_kernel(n, count, heads, info_ref, own_ref, got_ref, out_ref):
    rows = own_ref.shape[0] - heads
    lower = info_ref[n] == 0
    own = own_ref[:rows, :]
    got = got_ref[:rows, :]
    out_ref[:rows, :] = jnp.where(lower, own, got)
    out_ref[rows : 2 * rows, :] = jnp.where(lower, got, own)
    put_bias(out_ref, 2 * rows, get_bias(own_ref, rows, count) + get_bias(got_ref, rows, count))


def last_kernel(n, norm, count, info_ref, own_ref, got_ref, out_ref, bias_ref):
    rows = out_ref.shape[0] // 2
    lower = info_ref[n] == 0
    own = own_ref[:rows, :]
    got = got_ref[:rows, :]
    out_ref[:rows, :] = jnp.where(lower, own, got)
    out_ref[rows:, :] = jnp.where(lower, got, own)
    bias = (get_bias(own_ref, rows, count) + get_bias(got_ref, rows, count)) * norm
    for a in range(SPAN):
        bias_ref[a] = bias[:, a * SPAN : (a + 1) * SPAN]


def project_kernel(info_ref, s_ref, k_ref, w_ref, out_ref):
    rows = s_ref.shape[1]
    first = pl.ds(pl.multiple_of(info_ref[0] * rows, rows), rows)
    second = pl.ds(pl.multiple_of((1 - info_ref[0]) * rows, rows), rows)
    out = dot(s_ref[...], w_ref[first, :]) + dot(k_ref[...], w_ref[second, :])
    out_ref[...] = out.astype(BF16)


def shards(mesh_shape, queries, keys, values, rel_bias, out_weight, cotangent):
    lat_dev, lon_dev, width = queries.shape
    heads = rel_bias.shape[0]
    head_size = width // heads
    groups = heads // GROUP
    lanes = GROUP * head_size
    model = out_weight.shape[1]
    n_lat, n_lon = mesh_shape["lat"], mesh_shape["lon"]
    cols_pad = lon_dev + SLOTS
    outer_lat = lat_dev + 2 * RAD
    tokens = lat_dev * lon_dev
    norm = (tokens * n_lat * n_lon) ** (-0.5)
    east = [(i, (i + 1) % n_lon) for i in range(n_lon)]
    west = [(i, (i - 1) % n_lon) for i in range(n_lon)]
    pair_a = [(i, i ^ 1) for i in range(n_lat)]
    pair_b = [(i, i + 1) for i in range(1, n_lat - 1, 2)]
    pair_b = pair_b + [(j, i) for i, j in pair_b]
    win = (TILE + 2 * RAD) * cols_pad
    tiles = lat_dev // TILE
    lanes_q = TILE * GROUP * lon_dev
    n_keys = outer_lat * cols_pad
    n_side = lat_dev * RAD
    n_edge = RAD * lon_dev
    n_strip = RAD * cols_pad

    def shape(dims, dtype=BF16):
        return jax.ShapeDtypeStruct(dims, dtype)

    q_flat = queries.reshape(tokens, width)
    k_flat = keys.reshape(tokens, width)
    v_flat = values.reshape(tokens, width)
    cot = cotangent.reshape(tokens, model)

    lat_index = lax.axis_index("lat").astype(jnp.int32)
    core = lat_index % 2
    rounds, ends = rounds_of(mesh_shape)
    facts = [1 - core, lat_index, core] + [my_bit(bits) for bits in rounds]
    info = jnp.stack([x.astype(jnp.int32) for x in facts])
    smem = pl.BlockSpec(memory_space=pltpu.SMEM)
    vmem = pl.BlockSpec(memory_space=pltpu.VMEM)
    hbm = pl.BlockSpec(memory_space=pltpu.HBM)

    to_east, to_west, own_a, own_b = pl.pallas_call(
        functools.partial(pack_kernel, lat_dev, lon_dev),
        in_specs=[smem, hbm, hbm],
        out_shape=[shape((2, n_side, width))] * 2 + [shape((2, n_edge, width))] * 2,
        scratch_shapes=[pltpu.VMEM((2, tokens, width), BF16), pltpu.SemaphoreType.DMA((2,))],
        compiler_params=room(4),
        name="pack",
    )(info, in_hbm(k_flat), in_hbm(v_flat))
    from_west = lax.ppermute(to_east, "lon", east)
    from_east = lax.ppermute(to_west, "lon", west)
    from_b = lax.ppermute(own_b, "lat", pair_b)
    sizes = (lat_dev, lon_dev, cols_pad, head_size, lat_dev * n_lat)
    table, attended_grad = pl.pallas_call(
        functools.partial(prepare_kernel, lon_dev, cols_pad),
        in_specs=[smem, hbm, hbm],
        out_shape=[shape((win, groups * lanes_q), F32), shape((tokens, width))],
        scratch_shapes=[pltpu.VMEM((SPAN, cols_pad, heads * lon_dev), F32)] * 2
        + [pltpu.VMEM((tokens, model), BF16), pltpu.VMEM((width, model), BF16)]
        + [pltpu.SemaphoreType.DMA((2,))],
        compiler_params=room(6),
        name="prepare",
    )(rel_bias.transpose(1, 0, 2), in_hbm(cot), in_hbm(out_weight))
    from_west, from_east, from_b, table = lax.optimization_barrier(
        (from_west, from_east, from_b, table)
    )

    def corner(rows, *own):
        return pl.pallas_call(
            functools.partial(corner_kernel, lat_dev, bool(own)),
            in_specs=[smem] + [vmem] * (2 + len(own)),
            out_shape=shape((2, rows, width)),
            compiler_params=room(4),
            name="corner",
        )(info, from_west, from_east, *own)

    corner_b = corner(CORNER)
    corner_b, own_a = lax.optimization_barrier((corner_b, own_a))
    side_b = lax.ppermute(corner_b, "lat", pair_b)
    from_a = lax.ppermute(corner(n_edge + CORNER, own_a), "lat", pair_a)
    probs = (tiles, win, lanes_q)
    outer = (n_keys, lanes)

    def forward(n, dtype):
        return pl.pallas_call(
            functools.partial(fwd_kernel, sizes, n),
            in_specs=[smem] + [vmem] * 10,
            out_shape=[shape((tokens, lanes)), shape((lanes, model), dtype), shape(probs, F32)]
            + [shape(outer)] * 2,
            scratch_shapes=[pltpu.VMEM((lanes, n_keys), BF16), pltpu.VMEM((lanes, tokens), BF16)],
            compiler_params=room(8),
            name="attend_fwd",
        )(
            info, q_flat, k_flat, v_flat, from_west, from_east,
            from_a, from_b, side_b, table, cot,
        )

    def step_call(kernel, name, outs, *operands):
        scalars = [smem if x.dtype == jnp.int32 else vmem for x in operands]
        return pl.pallas_call(
            kernel, in_specs=scalars, out_shape=outs, compiler_params=room(4), name=name
        )(*operands)

    att_s, weight_s, p_s, k_s, v_s = forward(0, BF16)
    got = swap(weight_s, mesh_shape, rounds[0])
    att_k, keep, p_k, k_k, v_k = forward(2, F32)

    def halve(keep, got, number):
        half = (keep.shape[0] // 2, model)
        outs = [shape(half), shape(half, F32)]
        kernel = functools.partial(halve_kernel, 3 + number)
        return step_call(kernel, "halve", outs, info, keep, got)

    send, keep = halve(keep, got, 1)
    def backward(n, info, p, k, v, *before):
        size = width if before else lanes
        return pl.pallas_call(
            functools.partial(bwd_kernel, sizes, n),
            in_specs=[smem] + [vmem] * (5 + len(before)),
            out_shape=[shape((tokens, size))]
            + [shape((2, n_strip, size))] * 2
            + [shape((2, tokens, lanes), F32)] * 2
            + [shape((SPAN * cols_pad, 2 * GROUP * lon_dev), F32)],
            scratch_shapes=[pltpu.VMEM((lanes, n_keys), BF16)]
            + [pltpu.VMEM((n_keys, lanes), F32)] * 2
            + [pltpu.VMEM((win, lanes_q), F32)],
            compiler_params=room(10),
            name="attend_bwd",
        )(info, q_flat, attended_grad, p, k, v, *before)

    info_b, send = lax.optimization_barrier((info, send))
    got = swap(send, mesh_shape, rounds[1])
    *before, mid_s, side_s, fold_s = backward(0, info_b, p_s, k_s, v_s)
    got, fold_s = lax.optimization_barrier((got, fold_s))
    for number in range(2, len(rounds)):
        send, keep = halve(keep, got, number)
        if number == 2:
            info_b, send = lax.optimization_barrier((info, send))
        got = swap(send, mesh_shape, rounds[number])
    after = backward(2, info_b, p_k, k_k, v_k, *before)
    query_grad, strip_a, strip_b, mid_k, side_k, fold_k = after
    got, strip_a, strip_b, fold_k = lax.optimization_barrier((got, strip_a, strip_b, fold_k))
    get_b = lax.ppermute(strip_b, "lat", pair_b)
    get_a = lax.ppermute(strip_a, "lat", pair_a)

    count = 256
    bias_local = pl.pallas_call(
        functools.partial(bias_kernel, lon_dev, cols_pad),
        in_specs=[smem, vmem, vmem],
        out_shape=shape((heads, count), F32),
        scratch_shapes=[pltpu.VMEM((count, heads * lon_dev), F32)],
        compiler_params=room(4),
        name="bias_fold",
    )(info, fold_s, fold_k)
    block_out = pl.pallas_call(
        project_kernel,
        in_specs=[smem] + [vmem] * 3,
        out_shape=shape((tokens, model)),
        compiler_params=room(6),
        name="project",
    )(info, att_s, att_k, out_weight)
    note = shape((keep.shape[0] + heads, model))
    message = step_call(meet_kernel, "meet", note, keep, got, bias_local)
    got = swap(message, mesh_shape, ends[0])
    kernel = functools.partial(total_kernel, None, count, heads)
    message = step_call(kernel, "total", note, message, got)
    message, get_a, get_b, block_out = lax.optimization_barrier(
        (message, get_a, get_b, block_out)
    )
    got = swap(message, mesh_shape, ends[1])
    give_west, give_east = pl.pallas_call(
        functools.partial(side_kernel, lat_dev, lon_dev, cols_pad),
        in_specs=[smem] + [vmem] * 4,
        out_shape=[shape((2, n_side, width))] * 2,
        scratch_shapes=[pltpu.VMEM((tokens, width), F32)],
        compiler_params=room(6),
        name="side",
    )(info, side_s, side_k, get_a, get_b)
    get_east = lax.ppermute(give_west, "lon", west)
    get_west = lax.ppermute(give_east, "lon", east)
    kernel = functools.partial(total_kernel, norm, count, heads)
    message = step_call(kernel, "total", note, message, got)
    message, give_west, give_east = lax.optimization_barrier((message, give_west, give_east))

    for number in range(len(rounds) - 1, 0, -1):
        if number == 1:
            message, get_east, get_west = lax.optimization_barrier((message, get_east, get_west))
        got = swap(message, mesh_shape, rounds[number])
        note = shape((2 * message.shape[0] - heads, model))
        kernel = functools.partial(grow_kernel, 3 + number, count, heads)
        message = step_call(kernel, "grow", note, info, message, got)
    key_grad, value_grad = pl.pallas_call(
        functools.partial(join_kernel, lat_dev, lon_dev, cols_pad),
        in_specs=[smem] + [vmem] * 6,
        out_shape=[shape((tokens, width))] * 2,
        scratch_shapes=[pltpu.VMEM((tokens, width), F32)],
        compiler_params=room(6),
        name="join",
    )(info, mid_s, mid_k, get_a, get_b, get_west, get_east)
    got = swap(message, mesh_shape, rounds[0])
    weight_grad, bias_grad = step_call(
        functools.partial(last_kernel, 3, norm, count),
        "last",
        [shape((width, model)), shape((SPAN, heads, SPAN), F32)],
        info, message, got,
    )
    return (
        block_out.reshape(lat_dev, lon_dev, model),
        query_grad.reshape(queries.shape),
        key_grad.reshape(keys.shape),
        value_grad.reshape(values.shape),
        weight_grad,
        bias_grad.transpose(1, 0, 2),
    )


def solution(mesh):
    spec = P("lat", "lon", None)
    return jax.shard_map(
        functools.partial(shards, dict(mesh.shape)),
        mesh=mesh,
        in_specs=(spec, spec, spec, P(), P(), spec),
        out_specs=(spec, spec, spec, spec, P(), P()),
        check_vma=False,
    )
```

```python
import functools

import jax
import jax.numpy as jnp
from jax import lax
from jax.experimental import pallas as pl
from jax.experimental.pallas import tpu as pltpu
from jax.sharding import PartitionSpec as P

RAD = 6
SPAN = 2 * RAD + 1
TILE = 4
GROUP = 4
NEG = -1e30
NT = (((1,), (1,)), ((), ()))
F32 = jnp.float32
BF16 = jnp.bfloat16
SLOTS = 16
CORNER = 80
MIB = 1 << 20


def dot(a, b):
    return jnp.dot(a, b, preferred_element_type=F32)


def dot_nt(a, b):
    return lax.dot_general(a, b, NT, preferred_element_type=F32)


def in_hbm(x):
    return pltpu.with_memory_space_constraint(x, pltpu.HBM)


def room(mib):
    return pltpu.CompilerParams(vmem_limit_bytes=mib * MIB)


def iota2(shape, axis):
    return lax.broadcasted_iota(jnp.int32, shape, axis)


def hot(mask):
    return mask.astype(F32).astype(BF16)


def over(x, n):
    if n & (n - 1) == 0:
        return x >> (n.bit_length() - 1), x & (n - 1)
    return x // n, x % n


def down_iota(n):
    return iota2((n, 1), 0)


def along_iota(n):
    return iota2((1, n), 1)


def spread_heads(tile, cols, head_size):
    lane = over(iota2((cols, tile.shape[1]), 1), head_size)[0]
    zero = jnp.zeros((cols, tile.shape[1]), tile.dtype)
    parts = []
    for i in range(TILE):
        rows = tile[i * cols : (i + 1) * cols]
        for h in range(GROUP):
            parts.append(jnp.where(lane == h, rows, zero))
    return jnp.concatenate(parts, 0)


def head_mask(cols, head_size):
    shape = (GROUP * head_size, TILE * GROUP * cols)
    column = over(over(iota2(shape, 1), cols)[0], GROUP)[1]
    return over(iota2(shape, 0), head_size)[0] == column


def picker(cols):
    row_i, row_j = over(down_iota(TILE * cols), cols)
    high, col_j = over(along_iota(TILE * GROUP * cols), cols)
    return hot((row_i == over(high, GROUP)[0]) & (row_j == col_j))


def keep_rows(st, first_row, rows_all, cols_pad):
    parts = []
    for k in range(TILE + 2 * RAD):
        row = first_row + k
        inside = (row >= 0) & (row < rows_all)
        parts.append(jnp.where(inside, st[k * cols_pad : (k + 1) * cols_pad], NEG))
    return jnp.concatenate(parts, 0)


def take_cols(rows, cols, first):
    r, c = over(down_iota(rows * RAD), RAD)
    return hot(along_iota(rows * cols) == r * cols + first + c)


def put_cols(rows, cols, first):
    r, c = over(along_iota(rows * RAD), RAD)
    return hot(down_iota(rows * cols) == r * cols + first + c)


def put_corner(cols):
    n = along_iota(CORNER)
    half = RAD * RAD
    r, c = over(jnp.where(n < half, n, n - half), RAD)
    target = r * cols + c + jnp.where(n < half, 0, RAD)
    return hot((down_iota(RAD * cols) == target) & (n < 2 * half))


def pack_kernel(
    rows, cols, info_ref, k_hbm, v_hbm, east_ref, west_ref, a_ref, b_ref, x_ref, sem_ref
):
    copies = [
        pltpu.make_async_copy(ref, x_ref.at[i], sem_ref.at[i])
        for i, ref in enumerate((k_hbm, v_hbm))
    ]
    for copy in copies:
        copy.start()
    pick_east = take_cols(rows, cols, cols - RAD)
    pick_west = take_cols(rows, cols, 0)
    edge = RAD * cols
    odd = info_ref[2] == 1
    for i, copy in enumerate(copies):
        copy.wait()
        x = x_ref[i]
        east_ref[i] = dot(pick_east, x).astype(BF16)
        west_ref[i] = dot(pick_west, x).astype(BF16)
        down = x[(rows - RAD) * cols :]
        up = x[:edge]
        a_ref[i] = jnp.where(odd, up, down)
        b_ref[i] = jnp.where(odd, down, up)


def corner_kernel(rows, cols, info_ref, w_ref, e_ref, own_ref, a_ref, b_ref):
    half = RAD * RAD
    edge = RAD * cols
    n = down_iota(CORNER)
    src = along_iota(rows * RAD)
    odd = info_ref[2] == 1
    last = (rows - RAD) * RAD
    a_ref[:, :edge, :] = own_ref[...]
    for ref, lo, first in (
        (b_ref, 0, jnp.where(odd, last, 0)),
        (a_ref, edge, jnp.where(odd, 0, last)),
    ):
        pick_w = hot((src == first + n) & (n < half))
        pick_e = hot((src == first + n - half) & (n >= half) & (n < 2 * half))
        for i in range(2):
            side = dot(pick_w, w_ref[i]) + dot(pick_e, e_ref[i])
            ref[i, lo:, :] = side.astype(BF16)


def prepare_kernel(
    cols, cols_pad, rel_ref, cot_hbm, w_hbm, out_ref, grad_ref, c_ref, r_ref, cot_ref, w_ref,
    sem_ref,
):
    copies = [
        pltpu.make_async_copy(cot_hbm, cot_ref, sem_ref.at[0]),
        pltpu.make_async_copy(w_hbm, w_ref, sem_ref.at[1]),
    ]
    for copy in copies:
        copy.start()
    heads = rel_ref.shape[1]
    lanes = heads * cols
    half = lanes // 2
    shape = (cols_pad, lanes)
    offset = slot_offset(shape, cols)
    inside = (offset >= 0) & (offset < SPAN)
    head = over(iota2((1, lanes), 1), cols)[0]
    for a in range(SPAN):
        tile = jnp.full(shape, NEG, F32)
        for b in range(SPAN):
            row = jnp.full((1, lanes), rel_ref[a, 0, b], F32)
            for h in range(1, heads):
                row = jnp.where(head == h, rel_ref[a, h, b], row)
            tile = jnp.where(offset == b, row, tile)
        tile = jnp.where(inside, tile, NEG)
        c_ref[a] = tile
        r_ref[a] = pltpu.roll(tile, half, 1)
    low = iota2(shape, 1) < half
    blank = jnp.full(shape, NEG, F32)
    for g in range(2):
        first, second = (c_ref, r_ref) if g == 0 else (r_ref, c_ref)
        for pair in range(TILE // 2):
            i = 2 * pair
            lo = (g * TILE // 2 + pair) * lanes
            for k in range(TILE + 2 * RAD):
                a = k - i
                one = first[a] if 0 <= a < SPAN else blank
                two = second[a - 1] if 0 <= a - 1 < SPAN else blank
                out_ref[k * cols_pad : (k + 1) * cols_pad, lo : lo + lanes] = jnp.where(
                    low, one, two
                )
    for copy in copies:
        copy.wait()
    grad_ref[...] = dot_nt(cot_ref[...], w_ref[...]).astype(BF16)


def slot_offset(shape, cols):
    slot = iota2(shape, 0)
    pos = jnp.where(slot < cols, slot + RAD, jnp.where(slot < cols + RAD, slot - cols, slot))
    pos = jnp.where(slot < cols + 2 * RAD, pos, -1000)
    return pos - over(iota2(shape, 1), cols)[1]


def assemble(out_ref, i, rows, cols, cols_pad, own, refs, group, odd):
    w_ref, e_ref, a_ref, b_ref, c_ref = refs
    edge = RAD * cols
    side = dot(put_cols(rows, SLOTS, 0), w_ref[i, :, group])
    side = (side + dot(put_cols(rows, SLOTS, RAD), e_ref[i, :, group])).astype(BF16)
    for r in range(rows):
        lo = (RAD + r) * cols_pad
        out_ref[lo : lo + cols, :] = own[r * cols : (r + 1) * cols, group]
        out_ref[lo + cols : lo + cols + SLOTS, :] = side[r * SLOTS : (r + 1) * SLOTS]
    put = put_corner(SLOTS)
    below = (RAD + rows) * cols_pad
    corner_a = a_ref[i, edge:, group]
    for first, o_ref, corner in (
        (jnp.where(odd, 0, below), a_ref, corner_a),
        (jnp.where(odd, below, 0), b_ref, c_ref[i, :, group]),
    ):
        side = dot(put, corner).astype(BF16)
        for r in range(RAD):
            lo = pl.multiple_of(first + r * cols_pad, cols_pad)
            out_ref[pl.ds(lo, cols), :] = o_ref[i, r * cols : (r + 1) * cols, group]
            lo = pl.multiple_of(first + r * cols_pad + cols, cols)
            out_ref[pl.ds(lo, SLOTS), :] = side[r * SLOTS : (r + 1) * SLOTS]


def group_lanes(group, lanes):
    return pl.ds(pl.multiple_of(group * lanes, lanes), lanes)


def fwd_kernel(
    sizes, n, info_ref, q_ref, k_ref, v_ref, w_ref, e_ref, a_ref, b_ref, c_ref,
    bias_ref, cot_ref, out_ref, weight_ref, p_ref, ko_ref, vo_ref, vt_ref, at_ref,
):
    lat_dev, cols, cols_pad, head_size, rows_all = sizes
    scale = head_size ** (-0.5)
    group = group_lanes(info_ref[n], GROUP * head_size)
    refs = (w_ref, e_ref, a_ref, b_ref, c_ref)
    odd = info_ref[2] == 1
    assemble(ko_ref, 0, lat_dev, cols, cols_pad, k_ref, refs, group, odd)
    assemble(vo_ref, 1, lat_dev, cols, cols_pad, v_ref, refs, group, odd)
    vt_ref[...] = vo_ref[...].T
    mask = head_mask(cols, head_size)
    pick = picker(cols)
    win = (TILE + 2 * RAD) * cols_pad
    for t in range(lat_dev // TILE):
        lo = t * TILE * cols_pad
        qs = pl.ds(t * TILE * cols, TILE * cols)
        q_bd = spread_heads(q_ref[qs, group] * jnp.asarray(scale, BF16), cols, head_size)
        first = info_ref[1] * lat_dev + t * TILE - RAD
        st = dot_nt(ko_ref[pl.ds(lo, win), :], q_bd) + bias_ref[:, group]
        st = keep_rows(st, first, rows_all, cols_pad)
        m = jnp.max(st, 0, keepdims=True)
        e = jnp.exp(st - m)
        p = e * (1.0 / jnp.sum(e, 0, keepdims=True))
        p_ref[t] = p
        ot = dot(vt_ref[:, pl.ds(lo, win)], p.astype(BF16))
        ot = jnp.where(mask, ot, 0.0).astype(BF16)
        out_ref[qs, :] = dot_nt(pick, ot).astype(BF16)
    at_ref[...] = out_ref[...].T
    weight_ref[...] = dot(at_ref[...], cot_ref[...]).astype(weight_ref.dtype)


def bwd_kernel(sizes, n, info_ref, q_ref, g_ref, p_ref, k_ref, v_ref, *refs):
    dq_ref, sa_ref, sb_ref, mid_ref, side_ref, x_ref, kt_ref, dk_ref, dv_ref, db_ref = refs[-10:]
    before = refs[:-10]
    lat_dev, cols, cols_pad, head_size, rows_all = sizes
    scale = head_size ** (-0.5)
    mask = head_mask(cols, head_size)
    pick = picker(cols)
    win = (TILE + 2 * RAD) * cols_pad
    half = GROUP * cols
    low = iota2((cols_pad, 2 * half), 1) < half
    which = info_ref[n]
    group = group_lanes(which, GROUP * head_size)
    mine = group if before else slice(None)
    if before:
        other = group_lanes(1 - which, GROUP * head_size)
        dq_ref[:, other] = before[0][...]
        sa_ref[:, :, other] = before[1][...]
    kt_ref[...] = k_ref[...].T
    dk_ref[...] = jnp.zeros_like(dk_ref)
    dv_ref[...] = jnp.zeros_like(dv_ref)
    for t in range(lat_dev // TILE):
        lo = t * TILE * cols_pad
        qs = pl.ds(t * TILE * cols, TILE * cols)
        ws = pl.ds(lo, win)
        q_bd = spread_heads(q_ref[qs, group] * jnp.asarray(scale, BF16), cols, head_size)
        g_bd = spread_heads(g_ref[qs, group], cols, head_size)
        p = p_ref[t]
        slope = dot_nt(v_ref[ws, :], g_bd)
        inner = jnp.sum(p * slope, 0, keepdims=True)
        sg = p * (slope - inner)
        if t == 0:
            db_ref[...] = sg
        else:
            db_ref[...] += sg
        sgb = sg.astype(BF16)
        dqt = jnp.where(mask, dot(kt_ref[:, ws], sgb) * scale, 0.0).astype(BF16)
        dq_ref[qs, mine] = dot_nt(pick, dqt).astype(BF16)
        dk_ref[ws, :] += dot(sgb, q_bd)
        dv_ref[ws, :] += dot(p.astype(BF16), g_bd)
    edge = RAD * cols_pad
    odd = info_ref[2] == 1
    low_rows = edge + lat_dev * cols_pad
    first_a = pl.multiple_of(jnp.where(odd, 0, low_rows), cols_pad)
    first_b = pl.multiple_of(jnp.where(odd, low_rows, 0), cols_pad)
    for i, ref in enumerate((dk_ref, dv_ref)):
        sa_ref[i, :, mine] = ref[pl.ds(first_a, edge), :].astype(BF16)
        sb_ref[i] = ref[pl.ds(first_b, edge), :].astype(BF16)
        for r in range(lat_dev):
            lo = (RAD + r) * cols_pad
            mid_ref[i, r * cols : (r + 1) * cols, :] = ref[lo : lo + cols, :]
            side_ref[i, r * SLOTS : (r + 1) * SLOTS, :] = ref[lo + cols : lo + cols_pad, :]
    for a in range(SPAN):
        total = jnp.zeros((cols_pad, 2 * half), F32)
        for pair in range(TILE // 2):
            i = 2 * pair
            lanes = slice(pair * 2 * half, (pair + 1) * 2 * half)
            one = db_ref[(a + i) * cols_pad : (a + i + 1) * cols_pad, lanes]
            two = db_ref[(a + i + 1) * cols_pad : (a + i + 2) * cols_pad, lanes]
            total = total + jnp.where(low, one, two)
        x_ref[a * cols_pad : (a + 1) * cols_pad, :] = total


def bias_kernel(cols, cols_pad, info_ref, xs_ref, xk_ref, out_ref, z_ref):
    lanes = xs_ref.shape[1]
    half = lanes // 2
    shape = (cols_pad, lanes)
    low = (over(iota2(shape, 1), half)[0] == info_ref[0])
    offset = slot_offset(shape, cols)
    z_ref[...] = jnp.zeros_like(z_ref)
    for a in range(SPAN):
        rows = slice(a * cols_pad, (a + 1) * cols_pad)
        one = xs_ref[rows, :]
        two = xk_ref[rows, :]
        both = jnp.where(low, one + pltpu.roll(one, half, 1), two + pltpu.roll(two, half, 1))
        for b in range(SPAN):
            n = a * SPAN + b
            z_ref[n : n + 1, :] = jnp.sum(jnp.where(offset == b, both, 0.0), 0, keepdims=True)
    heads = out_ref.shape[0]
    pick = (over(iota2((heads, lanes), 1), cols)[0] == iota2((heads, lanes), 0)).astype(F32)
    out_ref[...] = lax.dot_general(
        pick, z_ref[...], NT, precision=lax.Precision.HIGHEST, preferred_element_type=F32
    )


def lat_terms(ref, i, rows, cols, cols_pad, first):
    parts = []
    for r in range(RAD):
        lo = r * cols_pad + first
        parts.append(ref[i, lo : lo + cols, :])
    return jnp.concatenate(parts, 0).astype(F32)


def strips(info_ref, rows, cols):
    odd = info_ref[2] == 1
    last = (rows - RAD) * cols
    return [pl.multiple_of(jnp.where(odd, x, last - x), cols) for x in (0, last)]


def both_lanes(info_ref, lanes):
    return group_lanes(info_ref[0], lanes), group_lanes(1 - info_ref[0], lanes)


def both_groups(info_ref, dst_ref, i, *refs):
    for ref, group in zip(refs, both_lanes(info_ref, refs[0].shape[2])):
        dst_ref[:, group] = ref[i]


def side_kernel(
    rows, cols, cols_pad, info_ref, ss_ref, sk_ref, a_ref, bk_ref, bs_ref, west_ref, east_ref,
    s_ref,
):
    edge = RAD * SLOTS
    pick_west = take_cols(rows, SLOTS, 0)
    pick_east = take_cols(rows, SLOTS, RAD)
    for i in range(2):
        both_groups(info_ref, s_ref, i, ss_ref, sk_ref)
        first_a, first_b = strips(info_ref, rows, SLOTS)
        s_ref[pl.ds(first_a, edge), :] += lat_terms(a_ref, i, rows, SLOTS, cols_pad, cols)
        for ref, group in zip((bk_ref, bs_ref), both_lanes(info_ref, bs_ref.shape[2])):
            s_ref[pl.ds(first_b, edge), group] += lat_terms(ref, i, rows, SLOTS, cols_pad, cols)
        x = s_ref[...].astype(BF16)
        west_ref[i] = dot(pick_west, x).astype(BF16)
        east_ref[i] = dot(pick_east, x).astype(BF16)


def join_kernel(
    rows, cols, cols_pad, info_ref, ms_ref, mk_ref, a_ref, bk_ref, bs_ref, w_ref, e_ref,
    k_ref, v_ref, s_ref,
):
    edge = RAD * cols
    put_west = put_cols(rows, cols, 0)
    put_east = put_cols(rows, cols, cols - RAD)
    for i, out_ref in enumerate((k_ref, v_ref)):
        both_groups(info_ref, s_ref, i, ms_ref, mk_ref)
        s_ref[...] += dot(put_west, w_ref[i]) + dot(put_east, e_ref[i])
        first_a, first_b = strips(info_ref, rows, cols)
        s_ref[pl.ds(first_a, edge), :] += lat_terms(a_ref, i, rows, cols, cols_pad, 0)
        for ref, group in zip((bk_ref, bs_ref), both_lanes(info_ref, bs_ref.shape[2])):
            s_ref[pl.ds(first_b, edge), group] += lat_terms(ref, i, rows, cols, cols_pad, 0)
        out_ref[...] = s_ref[...].astype(BF16)


def bits_of(mesh_shape):
    order = []
    for axis in ("lat", "lon"):
        bit = 1
        while bit < mesh_shape[axis]:
            order.append((axis, bit))
            bit *= 2
    return order


def rounds_of(mesh_shape):
    first, *rest = bits_of(mesh_shape)
    middle, ends = rest[:-2], rest[-2:]
    turned = middle[1:] + middle[:1]
    return [(first, first)] + list(zip(middle, turned)), list(zip(ends, ends[::-1]))


def partner_pairs(mesh_shape, bits):
    n_lat, n_lon = mesh_shape["lat"], mesh_shape["lon"]
    pairs = []
    for i in range(n_lat):
        axis, bit = bits[i % 2]
        for j in range(n_lon):
            a, b = (i ^ bit, j) if axis == "lat" else (i, j ^ bit)
            pairs.append((i * n_lon + j, a * n_lon + b))
    return pairs


def swap(x, mesh_shape, bits):
    return lax.ppermute(x, ("lat", "lon"), partner_pairs(mesh_shape, bits))


def my_bit(bits):
    def of(axis, bit):
        return (lax.axis_index(axis) // bit) % 2

    odd = lax.axis_index("lat") % 2
    return jnp.where(odd == 0, of(*bits[0]), of(*bits[1]))


def put_bias(ref, rows, bias):
    heads, count = bias.shape
    high = bias.astype(BF16)
    ref[rows:, :count] = high
    ref[rows:, count : 2 * count] = (bias - high.astype(F32)).astype(BF16)
    ref[rows:, 2 * count :] = jnp.zeros((heads, ref.shape[1] - 2 * count), BF16)


def get_bias(ref, rows, count):
    return ref[rows:, :count].astype(F32) + ref[rows:, count : 2 * count].astype(F32)


def halve_kernel(n, info_ref, keep_ref, got_ref, send_ref, out_ref):
    half = send_ref.shape[0]
    low = keep_ref[:half, :] + got_ref[:half, :].astype(F32)
    high = keep_ref[half:, :] + got_ref[half:, :].astype(F32)
    lower = info_ref[n] == 0
    send_ref[...] = jnp.where(lower, high, low).astype(BF16)
    out_ref[...] = jnp.where(lower, low, high)


def meet_kernel(keep_ref, got_ref, bias_ref, out_ref):
    rows = keep_ref.shape[0]
    out_ref[:rows, :] = (keep_ref[...] + got_ref[...].astype(F32)).astype(BF16)
    put_bias(out_ref, rows, bias_ref[...])


def total_kernel(norm, count, heads, own_ref, got_ref, out_ref):
    rows = own_ref.shape[0] - heads
    total = own_ref[:rows, :].astype(F32) + got_ref[:rows, :].astype(F32)
    out_ref[:rows, :] = (total if norm is None else total * norm).astype(BF16)
    put_bias(out_ref, rows, get_bias(own_ref, rows, count) + get_bias(got_ref, rows, count))


def grow_kernel(n, count, heads, info_ref, own_ref, got_ref, out_ref):
    rows = own_ref.shape[0] - heads
    lower = info_ref[n] == 0
    own = own_ref[:rows, :]
    got = got_ref[:rows, :]
    out_ref[:rows, :] = jnp.where(lower, own, got)
    out_ref[rows : 2 * rows, :] = jnp.where(lower, got, own)
    put_bias(out_ref, 2 * rows, get_bias(own_ref, rows, count) + get_bias(got_ref, rows, count))


def last_kernel(n, norm, count, info_ref, own_ref, got_ref, out_ref, bias_ref):
    rows = out_ref.shape[0] // 2
    lower = info_ref[n] == 0
    own = own_ref[:rows, :]
    got = got_ref[:rows, :]
    out_ref[:rows, :] = jnp.where(lower, own, got)
    out_ref[rows:, :] = jnp.where(lower, got, own)
    bias = (get_bias(own_ref, rows, count) + get_bias(got_ref, rows, count)) * norm
    for a in range(SPAN):
        bias_ref[a] = bias[:, a * SPAN : (a + 1) * SPAN]


def project_kernel(info_ref, s_ref, k_ref, w_ref, out_ref):
    rows = s_ref.shape[1]
    first = pl.ds(pl.multiple_of(info_ref[0] * rows, rows), rows)
    second = pl.ds(pl.multiple_of((1 - info_ref[0]) * rows, rows), rows)
    out = dot(s_ref[...], w_ref[first, :]) + dot(k_ref[...], w_ref[second, :])
    out_ref[...] = out.astype(BF16)


def shards(mesh_shape, queries, keys, values, rel_bias, out_weight, cotangent):
    lat_dev, lon_dev, width = queries.shape
    heads = rel_bias.shape[0]
    head_size = width // heads
    groups = heads // GROUP
    lanes = GROUP * head_size
    model = out_weight.shape[1]
    n_lat, n_lon = mesh_shape["lat"], mesh_shape["lon"]
    cols_pad = lon_dev + SLOTS
    outer_lat = lat_dev + 2 * RAD
    tokens = lat_dev * lon_dev
    norm = (tokens * n_lat * n_lon) ** (-0.5)
    east = [(i, (i + 1) % n_lon) for i in range(n_lon)]
    west = [(i, (i - 1) % n_lon) for i in range(n_lon)]
    pair_a = [(i, i ^ 1) for i in range(n_lat)]
    pair_b = [(i, i + 1) for i in range(1, n_lat - 1, 2)]
    pair_b = pair_b + [(j, i) for i, j in pair_b]
    win = (TILE + 2 * RAD) * cols_pad
    tiles = lat_dev // TILE
    lanes_q = TILE * GROUP * lon_dev
    n_keys = outer_lat * cols_pad
    n_side = lat_dev * RAD
    n_edge = RAD * lon_dev
    n_strip = RAD * cols_pad

    def shape(dims, dtype=BF16):
        return jax.ShapeDtypeStruct(dims, dtype)

    q_flat = queries.reshape(tokens, width)
    k_flat = keys.reshape(tokens, width)
    v_flat = values.reshape(tokens, width)
    cot = cotangent.reshape(tokens, model)

    lat_index = lax.axis_index("lat").astype(jnp.int32)
    core = lat_index % 2
    rounds, ends = rounds_of(mesh_shape)
    facts = [1 - core, lat_index, core] + [my_bit(bits) for bits in rounds]
    info = jnp.stack([x.astype(jnp.int32) for x in facts])
    smem = pl.BlockSpec(memory_space=pltpu.SMEM)
    vmem = pl.BlockSpec(memory_space=pltpu.VMEM)
    hbm = pl.BlockSpec(memory_space=pltpu.HBM)

    to_east, to_west, own_a, own_b = pl.pallas_call(
        functools.partial(pack_kernel, lat_dev, lon_dev),
        in_specs=[smem, hbm, hbm],
        out_shape=[shape((2, n_side, width))] * 2 + [shape((2, n_edge, width))] * 2,
        scratch_shapes=[pltpu.VMEM((2, tokens, width), BF16), pltpu.SemaphoreType.DMA((2,))],
        compiler_params=room(4),
        name="pack",
    )(info, in_hbm(k_flat), in_hbm(v_flat))
    from_west = lax.ppermute(to_east, "lon", east)
    from_east = lax.ppermute(to_west, "lon", west)
    from_b = lax.ppermute(own_b, "lat", pair_b)
    sizes = (lat_dev, lon_dev, cols_pad, head_size, lat_dev * n_lat)
    table, attended_grad = pl.pallas_call(
        functools.partial(prepare_kernel, lon_dev, cols_pad),
        in_specs=[smem, hbm, hbm],
        out_shape=[shape((win, groups * lanes_q), F32), shape((tokens, width))],
        scratch_shapes=[pltpu.VMEM((SPAN, cols_pad, heads * lon_dev), F32)] * 2
        + [pltpu.VMEM((tokens, model), BF16), pltpu.VMEM((width, model), BF16)]
        + [pltpu.SemaphoreType.DMA((2,))],
        compiler_params=room(6),
        name="prepare",
    )(rel_bias.transpose(1, 0, 2), in_hbm(cot), in_hbm(out_weight))
    from_west, from_east, from_b, table = lax.optimization_barrier(
        (from_west, from_east, from_b, table)
    )

    corner_a, corner_b = pl.pallas_call(
        functools.partial(corner_kernel, lat_dev, lon_dev),
        in_specs=[smem] + [vmem] * 3,
        out_shape=[shape((2, n_edge + CORNER, width)), shape((2, CORNER, width))],
        compiler_params=room(4),
        name="corner",
    )(info, from_west, from_east, own_a)
    side_b = lax.ppermute(corner_b, "lat", pair_b)
    from_a = lax.ppermute(corner_a, "lat", pair_a)
    probs = (tiles, win, lanes_q)
    outer = (n_keys, lanes)

    def forward(n, dtype):
        return pl.pallas_call(
            functools.partial(fwd_kernel, sizes, n),
            in_specs=[smem] + [vmem] * 10,
            out_shape=[shape((tokens, lanes)), shape((lanes, model), dtype), shape(probs, F32)]
            + [shape(outer)] * 2,
            scratch_shapes=[pltpu.VMEM((lanes, n_keys), BF16), pltpu.VMEM((lanes, tokens), BF16)],
            compiler_params=room(8),
            name="attend_fwd",
        )(
            info, q_flat, k_flat, v_flat, from_west, from_east,
            from_a, from_b, side_b, table, cot,
        )

    def step_call(kernel, name, outs, *operands):
        scalars = [smem if x.dtype == jnp.int32 else vmem for x in operands]
        return pl.pallas_call(
            kernel, in_specs=scalars, out_shape=outs, compiler_params=room(4), name=name
        )(*operands)

    att_s, weight_s, p_s, k_s, v_s = forward(0, BF16)
    got = swap(weight_s, mesh_shape, rounds[0])
    att_k, keep, p_k, k_k, v_k = forward(2, F32)

    def halve(keep, got, number):
        half = (keep.shape[0] // 2, model)
        outs = [shape(half), shape(half, F32)]
        kernel = functools.partial(halve_kernel, 3 + number)
        return step_call(kernel, "halve", outs, info, keep, got)

    send, keep = halve(keep, got, 1)
    def backward(n, info, p, k, v, *before):
        size = width if before else lanes
        return pl.pallas_call(
            functools.partial(bwd_kernel, sizes, n),
            in_specs=[smem] + [vmem] * (5 + len(before)),
            out_shape=[shape((tokens, size)), shape((2, n_strip, size))]
            + [shape((2, n_strip, lanes))]
            + [shape((2, tokens, lanes), F32)] * 2
            + [shape((SPAN * cols_pad, 2 * GROUP * lon_dev), F32)],
            scratch_shapes=[pltpu.VMEM((lanes, n_keys), BF16)]
            + [pltpu.VMEM((n_keys, lanes), F32)] * 2
            + [pltpu.VMEM((win, lanes_q), F32)],
            compiler_params=room(10),
            name="attend_bwd",
        )(info, q_flat, attended_grad, p, k, v, *before)

    info_b, send = lax.optimization_barrier((info, send))
    got = swap(send, mesh_shape, rounds[1])
    *before, strip_s, mid_s, side_s, fold_s = backward(0, info_b, p_s, k_s, v_s)
    got, fold_s = lax.optimization_barrier((got, fold_s))
    get_s = lax.ppermute(strip_s, "lat", pair_b)
    for number in range(2, len(rounds)):
        send, keep = halve(keep, got, number)
        if number == 2:
            info_b, send = lax.optimization_barrier((info, send))
        got = swap(send, mesh_shape, rounds[number])
    after = backward(2, info_b, p_k, k_k, v_k, *before)
    query_grad, strip_a, strip_b, mid_k, side_k, fold_k = after
    got, fold_k, get_s = lax.optimization_barrier((got, fold_k, get_s))

    count = 256
    bias_local = pl.pallas_call(
        functools.partial(bias_kernel, lon_dev, cols_pad),
        in_specs=[smem, vmem, vmem],
        out_shape=shape((heads, count), F32),
        scratch_shapes=[pltpu.VMEM((count, heads * lon_dev), F32)],
        compiler_params=room(4),
        name="bias_fold",
    )(info, fold_s, fold_k)
    block_out = pl.pallas_call(
        project_kernel,
        in_specs=[smem] + [vmem] * 3,
        out_shape=shape((tokens, model)),
        compiler_params=room(6),
        name="project",
    )(info, att_s, att_k, out_weight)
    note = shape((keep.shape[0] + heads, model))
    message = step_call(meet_kernel, "meet", note, keep, got, bias_local)
    message, strip_a, strip_b = lax.optimization_barrier((message, strip_a, strip_b))
    get_b = lax.ppermute(strip_b, "lat", pair_b)
    get_a = lax.ppermute(strip_a, "lat", pair_a)
    got = swap(message, mesh_shape, ends[0])
    kernel = functools.partial(total_kernel, None, count, heads)
    message = step_call(kernel, "total", note, message, got)
    message, block_out = lax.optimization_barrier((message, block_out))
    got = swap(message, mesh_shape, ends[1])
    give_west, give_east = pl.pallas_call(
        functools.partial(side_kernel, lat_dev, lon_dev, cols_pad),
        in_specs=[smem] + [vmem] * 5,
        out_shape=[shape((2, n_side, width))] * 2,
        scratch_shapes=[pltpu.VMEM((tokens, width), F32)],
        compiler_params=room(6),
        name="side",
    )(info, side_s, side_k, get_a, get_b, get_s)
    get_east = lax.ppermute(give_west, "lon", west)
    get_west = lax.ppermute(give_east, "lon", east)
    kernel = functools.partial(total_kernel, norm, count, heads)
    message = step_call(kernel, "total", note, message, got)
    message, give_west, give_east = lax.optimization_barrier((message, give_west, give_east))

    for number in range(len(rounds) - 1, 0, -1):
        if number == 1:
            message, get_east, get_west = lax.optimization_barrier((message, get_east, get_west))
        got = swap(message, mesh_shape, rounds[number])
        if number == 1:
            key_grad, value_grad = pl.pallas_call(
                functools.partial(join_kernel, lat_dev, lon_dev, cols_pad),
                in_specs=[smem] + [vmem] * 7,
                out_shape=[shape((tokens, width))] * 2,
                scratch_shapes=[pltpu.VMEM((tokens, width), F32)],
                compiler_params=room(6),
                name="join",
            )(info, mid_s, mid_k, get_a, get_b, get_s, get_west, get_east)
            got, key_grad = lax.optimization_barrier((got, key_grad))
        note = shape((2 * message.shape[0] - heads, model))
        kernel = functools.partial(grow_kernel, 3 + number, count, heads)
        message = step_call(kernel, "grow", note, info, message, got)
    got = swap(message, mesh_shape, rounds[0])
    weight_grad, bias_grad = step_call(
        functools.partial(last_kernel, 3, norm, count),
        "last",
        [shape((width, model)), shape((SPAN, heads, SPAN), F32)],
        info, message, got,
    )
    return (
        block_out.reshape(lat_dev, lon_dev, model),
        query_grad.reshape(queries.shape),
        key_grad.reshape(keys.shape),
        value_grad.reshape(values.shape),
        weight_grad,
        bias_grad.transpose(1, 0, 2),
    )


def solution(mesh):
    spec = P("lat", "lon", None)
    return jax.shard_map(
        functools.partial(shards, dict(mesh.shape)),
        mesh=mesh,
        in_specs=(spec, spec, spec, P(), P(), spec),
        out_specs=(spec, spec, spec, spec, P(), P()),
        check_vma=False,
    )
```

```python
import functools

import jax
import jax.numpy as jnp
from jax import lax
from jax.experimental import pallas as pl
from jax.experimental.pallas import tpu as pltpu
from jax.sharding import PartitionSpec as P

RAD = 6
SPAN = 2 * RAD + 1
TILE = 4
GROUP = 4
NEG = -1e30
NT = (((1,), (1,)), ((), ()))
F32 = jnp.float32
BF16 = jnp.bfloat16
SLOTS = 16
CORNER = 80
MIB = 1 << 20


def dot(a, b):
    return jnp.dot(a, b, preferred_element_type=F32)


def dot_nt(a, b):
    return lax.dot_general(a, b, NT, preferred_element_type=F32)


def in_hbm(x):
    return pltpu.with_memory_space_constraint(x, pltpu.HBM)


def room(mib):
    return pltpu.CompilerParams(vmem_limit_bytes=mib * MIB)


def iota2(shape, axis):
    return lax.broadcasted_iota(jnp.int32, shape, axis)


def hot(mask):
    return mask.astype(F32).astype(BF16)


def over(x, n):
    if n & (n - 1) == 0:
        return x >> (n.bit_length() - 1), x & (n - 1)
    return x // n, x % n


def down_iota(n):
    return iota2((n, 1), 0)


def along_iota(n):
    return iota2((1, n), 1)


def spread_heads(tile, cols, head_size):
    lane = over(iota2((cols, tile.shape[1]), 1), head_size)[0]
    zero = jnp.zeros((cols, tile.shape[1]), tile.dtype)
    parts = []
    for i in range(TILE):
        rows = tile[i * cols : (i + 1) * cols]
        for h in range(GROUP):
            parts.append(jnp.where(lane == h, rows, zero))
    return jnp.concatenate(parts, 0)


def head_mask(cols, head_size):
    shape = (GROUP * head_size, TILE * GROUP * cols)
    column = over(over(iota2(shape, 1), cols)[0], GROUP)[1]
    return over(iota2(shape, 0), head_size)[0] == column


def picker(cols):
    row_i, row_j = over(down_iota(TILE * cols), cols)
    high, col_j = over(along_iota(TILE * GROUP * cols), cols)
    return hot((row_i == over(high, GROUP)[0]) & (row_j == col_j))


def keep_rows(st, first_row, rows_all, cols_pad):
    parts = []
    for k in range(TILE + 2 * RAD):
        row = first_row + k
        inside = (row >= 0) & (row < rows_all)
        parts.append(jnp.where(inside, st[k * cols_pad : (k + 1) * cols_pad], NEG))
    return jnp.concatenate(parts, 0)


def take_cols(rows, cols, first):
    r, c = over(down_iota(rows * RAD), RAD)
    return hot(along_iota(rows * cols) == r * cols + first + c)


def put_cols(rows, cols, first):
    r, c = over(along_iota(rows * RAD), RAD)
    return hot(down_iota(rows * cols) == r * cols + first + c)


def put_corner(cols):
    n = along_iota(CORNER)
    half = RAD * RAD
    r, c = over(jnp.where(n < half, n, n - half), RAD)
    target = r * cols + c + jnp.where(n < half, 0, RAD)
    return hot((down_iota(RAD * cols) == target) & (n < 2 * half))


def pack_kernel(
    rows, cols, info_ref, k_hbm, v_hbm, east_ref, west_ref, a_ref, b_ref, x_ref, sem_ref
):
    copies = [
        pltpu.make_async_copy(ref, x_ref.at[i], sem_ref.at[i])
        for i, ref in enumerate((k_hbm, v_hbm))
    ]
    for copy in copies:
        copy.start()
    pick_east = take_cols(rows, cols, cols - RAD)
    pick_west = take_cols(rows, cols, 0)
    edge = RAD * cols
    odd = info_ref[2] == 1
    for i, copy in enumerate(copies):
        copy.wait()
        x = x_ref[i]
        east_ref[i] = dot(pick_east, x).astype(BF16)
        west_ref[i] = dot(pick_west, x).astype(BF16)
        down = x[(rows - RAD) * cols :]
        up = x[:edge]
        a_ref[i] = jnp.where(odd, up, down)
        b_ref[i] = jnp.where(odd, down, up)


def corner_kernel(rows, cols, info_ref, w_ref, e_ref, own_ref, a_ref, b_ref):
    half = RAD * RAD
    edge = RAD * cols
    n = down_iota(CORNER)
    src = along_iota(rows * RAD)
    odd = info_ref[2] == 1
    last = (rows - RAD) * RAD
    a_ref[:, :edge, :] = own_ref[...]
    for ref, lo, first in (
        (b_ref, 0, jnp.where(odd, last, 0)),
        (a_ref, edge, jnp.where(odd, 0, last)),
    ):
        pick_w = hot((src == first + n) & (n < half))
        pick_e = hot((src == first + n - half) & (n >= half) & (n < 2 * half))
        for i in range(2):
            side = dot(pick_w, w_ref[i]) + dot(pick_e, e_ref[i])
            ref[i, lo:, :] = side.astype(BF16)


def prepare_kernel(
    cols, cols_pad, rel_ref, cot_hbm, w_hbm, out_ref, grad_ref, c_ref, r_ref, cot_ref, w_ref,
    sem_ref,
):
    copies = [
        pltpu.make_async_copy(cot_hbm, cot_ref, sem_ref.at[0]),
        pltpu.make_async_copy(w_hbm, w_ref, sem_ref.at[1]),
    ]
    for copy in copies:
        copy.start()
    heads = rel_ref.shape[1]
    lanes = heads * cols
    half = lanes // 2
    shape = (cols_pad, lanes)
    offset = slot_offset(shape, cols)
    inside = (offset >= 0) & (offset < SPAN)
    head = over(iota2((1, lanes), 1), cols)[0]
    for a in range(SPAN):
        tile = jnp.full(shape, NEG, F32)
        for b in range(SPAN):
            row = jnp.full((1, lanes), rel_ref[a, 0, b], F32)
            for h in range(1, heads):
                row = jnp.where(head == h, rel_ref[a, h, b], row)
            tile = jnp.where(offset == b, row, tile)
        tile = jnp.where(inside, tile, NEG)
        c_ref[a] = tile
        r_ref[a] = pltpu.roll(tile, half, 1)
    low = iota2(shape, 1) < half
    blank = jnp.full(shape, NEG, F32)
    for g in range(2):
        first, second = (c_ref, r_ref) if g == 0 else (r_ref, c_ref)
        for pair in range(TILE // 2):
            i = 2 * pair
            lo = (g * TILE // 2 + pair) * lanes
            for k in range(TILE + 2 * RAD):
                a = k - i
                one = first[a] if 0 <= a < SPAN else blank
                two = second[a - 1] if 0 <= a - 1 < SPAN else blank
                out_ref[k * cols_pad : (k + 1) * cols_pad, lo : lo + lanes] = jnp.where(
                    low, one, two
                )
    for copy in copies:
        copy.wait()
    grad_ref[...] = dot_nt(cot_ref[...], w_ref[...]).astype(BF16)


def slot_offset(shape, cols):
    slot = iota2(shape, 0)
    pos = jnp.where(slot < cols, slot + RAD, jnp.where(slot < cols + RAD, slot - cols, slot))
    pos = jnp.where(slot < cols + 2 * RAD, pos, -1000)
    return pos - over(iota2(shape, 1), cols)[1]


def assemble(out_ref, i, rows, cols, cols_pad, own, refs, group, odd):
    w_ref, e_ref, a_ref, b_ref, c_ref = refs
    edge = RAD * cols
    side = dot(put_cols(rows, SLOTS, 0), w_ref[i, :, group])
    side = (side + dot(put_cols(rows, SLOTS, RAD), e_ref[i, :, group])).astype(BF16)
    for r in range(rows):
        lo = (RAD + r) * cols_pad
        out_ref[lo : lo + cols, :] = own[r * cols : (r + 1) * cols, group]
        out_ref[lo + cols : lo + cols + SLOTS, :] = side[r * SLOTS : (r + 1) * SLOTS]
    put = put_corner(SLOTS)
    below = (RAD + rows) * cols_pad
    corner_a = a_ref[i, edge:, group]
    for first, o_ref, corner in (
        (jnp.where(odd, 0, below), a_ref, corner_a),
        (jnp.where(odd, below, 0), b_ref, c_ref[i, :, group]),
    ):
        side = dot(put, corner).astype(BF16)
        for r in range(RAD):
            lo = pl.multiple_of(first + r * cols_pad, cols_pad)
            out_ref[pl.ds(lo, cols), :] = o_ref[i, r * cols : (r + 1) * cols, group]
            lo = pl.multiple_of(first + r * cols_pad + cols, cols)
            out_ref[pl.ds(lo, SLOTS), :] = side[r * SLOTS : (r + 1) * SLOTS]


def group_lanes(group, lanes):
    return pl.ds(pl.multiple_of(group * lanes, lanes), lanes)


def fwd_kernel(
    sizes, n, info_ref, q_ref, k_ref, v_ref, w_ref, e_ref, a_ref, b_ref, c_ref,
    bias_ref, cot_ref, out_ref, weight_ref, p_ref, ko_ref, vo_ref, vt_ref, at_ref,
):
    lat_dev, cols, cols_pad, head_size, rows_all = sizes
    scale = head_size ** (-0.5)
    group = group_lanes(info_ref[n], GROUP * head_size)
    refs = (w_ref, e_ref, a_ref, b_ref, c_ref)
    odd = info_ref[2] == 1
    assemble(ko_ref, 0, lat_dev, cols, cols_pad, k_ref, refs, group, odd)
    assemble(vo_ref, 1, lat_dev, cols, cols_pad, v_ref, refs, group, odd)
    vt_ref[...] = vo_ref[...].T
    mask = head_mask(cols, head_size)
    pick = picker(cols)
    win = (TILE + 2 * RAD) * cols_pad
    for t in range(lat_dev // TILE):
        lo = t * TILE * cols_pad
        qs = pl.ds(t * TILE * cols, TILE * cols)
        q_bd = spread_heads(q_ref[qs, group] * jnp.asarray(scale, BF16), cols, head_size)
        first = info_ref[1] * lat_dev + t * TILE - RAD
        st = dot_nt(ko_ref[pl.ds(lo, win), :], q_bd) + bias_ref[:, group]
        st = keep_rows(st, first, rows_all, cols_pad)
        m = jnp.max(st, 0, keepdims=True)
        e = jnp.exp(st - m)
        p = e * (1.0 / jnp.sum(e, 0, keepdims=True))
        p_ref[t] = p
        ot = dot(vt_ref[:, pl.ds(lo, win)], p.astype(BF16))
        ot = jnp.where(mask, ot, 0.0).astype(BF16)
        out_ref[qs, :] = dot_nt(pick, ot).astype(BF16)
    at_ref[...] = out_ref[...].T
    weight_ref[...] = dot(at_ref[...], cot_ref[...]).astype(weight_ref.dtype)


def bwd_kernel(sizes, n, info_ref, q_ref, g_ref, p_ref, k_ref, v_ref, *refs):
    dq_ref, sa_ref, sb_ref, mid_ref, side_ref, x_ref, kt_ref, dk_ref, dv_ref, db_ref = refs[-10:]
    before = refs[:-10]
    lat_dev, cols, cols_pad, head_size, rows_all = sizes
    scale = head_size ** (-0.5)
    mask = head_mask(cols, head_size)
    pick = picker(cols)
    win = (TILE + 2 * RAD) * cols_pad
    half = GROUP * cols
    low = iota2((cols_pad, 2 * half), 1) < half
    which = info_ref[n]
    group = group_lanes(which, GROUP * head_size)
    mine = group if before else slice(None)
    if before:
        other = group_lanes(1 - which, GROUP * head_size)
        dq_ref[:, other] = before[0][...]
        sa_ref[:, :, other] = before[1][...]
    kt_ref[...] = k_ref[...].T
    dk_ref[...] = jnp.zeros_like(dk_ref)
    dv_ref[...] = jnp.zeros_like(dv_ref)
    for t in range(lat_dev // TILE):
        lo = t * TILE * cols_pad
        qs = pl.ds(t * TILE * cols, TILE * cols)
        ws = pl.ds(lo, win)
        q_bd = spread_heads(q_ref[qs, group] * jnp.asarray(scale, BF16), cols, head_size)
        g_bd = spread_heads(g_ref[qs, group], cols, head_size)
        p = p_ref[t]
        slope = dot_nt(v_ref[ws, :], g_bd)
        inner = jnp.sum(p * slope, 0, keepdims=True)
        sg = p * (slope - inner)
        if t == 0:
            db_ref[...] = sg
        else:
            db_ref[...] += sg
        sgb = sg.astype(BF16)
        dqt = jnp.where(mask, dot(kt_ref[:, ws], sgb) * scale, 0.0).astype(BF16)
        dq_ref[qs, mine] = dot_nt(pick, dqt).astype(BF16)
        dk_ref[ws, :] += dot(sgb, q_bd)
        dv_ref[ws, :] += dot(p.astype(BF16), g_bd)
    edge = RAD * cols_pad
    odd = info_ref[2] == 1
    low_rows = edge + lat_dev * cols_pad
    first_a = pl.multiple_of(jnp.where(odd, 0, low_rows), cols_pad)
    first_b = pl.multiple_of(jnp.where(odd, low_rows, 0), cols_pad)
    for i, ref in enumerate((dk_ref, dv_ref)):
        sa_ref[i, :, mine] = ref[pl.ds(first_a, edge), :].astype(BF16)
        sb_ref[i] = ref[pl.ds(first_b, edge), :].astype(BF16)
        for r in range(lat_dev):
            lo = (RAD + r) * cols_pad
            mid_ref[i, r * cols : (r + 1) * cols, :] = ref[lo : lo + cols, :]
            side_ref[i, r * SLOTS : (r + 1) * SLOTS, :] = ref[lo + cols : lo + cols_pad, :]
    for a in range(SPAN):
        total = jnp.zeros((cols_pad, 2 * half), F32)
        for pair in range(TILE // 2):
            i = 2 * pair
            lanes = slice(pair * 2 * half, (pair + 1) * 2 * half)
            one = db_ref[(a + i) * cols_pad : (a + i + 1) * cols_pad, lanes]
            two = db_ref[(a + i + 1) * cols_pad : (a + i + 2) * cols_pad, lanes]
            total = total + jnp.where(low, one, two)
        x_ref[a * cols_pad : (a + 1) * cols_pad, :] = total


def bias_kernel(cols, cols_pad, info_ref, xs_ref, xk_ref, out_ref, z_ref):
    lanes = xs_ref.shape[1]
    half = lanes // 2
    shape = (cols_pad, lanes)
    low = (over(iota2(shape, 1), half)[0] == info_ref[0])
    offset = slot_offset(shape, cols)
    z_ref[...] = jnp.zeros_like(z_ref)
    for a in range(SPAN):
        rows = slice(a * cols_pad, (a + 1) * cols_pad)
        one = xs_ref[rows, :]
        two = xk_ref[rows, :]
        both = jnp.where(low, one + pltpu.roll(one, half, 1), two + pltpu.roll(two, half, 1))
        for b in range(SPAN):
            n = a * SPAN + b
            z_ref[n : n + 1, :] = jnp.sum(jnp.where(offset == b, both, 0.0), 0, keepdims=True)
    heads = out_ref.shape[0]
    pick = (over(iota2((heads, lanes), 1), cols)[0] == iota2((heads, lanes), 0)).astype(F32)
    out_ref[...] = lax.dot_general(
        pick, z_ref[...], NT, precision=lax.Precision.HIGHEST, preferred_element_type=F32
    )


def lat_terms(ref, i, rows, cols, cols_pad, first):
    parts = []
    for r in range(RAD):
        lo = r * cols_pad + first
        parts.append(ref[i, lo : lo + cols, :])
    return jnp.concatenate(parts, 0).astype(F32)


def strips(info_ref, rows, cols):
    odd = info_ref[2] == 1
    last = (rows - RAD) * cols
    return [pl.multiple_of(jnp.where(odd, x, last - x), cols) for x in (0, last)]


def both_lanes(info_ref, lanes):
    return group_lanes(info_ref[0], lanes), group_lanes(1 - info_ref[0], lanes)


def both_groups(info_ref, dst_ref, i, *refs):
    for ref, group in zip(refs, both_lanes(info_ref, refs[0].shape[2])):
        dst_ref[:, group] = ref[i]


def side_kernel(
    rows, cols, cols_pad, info_ref, ss_ref, sk_ref, a_ref, bk_ref, bs_ref, west_ref, east_ref,
    s_ref,
):
    edge = RAD * SLOTS
    pick_west = take_cols(rows, SLOTS, 0)
    pick_east = take_cols(rows, SLOTS, RAD)
    for i in range(2):
        both_groups(info_ref, s_ref, i, ss_ref, sk_ref)
        first_a, first_b = strips(info_ref, rows, SLOTS)
        s_ref[pl.ds(first_a, edge), :] += lat_terms(a_ref, i, rows, SLOTS, cols_pad, cols)
        for ref, group in zip((bk_ref, bs_ref), both_lanes(info_ref, bs_ref.shape[2])):
            s_ref[pl.ds(first_b, edge), group] += lat_terms(ref, i, rows, SLOTS, cols_pad, cols)
        x = s_ref[...].astype(BF16)
        west_ref[i] = dot(pick_west, x).astype(BF16)
        east_ref[i] = dot(pick_east, x).astype(BF16)


def join_kernel(
    rows, cols, cols_pad, info_ref, ms_ref, mk_ref, a_ref, bk_ref, bs_ref, w_ref, e_ref,
    k_ref, v_ref, s_ref,
):
    edge = RAD * cols
    put_west = put_cols(rows, cols, 0)
    put_east = put_cols(rows, cols, cols - RAD)
    for i, out_ref in enumerate((k_ref, v_ref)):
        both_groups(info_ref, s_ref, i, ms_ref, mk_ref)
        s_ref[...] += dot(put_west, w_ref[i]) + dot(put_east, e_ref[i])
        first_a, first_b = strips(info_ref, rows, cols)
        s_ref[pl.ds(first_a, edge), :] += lat_terms(a_ref, i, rows, cols, cols_pad, 0)
        for ref, group in zip((bk_ref, bs_ref), both_lanes(info_ref, bs_ref.shape[2])):
            s_ref[pl.ds(first_b, edge), group] += lat_terms(ref, i, rows, cols, cols_pad, 0)
        out_ref[...] = s_ref[...].astype(BF16)


def bits_of(mesh_shape):
    order = []
    for axis in ("lat", "lon"):
        bit = 1
        while bit < mesh_shape[axis]:
            order.append((axis, bit))
            bit *= 2
    return order


def rounds_of(mesh_shape):
    first, *rest = bits_of(mesh_shape)
    rest[-3], rest[-2] = rest[-2], rest[-3]
    middle, ends = rest[:-2], rest[-2:]
    turned = middle[1:] + middle[:1]
    return [(first, first)] + list(zip(middle, turned)), list(zip(ends, ends[::-1]))


def partner_pairs(mesh_shape, bits):
    n_lat, n_lon = mesh_shape["lat"], mesh_shape["lon"]
    pairs = []
    for i in range(n_lat):
        axis, bit = bits[i % 2]
        for j in range(n_lon):
            a, b = (i ^ bit, j) if axis == "lat" else (i, j ^ bit)
            pairs.append((i * n_lon + j, a * n_lon + b))
    return pairs


def swap(x, mesh_shape, bits):
    return lax.ppermute(x, ("lat", "lon"), partner_pairs(mesh_shape, bits))


def my_bit(bits):
    def of(axis, bit):
        return (lax.axis_index(axis) // bit) % 2

    odd = lax.axis_index("lat") % 2
    return jnp.where(odd == 0, of(*bits[0]), of(*bits[1]))


def put_bias(ref, rows, bias):
    heads, count = bias.shape
    high = bias.astype(BF16)
    ref[rows:, :count] = high
    ref[rows:, count : 2 * count] = (bias - high.astype(F32)).astype(BF16)
    ref[rows:, 2 * count :] = jnp.zeros((heads, ref.shape[1] - 2 * count), BF16)


def get_bias(ref, rows, count):
    return ref[rows:, :count].astype(F32) + ref[rows:, count : 2 * count].astype(F32)


def halve_kernel(n, info_ref, keep_ref, got_ref, send_ref, out_ref):
    half = send_ref.shape[0]
    low = keep_ref[:half, :] + got_ref[:half, :].astype(F32)
    high = keep_ref[half:, :] + got_ref[half:, :].astype(F32)
    lower = info_ref[n] == 0
    send_ref[...] = jnp.where(lower, high, low).astype(BF16)
    out_ref[...] = jnp.where(lower, low, high)


def meet_kernel(keep_ref, got_ref, bias_ref, out_ref):
    rows = keep_ref.shape[0]
    out_ref[:rows, :] = (keep_ref[...] + got_ref[...].astype(F32)).astype(BF16)
    put_bias(out_ref, rows, bias_ref[...])


def total_kernel(norm, count, heads, own_ref, got_ref, out_ref):
    rows = own_ref.shape[0] - heads
    total = own_ref[:rows, :].astype(F32) + got_ref[:rows, :].astype(F32)
    out_ref[:rows, :] = (total if norm is None else total * norm).astype(BF16)
    put_bias(out_ref, rows, get_bias(own_ref, rows, count) + get_bias(got_ref, rows, count))


def grow_kernel(n, count, heads, info_ref, own_ref, got_ref, out_ref):
    rows = own_ref.shape[0] - heads
    lower = info_ref[n] == 0
    own = own_ref[:rows, :]
    got = got_ref[:rows, :]
    out_ref[:rows, :] = jnp.where(lower, own, got)
    out_ref[rows : 2 * rows, :] = jnp.where(lower, got, own)
    put_bias(out_ref, 2 * rows, get_bias(own_ref, rows, count) + get_bias(got_ref, rows, count))


def last_kernel(n, norm, count, info_ref, own_ref, got_ref, out_ref, bias_ref):
    rows = out_ref.shape[0] // 2
    lower = info_ref[n] == 0
    own = own_ref[:rows, :]
    got = got_ref[:rows, :]
    out_ref[:rows, :] = jnp.where(lower, own, got)
    out_ref[rows:, :] = jnp.where(lower, got, own)
    bias = (get_bias(own_ref, rows, count) + get_bias(got_ref, rows, count)) * norm
    for a in range(SPAN):
        bias_ref[a] = bias[:, a * SPAN : (a + 1) * SPAN]


def project_kernel(info_ref, s_ref, k_ref, w_ref, out_ref):
    rows = s_ref.shape[1]
    first = pl.ds(pl.multiple_of(info_ref[0] * rows, rows), rows)
    second = pl.ds(pl.multiple_of((1 - info_ref[0]) * rows, rows), rows)
    out = dot(s_ref[...], w_ref[first, :]) + dot(k_ref[...], w_ref[second, :])
    out_ref[...] = out.astype(BF16)


def shards(mesh_shape, queries, keys, values, rel_bias, out_weight, cotangent):
    lat_dev, lon_dev, width = queries.shape
    heads = rel_bias.shape[0]
    head_size = width // heads
    groups = heads // GROUP
    lanes = GROUP * head_size
    model = out_weight.shape[1]
    n_lat, n_lon = mesh_shape["lat"], mesh_shape["lon"]
    cols_pad = lon_dev + SLOTS
    outer_lat = lat_dev + 2 * RAD
    tokens = lat_dev * lon_dev
    norm = (tokens * n_lat * n_lon) ** (-0.5)
    east = [(i, (i + 1) % n_lon) for i in range(n_lon)]
    west = [(i, (i - 1) % n_lon) for i in range(n_lon)]
    pair_a = [(i, i ^ 1) for i in range(n_lat)]
    pair_b = [(i, i + 1) for i in range(1, n_lat - 1, 2)]
    pair_b = pair_b + [(j, i) for i, j in pair_b]
    win = (TILE + 2 * RAD) * cols_pad
    tiles = lat_dev // TILE
    lanes_q = TILE * GROUP * lon_dev
    n_keys = outer_lat * cols_pad
    n_side = lat_dev * RAD
    n_edge = RAD * lon_dev
    n_strip = RAD * cols_pad

    def shape(dims, dtype=BF16):
        return jax.ShapeDtypeStruct(dims, dtype)

    q_flat = queries.reshape(tokens, width)
    k_flat = keys.reshape(tokens, width)
    v_flat = values.reshape(tokens, width)
    cot = cotangent.reshape(tokens, model)

    lat_index = lax.axis_index("lat").astype(jnp.int32)
    core = lat_index % 2
    rounds, ends = rounds_of(mesh_shape)
    facts = [1 - core, lat_index, core] + [my_bit(bits) for bits in rounds]
    info = jnp.stack([x.astype(jnp.int32) for x in facts])
    smem = pl.BlockSpec(memory_space=pltpu.SMEM)
    vmem = pl.BlockSpec(memory_space=pltpu.VMEM)
    hbm = pl.BlockSpec(memory_space=pltpu.HBM)

    to_east, to_west, own_a, own_b = pl.pallas_call(
        functools.partial(pack_kernel, lat_dev, lon_dev),
        in_specs=[smem, hbm, hbm],
        out_shape=[shape((2, n_side, width))] * 2 + [shape((2, n_edge, width))] * 2,
        scratch_shapes=[pltpu.VMEM((2, tokens, width), BF16), pltpu.SemaphoreType.DMA((2,))],
        compiler_params=room(4),
        name="pack",
    )(info, in_hbm(k_flat), in_hbm(v_flat))
    from_west = lax.ppermute(to_east, "lon", east)
    from_east = lax.ppermute(to_west, "lon", west)
    from_b = lax.ppermute(own_b, "lat", pair_b)
    sizes = (lat_dev, lon_dev, cols_pad, head_size, lat_dev * n_lat)
    table, attended_grad = pl.pallas_call(
        functools.partial(prepare_kernel, lon_dev, cols_pad),
        in_specs=[smem, hbm, hbm],
        out_shape=[shape((win, groups * lanes_q), F32), shape((tokens, width))],
        scratch_shapes=[pltpu.VMEM((SPAN, cols_pad, heads * lon_dev), F32)] * 2
        + [pltpu.VMEM((tokens, model), BF16), pltpu.VMEM((width, model), BF16)]
        + [pltpu.SemaphoreType.DMA((2,))],
        compiler_params=room(6),
        name="prepare",
    )(rel_bias.transpose(1, 0, 2), in_hbm(cot), in_hbm(out_weight))
    from_west, from_east, from_b, table = lax.optimization_barrier(
        (from_west, from_east, from_b, table)
    )

    corner_a, corner_b = pl.pallas_call(
        functools.partial(corner_kernel, lat_dev, lon_dev),
        in_specs=[smem] + [vmem] * 3,
        out_shape=[shape((2, n_edge + CORNER, width)), shape((2, CORNER, width))],
        compiler_params=room(4),
        name="corner",
    )(info, from_west, from_east, own_a)
    side_b = lax.ppermute(corner_b, "lat", pair_b)
    from_a = lax.ppermute(corner_a, "lat", pair_a)
    probs = (tiles, win, lanes_q)
    outer = (n_keys, lanes)

    def forward(n, dtype):
        return pl.pallas_call(
            functools.partial(fwd_kernel, sizes, n),
            in_specs=[smem] + [vmem] * 10,
            out_shape=[shape((tokens, lanes)), shape((lanes, model), dtype), shape(probs, F32)]
            + [shape(outer)] * 2,
            scratch_shapes=[pltpu.VMEM((lanes, n_keys), BF16), pltpu.VMEM((lanes, tokens), BF16)],
            compiler_params=room(8),
            name="attend_fwd",
        )(
            info, q_flat, k_flat, v_flat, from_west, from_east,
            from_a, from_b, side_b, table, cot,
        )

    def step_call(kernel, name, outs, *operands):
        scalars = [smem if x.dtype == jnp.int32 else vmem for x in operands]
        return pl.pallas_call(
            kernel, in_specs=scalars, out_shape=outs, compiler_params=room(4), name=name
        )(*operands)

    att_s, weight_s, p_s, k_s, v_s = forward(0, BF16)
    got = swap(weight_s, mesh_shape, rounds[0])
    att_k, keep, p_k, k_k, v_k = forward(2, F32)

    def halve(keep, got, number):
        half = (keep.shape[0] // 2, model)
        outs = [shape(half), shape(half, F32)]
        kernel = functools.partial(halve_kernel, 3 + number)
        return step_call(kernel, "halve", outs, info, keep, got)

    send, keep = halve(keep, got, 1)
    def backward(n, info, p, k, v, *before):
        size = width if before else lanes
        return pl.pallas_call(
            functools.partial(bwd_kernel, sizes, n),
            in_specs=[smem] + [vmem] * (5 + len(before)),
            out_shape=[shape((tokens, size)), shape((2, n_strip, size))]
            + [shape((2, n_strip, lanes))]
            + [shape((2, tokens, lanes), F32)] * 2
            + [shape((SPAN * cols_pad, 2 * GROUP * lon_dev), F32)],
            scratch_shapes=[pltpu.VMEM((lanes, n_keys), BF16)]
            + [pltpu.VMEM((n_keys, lanes), F32)] * 2
            + [pltpu.VMEM((win, lanes_q), F32)],
            compiler_params=room(10),
            name="attend_bwd",
        )(info, q_flat, attended_grad, p, k, v, *before)

    info_b, send = lax.optimization_barrier((info, send))
    got = swap(send, mesh_shape, rounds[1])
    *before, strip_s, mid_s, side_s, fold_s = backward(0, info_b, p_s, k_s, v_s)
    got, fold_s = lax.optimization_barrier((got, fold_s))
    get_s = lax.ppermute(strip_s, "lat", pair_b)
    for number in range(2, len(rounds)):
        send, keep = halve(keep, got, number)
        if number == 2:
            info_b, send = lax.optimization_barrier((info, send))
        got = swap(send, mesh_shape, rounds[number])
    after = backward(2, info_b, p_k, k_k, v_k, *before)
    query_grad, strip_a, strip_b, mid_k, side_k, fold_k = after
    got, fold_k, strip_a, strip_b, get_s = lax.optimization_barrier(
        (got, fold_k, strip_a, strip_b, get_s)
    )
    get_b = lax.ppermute(strip_b, "lat", pair_b)
    get_a = lax.ppermute(strip_a, "lat", pair_a)

    count = 256
    bias_local = pl.pallas_call(
        functools.partial(bias_kernel, lon_dev, cols_pad),
        in_specs=[smem, vmem, vmem],
        out_shape=shape((heads, count), F32),
        scratch_shapes=[pltpu.VMEM((count, heads * lon_dev), F32)],
        compiler_params=room(4),
        name="bias_fold",
    )(info, fold_s, fold_k)
    block_out = pl.pallas_call(
        project_kernel,
        in_specs=[smem] + [vmem] * 3,
        out_shape=shape((tokens, model)),
        compiler_params=room(6),
        name="project",
    )(info, att_s, att_k, out_weight)
    note = shape((keep.shape[0] + heads, model))
    message = step_call(meet_kernel, "meet", note, keep, got, bias_local)
    got = swap(message, mesh_shape, ends[0])
    kernel = functools.partial(total_kernel, None, count, heads)
    message = step_call(kernel, "total", note, message, got)
    message, block_out = lax.optimization_barrier((message, block_out))
    got = swap(message, mesh_shape, ends[1])
    give_west, give_east = pl.pallas_call(
        functools.partial(side_kernel, lat_dev, lon_dev, cols_pad),
        in_specs=[smem] + [vmem] * 5,
        out_shape=[shape((2, n_side, width))] * 2,
        scratch_shapes=[pltpu.VMEM((tokens, width), F32)],
        compiler_params=room(6),
        name="side",
    )(info, side_s, side_k, get_a, get_b, get_s)
    get_east = lax.ppermute(give_west, "lon", west)
    get_west = lax.ppermute(give_east, "lon", east)
    kernel = functools.partial(total_kernel, norm, count, heads)
    message = step_call(kernel, "total", note, message, got)
    message, give_west, give_east = lax.optimization_barrier((message, give_west, give_east))

    for number in range(len(rounds) - 1, 0, -1):
        if number == 1:
            message, get_east, get_west = lax.optimization_barrier((message, get_east, get_west))
        got = swap(message, mesh_shape, rounds[number])
        if number == 1:
            key_grad, value_grad = pl.pallas_call(
                functools.partial(join_kernel, lat_dev, lon_dev, cols_pad),
                in_specs=[smem] + [vmem] * 7,
                out_shape=[shape((tokens, width))] * 2,
                scratch_shapes=[pltpu.VMEM((tokens, width), F32)],
                compiler_params=room(6),
                name="join",
            )(info, mid_s, mid_k, get_a, get_b, get_s, get_west, get_east)
            got, key_grad = lax.optimization_barrier((got, key_grad))
        note = shape((2 * message.shape[0] - heads, model))
        kernel = functools.partial(grow_kernel, 3 + number, count, heads)
        message = step_call(kernel, "grow", note, info, message, got)
    got = swap(message, mesh_shape, rounds[0])
    weight_grad, bias_grad = step_call(
        functools.partial(last_kernel, 3, norm, count),
        "last",
        [shape((width, model)), shape((SPAN, heads, SPAN), F32)],
        info, message, got,
    )
    return (
        block_out.reshape(lat_dev, lon_dev, model),
        query_grad.reshape(queries.shape),
        key_grad.reshape(keys.shape),
        value_grad.reshape(values.shape),
        weight_grad,
        bias_grad.transpose(1, 0, 2),
    )


def solution(mesh):
    spec = P("lat", "lon", None)
    return jax.shard_map(
        functools.partial(shards, dict(mesh.shape)),
        mesh=mesh,
        in_specs=(spec, spec, spec, P(), P(), spec),
        out_specs=(spec, spec, spec, spec, P(), P()),
        check_vma=False,
    )
```

```python
import functools

import jax
import jax.numpy as jnp
from jax import lax
from jax.experimental import pallas as pl
from jax.experimental.pallas import tpu as pltpu
from jax.sharding import PartitionSpec as P

RAD = 6
SPAN = 2 * RAD + 1
TILE = 4
GROUP = 4
NEG = -1e30
NT = (((1,), (1,)), ((), ()))
F32 = jnp.float32
BF16 = jnp.bfloat16
SLOTS = 16
CORNER = 80
MIB = 1 << 20


def dot(a, b):
    return jnp.dot(a, b, preferred_element_type=F32)


def dot_nt(a, b):
    return lax.dot_general(a, b, NT, preferred_element_type=F32)


def in_hbm(x):
    return pltpu.with_memory_space_constraint(x, pltpu.HBM)


def room(mib):
    return pltpu.CompilerParams(vmem_limit_bytes=mib * MIB)


def iota2(shape, axis):
    return lax.broadcasted_iota(jnp.int32, shape, axis)


def hot(mask):
    return mask.astype(F32).astype(BF16)


def over(x, n):
    if n & (n - 1) == 0:
        return x >> (n.bit_length() - 1), x & (n - 1)
    return x // n, x % n


def down_iota(n):
    return iota2((n, 1), 0)


def along_iota(n):
    return iota2((1, n), 1)


def spread_heads(tile, cols, head_size):
    lane = over(iota2((cols, tile.shape[1]), 1), head_size)[0]
    zero = jnp.zeros((cols, tile.shape[1]), tile.dtype)
    parts = []
    for i in range(TILE):
        rows = tile[i * cols : (i + 1) * cols]
        for h in range(GROUP):
            parts.append(jnp.where(lane == h, rows, zero))
    return jnp.concatenate(parts, 0)


def head_mask(cols, head_size):
    shape = (GROUP * head_size, TILE * GROUP * cols)
    column = over(over(iota2(shape, 1), cols)[0], GROUP)[1]
    return over(iota2(shape, 0), head_size)[0] == column


def picker(cols):
    row_i, row_j = over(down_iota(TILE * cols), cols)
    high, col_j = over(along_iota(TILE * GROUP * cols), cols)
    return hot((row_i == over(high, GROUP)[0]) & (row_j == col_j))


def keep_rows(st, first_row, rows_all, cols_pad):
    parts = []
    for k in range(TILE + 2 * RAD):
        row = first_row + k
        inside = (row >= 0) & (row < rows_all)
        parts.append(jnp.where(inside, st[k * cols_pad : (k + 1) * cols_pad], NEG))
    return jnp.concatenate(parts, 0)


def take_cols(rows, cols, first):
    r, c = over(down_iota(rows * RAD), RAD)
    return hot(along_iota(rows * cols) == r * cols + first + c)


def put_cols(rows, cols, first):
    r, c = over(along_iota(rows * RAD), RAD)
    return hot(down_iota(rows * cols) == r * cols + first + c)


def put_corner(cols):
    n = along_iota(CORNER)
    half = RAD * RAD
    r, c = over(jnp.where(n < half, n, n - half), RAD)
    target = r * cols + c + jnp.where(n < half, 0, RAD)
    return hot((down_iota(RAD * cols) == target) & (n < 2 * half))


def pack_kernel(
    rows, cols, info_ref, k_hbm, v_hbm, east_ref, west_ref, a_ref, b_ref, x_ref, sem_ref
):
    copies = [
        pltpu.make_async_copy(ref, x_ref.at[i], sem_ref.at[i])
        for i, ref in enumerate((k_hbm, v_hbm))
    ]
    for copy in copies:
        copy.start()
    pick_east = take_cols(rows, cols, cols - RAD)
    pick_west = take_cols(rows, cols, 0)
    edge = RAD * cols
    odd = info_ref[2] == 1
    for i, copy in enumerate(copies):
        copy.wait()
        x = x_ref[i]
        east_ref[i] = dot(pick_east, x).astype(BF16)
        west_ref[i] = dot(pick_west, x).astype(BF16)
        down = x[(rows - RAD) * cols :]
        up = x[:edge]
        a_ref[i] = jnp.where(odd, up, down)
        b_ref[i] = jnp.where(odd, down, up)


def corner_kernel(rows, cols, info_ref, w_ref, e_ref, own_ref, a_ref, b_ref):
    half = RAD * RAD
    edge = RAD * cols
    n = down_iota(CORNER)
    src = along_iota(rows * RAD)
    odd = info_ref[2] == 1
    last = (rows - RAD) * RAD
    a_ref[:, :edge, :] = own_ref[...]
    for ref, lo, first in (
        (b_ref, 0, jnp.where(odd, last, 0)),
        (a_ref, edge, jnp.where(odd, 0, last)),
    ):
        pick_w = hot((src == first + n) & (n < half))
        pick_e = hot((src == first + n - half) & (n >= half) & (n < 2 * half))
        for i in range(2):
            side = dot(pick_w, w_ref[i]) + dot(pick_e, e_ref[i])
            ref[i, lo:, :] = side.astype(BF16)


def prepare_kernel(
    cols, cols_pad, rel_ref, cot_hbm, w_hbm, out_ref, grad_ref, c_ref, r_ref, cot_ref, w_ref,
    sem_ref,
):
    copies = [
        pltpu.make_async_copy(cot_hbm, cot_ref, sem_ref.at[0]),
        pltpu.make_async_copy(w_hbm, w_ref, sem_ref.at[1]),
    ]
    for copy in copies:
        copy.start()
    heads = rel_ref.shape[1]
    lanes = heads * cols
    half = lanes // 2
    shape = (cols_pad, lanes)
    offset = slot_offset(shape, cols)
    inside = (offset >= 0) & (offset < SPAN)
    head = over(iota2((1, lanes), 1), cols)[0]
    for a in range(SPAN):
        tile = jnp.full(shape, NEG, F32)
        for b in range(SPAN):
            row = jnp.full((1, lanes), rel_ref[a, 0, b], F32)
            for h in range(1, heads):
                row = jnp.where(head == h, rel_ref[a, h, b], row)
            tile = jnp.where(offset == b, row, tile)
        tile = jnp.where(inside, tile, NEG)
        c_ref[a] = tile
        r_ref[a] = pltpu.roll(tile, half, 1)
    low = iota2(shape, 1) < half
    blank = jnp.full(shape, NEG, F32)
    for g in range(2):
        first, second = (c_ref, r_ref) if g == 0 else (r_ref, c_ref)
        for pair in range(TILE // 2):
            i = 2 * pair
            lo = (g * TILE // 2 + pair) * lanes
            for k in range(TILE + 2 * RAD):
                a = k - i
                one = first[a] if 0 <= a < SPAN else blank
                two = second[a - 1] if 0 <= a - 1 < SPAN else blank
                out_ref[k * cols_pad : (k + 1) * cols_pad, lo : lo + lanes] = jnp.where(
                    low, one, two
                )
    for copy in copies:
        copy.wait()
    grad_ref[...] = dot_nt(cot_ref[...], w_ref[...]).astype(BF16)


def slot_offset(shape, cols):
    slot = iota2(shape, 0)
    pos = jnp.where(slot < cols, slot + RAD, jnp.where(slot < cols + RAD, slot - cols, slot))
    pos = jnp.where(slot < cols + 2 * RAD, pos, -1000)
    return pos - over(iota2(shape, 1), cols)[1]


def assemble(out_ref, i, rows, cols, cols_pad, own, refs, group, odd):
    w_ref, e_ref, a_ref, b_ref, c_ref = refs
    edge = RAD * cols
    side = dot(put_cols(rows, SLOTS, 0), w_ref[i, :, group])
    side = (side + dot(put_cols(rows, SLOTS, RAD), e_ref[i, :, group])).astype(BF16)
    for r in range(rows):
        lo = (RAD + r) * cols_pad
        out_ref[lo : lo + cols, :] = own[r * cols : (r + 1) * cols, group]
        out_ref[lo + cols : lo + cols + SLOTS, :] = side[r * SLOTS : (r + 1) * SLOTS]
    put = put_corner(SLOTS)
    below = (RAD + rows) * cols_pad
    corner_a = a_ref[i, edge:, group]
    for first, o_ref, corner in (
        (jnp.where(odd, 0, below), a_ref, corner_a),
        (jnp.where(odd, below, 0), b_ref, c_ref[i, :, group]),
    ):
        side = dot(put, corner).astype(BF16)
        for r in range(RAD):
            lo = pl.multiple_of(first + r * cols_pad, cols_pad)
            out_ref[pl.ds(lo, cols), :] = o_ref[i, r * cols : (r + 1) * cols, group]
            lo = pl.multiple_of(first + r * cols_pad + cols, cols)
            out_ref[pl.ds(lo, SLOTS), :] = side[r * SLOTS : (r + 1) * SLOTS]


def group_lanes(group, lanes):
    return pl.ds(pl.multiple_of(group * lanes, lanes), lanes)


def fwd_kernel(
    sizes, n, info_ref, q_ref, k_ref, v_ref, w_ref, e_ref, a_ref, b_ref, c_ref,
    bias_ref, cot_ref, out_ref, weight_ref, p_ref, ko_ref, vo_ref, vt_ref, at_ref,
):
    lat_dev, cols, cols_pad, head_size, rows_all = sizes
    scale = head_size ** (-0.5)
    group = group_lanes(info_ref[n], GROUP * head_size)
    refs = (w_ref, e_ref, a_ref, b_ref, c_ref)
    odd = info_ref[2] == 1
    assemble(ko_ref, 0, lat_dev, cols, cols_pad, k_ref, refs, group, odd)
    assemble(vo_ref, 1, lat_dev, cols, cols_pad, v_ref, refs, group, odd)
    vt_ref[...] = vo_ref[...].T
    mask = head_mask(cols, head_size)
    pick = picker(cols)
    win = (TILE + 2 * RAD) * cols_pad
    for t in range(lat_dev // TILE):
        lo = t * TILE * cols_pad
        qs = pl.ds(t * TILE * cols, TILE * cols)
        q_bd = spread_heads(q_ref[qs, group] * jnp.asarray(scale, BF16), cols, head_size)
        first = info_ref[1] * lat_dev + t * TILE - RAD
        st = dot_nt(ko_ref[pl.ds(lo, win), :], q_bd) + bias_ref[:, group]
        st = keep_rows(st, first, rows_all, cols_pad)
        m = jnp.max(st, 0, keepdims=True)
        e = jnp.exp(st - m)
        p = e * (1.0 / jnp.sum(e, 0, keepdims=True))
        p_ref[t] = p
        ot = dot(vt_ref[:, pl.ds(lo, win)], p.astype(BF16))
        ot = jnp.where(mask, ot, 0.0).astype(BF16)
        out_ref[qs, :] = dot_nt(pick, ot).astype(BF16)
    at_ref[...] = out_ref[...].T
    weight_ref[...] = dot(at_ref[...], cot_ref[...]).astype(weight_ref.dtype)


def bwd_kernel(sizes, n, info_ref, q_ref, g_ref, p_ref, k_ref, v_ref, *refs):
    dq_ref, sa_ref, sb_ref, mid_ref, side_ref, x_ref, kt_ref, dk_ref, dv_ref, db_ref = refs[-10:]
    before = refs[:-10]
    lat_dev, cols, cols_pad, head_size, rows_all = sizes
    scale = head_size ** (-0.5)
    mask = head_mask(cols, head_size)
    pick = picker(cols)
    win = (TILE + 2 * RAD) * cols_pad
    half = GROUP * cols
    low = iota2((cols_pad, 2 * half), 1) < half
    which = info_ref[n]
    group = group_lanes(which, GROUP * head_size)
    mine = group if before else slice(None)
    if before:
        other = group_lanes(1 - which, GROUP * head_size)
        dq_ref[:, other] = before[0][...]
        sa_ref[:, :, other] = before[1][...]
    kt_ref[...] = k_ref[...].T
    dk_ref[...] = jnp.zeros_like(dk_ref)
    dv_ref[...] = jnp.zeros_like(dv_ref)
    for t in range(lat_dev // TILE):
        lo = t * TILE * cols_pad
        qs = pl.ds(t * TILE * cols, TILE * cols)
        ws = pl.ds(lo, win)
        q_bd = spread_heads(q_ref[qs, group] * jnp.asarray(scale, BF16), cols, head_size)
        g_bd = spread_heads(g_ref[qs, group], cols, head_size)
        p = p_ref[t]
        slope = dot_nt(v_ref[ws, :], g_bd)
        inner = jnp.sum(p * slope, 0, keepdims=True)
        sg = p * (slope - inner)
        if t == 0:
            db_ref[...] = sg
        else:
            db_ref[...] += sg
        sgb = sg.astype(BF16)
        dqt = jnp.where(mask, dot(kt_ref[:, ws], sgb) * scale, 0.0).astype(BF16)
        dq_ref[qs, mine] = dot_nt(pick, dqt).astype(BF16)
        dk_ref[ws, :] += dot(sgb, q_bd)
        dv_ref[ws, :] += dot(p.astype(BF16), g_bd)
    edge = RAD * cols_pad
    odd = info_ref[2] == 1
    low_rows = edge + lat_dev * cols_pad
    first_a = pl.multiple_of(jnp.where(odd, 0, low_rows), cols_pad)
    first_b = pl.multiple_of(jnp.where(odd, low_rows, 0), cols_pad)
    for i, ref in enumerate((dk_ref, dv_ref)):
        sa_ref[i, :, mine] = ref[pl.ds(first_a, edge), :].astype(BF16)
        sb_ref[i] = ref[pl.ds(first_b, edge), :].astype(BF16)
        for r in range(lat_dev):
            lo = (RAD + r) * cols_pad
            mid_ref[i, r * cols : (r + 1) * cols, :] = ref[lo : lo + cols, :]
            side_ref[i, r * SLOTS : (r + 1) * SLOTS, :] = ref[lo + cols : lo + cols_pad, :]
    for a in range(SPAN):
        total = jnp.zeros((cols_pad, 2 * half), F32)
        for pair in range(TILE // 2):
            i = 2 * pair
            lanes = slice(pair * 2 * half, (pair + 1) * 2 * half)
            one = db_ref[(a + i) * cols_pad : (a + i + 1) * cols_pad, lanes]
            two = db_ref[(a + i + 1) * cols_pad : (a + i + 2) * cols_pad, lanes]
            total = total + jnp.where(low, one, two)
        x_ref[a * cols_pad : (a + 1) * cols_pad, :] = total


def bias_kernel(cols, cols_pad, info_ref, xs_ref, xk_ref, out_ref, z_ref):
    lanes = xs_ref.shape[1]
    half = lanes // 2
    shape = (cols_pad, lanes)
    low = (over(iota2(shape, 1), half)[0] == info_ref[0])
    offset = slot_offset(shape, cols)
    z_ref[...] = jnp.zeros_like(z_ref)
    for a in range(SPAN):
        rows = slice(a * cols_pad, (a + 1) * cols_pad)
        one = xs_ref[rows, :]
        two = xk_ref[rows, :]
        both = jnp.where(low, one + pltpu.roll(one, half, 1), two + pltpu.roll(two, half, 1))
        for b in range(SPAN):
            n = a * SPAN + b
            z_ref[n : n + 1, :] = jnp.sum(jnp.where(offset == b, both, 0.0), 0, keepdims=True)
    heads = out_ref.shape[0]
    pick = (over(iota2((heads, lanes), 1), cols)[0] == iota2((heads, lanes), 0)).astype(F32)
    out_ref[...] = lax.dot_general(
        pick, z_ref[...], NT, precision=lax.Precision.HIGHEST, preferred_element_type=F32
    )


def lat_terms(ref, i, rows, cols, cols_pad, first):
    parts = []
    for r in range(RAD):
        lo = r * cols_pad + first
        parts.append(ref[i, lo : lo + cols, :])
    return jnp.concatenate(parts, 0).astype(F32)


def strips(info_ref, rows, cols):
    odd = info_ref[2] == 1
    last = (rows - RAD) * cols
    return [pl.multiple_of(jnp.where(odd, x, last - x), cols) for x in (0, last)]


def both_lanes(info_ref, lanes):
    return group_lanes(info_ref[0], lanes), group_lanes(1 - info_ref[0], lanes)


def both_groups(info_ref, dst_ref, i, *refs):
    for ref, group in zip(refs, both_lanes(info_ref, refs[0].shape[2])):
        dst_ref[:, group] = ref[i]


def side_kernel(
    rows, cols, cols_pad, info_ref, ss_ref, sk_ref, a_ref, bk_ref, bs_ref, west_ref, east_ref,
    s_ref,
):
    edge = RAD * SLOTS
    pick_west = take_cols(rows, SLOTS, 0)
    pick_east = take_cols(rows, SLOTS, RAD)
    for i in range(2):
        both_groups(info_ref, s_ref, i, ss_ref, sk_ref)
        first_a, first_b = strips(info_ref, rows, SLOTS)
        s_ref[pl.ds(first_a, edge), :] += lat_terms(a_ref, i, rows, SLOTS, cols_pad, cols)
        for ref, group in zip((bk_ref, bs_ref), both_lanes(info_ref, bs_ref.shape[2])):
            s_ref[pl.ds(first_b, edge), group] += lat_terms(ref, i, rows, SLOTS, cols_pad, cols)
        x = s_ref[...].astype(BF16)
        west_ref[i] = dot(pick_west, x).astype(BF16)
        east_ref[i] = dot(pick_east, x).astype(BF16)


def join_kernel(
    rows, cols, cols_pad, info_ref, ms_ref, mk_ref, a_ref, bk_ref, bs_ref, w_ref, e_ref,
    k_ref, v_ref, s_ref,
):
    edge = RAD * cols
    put_west = put_cols(rows, cols, 0)
    put_east = put_cols(rows, cols, cols - RAD)
    for i, out_ref in enumerate((k_ref, v_ref)):
        both_groups(info_ref, s_ref, i, ms_ref, mk_ref)
        s_ref[...] += dot(put_west, w_ref[i]) + dot(put_east, e_ref[i])
        first_a, first_b = strips(info_ref, rows, cols)
        s_ref[pl.ds(first_a, edge), :] += lat_terms(a_ref, i, rows, cols, cols_pad, 0)
        for ref, group in zip((bk_ref, bs_ref), both_lanes(info_ref, bs_ref.shape[2])):
            s_ref[pl.ds(first_b, edge), group] += lat_terms(ref, i, rows, cols, cols_pad, 0)
        out_ref[...] = s_ref[...].astype(BF16)


def bits_of(mesh_shape):
    order = []
    for axis in ("lat", "lon"):
        bit = 1
        while bit < mesh_shape[axis]:
            order.append((axis, bit))
            bit *= 2
    return order


def rounds_of(mesh_shape):
    first, *rest = bits_of(mesh_shape)
    rest[-3], rest[-2] = rest[-2], rest[-3]
    middle, ends = rest[:-2], rest[-2:]
    turned = middle[1:] + middle[:1]
    return [(first, first)] + list(zip(middle, turned)), list(zip(ends, ends[::-1]))


def partner_pairs(mesh_shape, bits):
    n_lat, n_lon = mesh_shape["lat"], mesh_shape["lon"]
    pairs = []
    for i in range(n_lat):
        axis, bit = bits[i % 2]
        for j in range(n_lon):
            a, b = (i ^ bit, j) if axis == "lat" else (i, j ^ bit)
            pairs.append((i * n_lon + j, a * n_lon + b))
    return pairs


def swap(x, mesh_shape, bits):
    return lax.ppermute(x, ("lat", "lon"), partner_pairs(mesh_shape, bits))


def my_bit(bits):
    def of(axis, bit):
        return (lax.axis_index(axis) // bit) % 2

    odd = lax.axis_index("lat") % 2
    return jnp.where(odd == 0, of(*bits[0]), of(*bits[1]))


def put_bias(ref, rows, bias):
    heads, count = bias.shape
    high = bias.astype(BF16)
    ref[rows:, :count] = high
    ref[rows:, count : 2 * count] = (bias - high.astype(F32)).astype(BF16)
    ref[rows:, 2 * count :] = jnp.zeros((heads, ref.shape[1] - 2 * count), BF16)


def get_bias(ref, rows, count):
    return ref[rows:, :count].astype(F32) + ref[rows:, count : 2 * count].astype(F32)


def halve_kernel(n, info_ref, keep_ref, got_ref, send_ref, out_ref):
    half = send_ref.shape[0]
    low = keep_ref[:half, :] + got_ref[:half, :].astype(F32)
    high = keep_ref[half:, :] + got_ref[half:, :].astype(F32)
    lower = info_ref[n] == 0
    send_ref[...] = jnp.where(lower, high, low).astype(BF16)
    out_ref[...] = jnp.where(lower, low, high)


def meet_kernel(keep_ref, got_ref, bias_ref, out_ref):
    rows = keep_ref.shape[0]
    out_ref[:rows, :] = (keep_ref[...] + got_ref[...].astype(F32)).astype(BF16)
    put_bias(out_ref, rows, bias_ref[...])


def total_kernel(norm, count, heads, own_ref, got_ref, out_ref):
    rows = own_ref.shape[0] - heads
    total = own_ref[:rows, :].astype(F32) + got_ref[:rows, :].astype(F32)
    out_ref[:rows, :] = (total if norm is None else total * norm).astype(BF16)
    put_bias(out_ref, rows, get_bias(own_ref, rows, count) + get_bias(got_ref, rows, count))


def grow_kernel(n, count, heads, info_ref, own_ref, got_ref, out_ref):
    rows = own_ref.shape[0] - heads
    lower = info_ref[n] == 0
    own = own_ref[:rows, :]
    got = got_ref[:rows, :]
    out_ref[:rows, :] = jnp.where(lower, own, got)
    out_ref[rows : 2 * rows, :] = jnp.where(lower, got, own)
    put_bias(out_ref, 2 * rows, get_bias(own_ref, rows, count) + get_bias(got_ref, rows, count))


def last_kernel(n, norm, count, info_ref, own_ref, got_ref, out_ref, bias_ref):
    rows = out_ref.shape[0] // 2
    lower = info_ref[n] == 0
    own = own_ref[:rows, :]
    got = got_ref[:rows, :]
    out_ref[:rows, :] = jnp.where(lower, own, got)
    out_ref[rows:, :] = jnp.where(lower, got, own)
    bias = (get_bias(own_ref, rows, count) + get_bias(got_ref, rows, count)) * norm
    for a in range(SPAN):
        bias_ref[a] = bias[:, a * SPAN : (a + 1) * SPAN]


def project_kernel(info_ref, s_ref, k_ref, w_ref, out_ref):
    rows = s_ref.shape[1]
    first = pl.ds(pl.multiple_of(info_ref[0] * rows, rows), rows)
    second = pl.ds(pl.multiple_of((1 - info_ref[0]) * rows, rows), rows)
    out = dot(s_ref[...], w_ref[first, :]) + dot(k_ref[...], w_ref[second, :])
    out_ref[...] = out.astype(BF16)


def shards(mesh_shape, queries, keys, values, rel_bias, out_weight, cotangent):
    lat_dev, lon_dev, width = queries.shape
    heads = rel_bias.shape[0]
    head_size = width // heads
    groups = heads // GROUP
    lanes = GROUP * head_size
    model = out_weight.shape[1]
    n_lat, n_lon = mesh_shape["lat"], mesh_shape["lon"]
    cols_pad = lon_dev + SLOTS
    outer_lat = lat_dev + 2 * RAD
    tokens = lat_dev * lon_dev
    norm = (tokens * n_lat * n_lon) ** (-0.5)
    east = [(i, (i + 1) % n_lon) for i in range(n_lon)]
    west = [(i, (i - 1) % n_lon) for i in range(n_lon)]
    pair_a = [(i, i ^ 1) for i in range(n_lat)]
    pair_b = [(i, i + 1) for i in range(1, n_lat - 1, 2)]
    pair_b = pair_b + [(j, i) for i, j in pair_b]
    win = (TILE + 2 * RAD) * cols_pad
    tiles = lat_dev // TILE
    lanes_q = TILE * GROUP * lon_dev
    n_keys = outer_lat * cols_pad
    n_side = lat_dev * RAD
    n_edge = RAD * lon_dev
    n_strip = RAD * cols_pad

    def shape(dims, dtype=BF16):
        return jax.ShapeDtypeStruct(dims, dtype)

    q_flat = queries.reshape(tokens, width)
    k_flat = keys.reshape(tokens, width)
    v_flat = values.reshape(tokens, width)
    cot = cotangent.reshape(tokens, model)

    lat_index = lax.axis_index("lat").astype(jnp.int32)
    core = lat_index % 2
    rounds, ends = rounds_of(mesh_shape)
    facts = [1 - core, lat_index, core] + [my_bit(bits) for bits in rounds]
    info = jnp.stack([x.astype(jnp.int32) for x in facts])
    smem = pl.BlockSpec(memory_space=pltpu.SMEM)
    vmem = pl.BlockSpec(memory_space=pltpu.VMEM)
    hbm = pl.BlockSpec(memory_space=pltpu.HBM)

    to_east, to_west, own_a, own_b = pl.pallas_call(
        functools.partial(pack_kernel, lat_dev, lon_dev),
        in_specs=[smem, hbm, hbm],
        out_shape=[shape((2, n_side, width))] * 2 + [shape((2, n_edge, width))] * 2,
        scratch_shapes=[pltpu.VMEM((2, tokens, width), BF16), pltpu.SemaphoreType.DMA((2,))],
        compiler_params=room(4),
        name="pack",
    )(info, in_hbm(k_flat), in_hbm(v_flat))
    from_west = lax.ppermute(to_east, "lon", east)
    from_east = lax.ppermute(to_west, "lon", west)
    from_b = lax.ppermute(own_b, "lat", pair_b)
    sizes = (lat_dev, lon_dev, cols_pad, head_size, lat_dev * n_lat)
    table, attended_grad = pl.pallas_call(
        functools.partial(prepare_kernel, lon_dev, cols_pad),
        in_specs=[smem, hbm, hbm],
        out_shape=[shape((win, groups * lanes_q), F32), shape((tokens, width))],
        scratch_shapes=[pltpu.VMEM((SPAN, cols_pad, heads * lon_dev), F32)] * 2
        + [pltpu.VMEM((tokens, model), BF16), pltpu.VMEM((width, model), BF16)]
        + [pltpu.SemaphoreType.DMA((2,))],
        compiler_params=room(6),
        name="prepare",
    )(rel_bias.transpose(1, 0, 2), in_hbm(cot), in_hbm(out_weight))
    from_west, from_east, from_b, table = lax.optimization_barrier(
        (from_west, from_east, from_b, table)
    )

    corner_a, corner_b = pl.pallas_call(
        functools.partial(corner_kernel, lat_dev, lon_dev),
        in_specs=[smem] + [vmem] * 3,
        out_shape=[shape((2, n_edge + CORNER, width)), shape((2, CORNER, width))],
        compiler_params=room(4),
        name="corner",
    )(info, from_west, from_east, own_a)
    side_b = lax.ppermute(corner_b, "lat", pair_b)
    from_a = lax.ppermute(corner_a, "lat", pair_a)
    probs = (tiles, win, lanes_q)
    outer = (n_keys, lanes)

    def forward(n, dtype):
        return pl.pallas_call(
            functools.partial(fwd_kernel, sizes, n),
            in_specs=[smem] + [vmem] * 10,
            out_shape=[shape((tokens, lanes)), shape((lanes, model), dtype), shape(probs, F32)]
            + [shape(outer)] * 2,
            scratch_shapes=[pltpu.VMEM((lanes, n_keys), BF16), pltpu.VMEM((lanes, tokens), BF16)],
            compiler_params=room(8),
            name="attend_fwd",
        )(
            info, q_flat, k_flat, v_flat, from_west, from_east,
            from_a, from_b, side_b, table, cot,
        )

    def step_call(kernel, name, outs, *operands):
        scalars = [smem if x.dtype == jnp.int32 else vmem for x in operands]
        return pl.pallas_call(
            kernel, in_specs=scalars, out_shape=outs, compiler_params=room(4), name=name
        )(*operands)

    att_s, weight_s, p_s, k_s, v_s = forward(0, BF16)
    got = swap(weight_s, mesh_shape, rounds[0])
    att_k, keep, p_k, k_k, v_k = forward(2, F32)

    def halve(keep, got, number):
        half = (keep.shape[0] // 2, model)
        outs = [shape(half), shape(half, F32)]
        kernel = functools.partial(halve_kernel, 3 + number)
        return step_call(kernel, "halve", outs, info, keep, got)

    send, keep = halve(keep, got, 1)
    def backward(n, info, p, k, v, *before):
        size = width if before else lanes
        return pl.pallas_call(
            functools.partial(bwd_kernel, sizes, n),
            in_specs=[smem] + [vmem] * (5 + len(before)),
            out_shape=[shape((tokens, size)), shape((2, n_strip, size))]
            + [shape((2, n_strip, lanes))]
            + [shape((2, tokens, lanes), F32)] * 2
            + [shape((SPAN * cols_pad, 2 * GROUP * lon_dev), F32)],
            scratch_shapes=[pltpu.VMEM((lanes, n_keys), BF16)]
            + [pltpu.VMEM((n_keys, lanes), F32)] * 2
            + [pltpu.VMEM((win, lanes_q), F32)],
            compiler_params=room(10),
            name="attend_bwd",
        )(info, q_flat, attended_grad, p, k, v, *before)

    info_b, send = lax.optimization_barrier((info, send))
    got = swap(send, mesh_shape, rounds[1])
    *before, strip_s, mid_s, side_s, fold_s = backward(0, info_b, p_s, k_s, v_s)
    got, fold_s = lax.optimization_barrier((got, fold_s))
    get_s = lax.ppermute(strip_s, "lat", pair_b)
    for number in range(2, len(rounds)):
        send, keep = halve(keep, got, number)
        if number == 2:
            info_b, send = lax.optimization_barrier((info, send))
        got = swap(send, mesh_shape, rounds[number])
    after = backward(2, info_b, p_k, k_k, v_k, *before)
    query_grad, strip_a, strip_b, mid_k, side_k, fold_k = after
    got, fold_k, strip_a, strip_b, get_s = lax.optimization_barrier(
        (got, fold_k, strip_a, strip_b, get_s)
    )
    get_b = lax.ppermute(strip_b, "lat", pair_b)
    get_a = lax.ppermute(strip_a, "lat", pair_a)

    count = 256
    bias_local = pl.pallas_call(
        functools.partial(bias_kernel, lon_dev, cols_pad),
        in_specs=[smem, vmem, vmem],
        out_shape=shape((heads, count), F32),
        scratch_shapes=[pltpu.VMEM((count, heads * lon_dev), F32)],
        compiler_params=room(4),
        name="bias_fold",
    )(info, fold_s, fold_k)
    block_out = pl.pallas_call(
        project_kernel,
        in_specs=[smem] + [vmem] * 3,
        out_shape=shape((tokens, model)),
        compiler_params=room(6),
        name="project",
    )(info, att_s, att_k, out_weight)
    note = shape((keep.shape[0] + heads, model))
    message = step_call(meet_kernel, "meet", note, keep, got, bias_local)
    got = swap(message, mesh_shape, ends[0])
    kernel = functools.partial(total_kernel, None, count, heads)
    message = step_call(kernel, "total", note, message, got)
    got = swap(message, mesh_shape, ends[1])
    give_west, give_east = pl.pallas_call(
        functools.partial(side_kernel, lat_dev, lon_dev, cols_pad),
        in_specs=[smem] + [vmem] * 5,
        out_shape=[shape((2, n_side, width))] * 2,
        scratch_shapes=[pltpu.VMEM((tokens, width), F32)],
        compiler_params=room(6),
        name="side",
    )(info, side_s, side_k, get_a, get_b, get_s)
    get_east = lax.ppermute(give_west, "lon", west)
    get_west = lax.ppermute(give_east, "lon", east)
    kernel = functools.partial(total_kernel, norm, count, heads)
    message = step_call(kernel, "total", note, message, got)
    message, give_west, give_east = lax.optimization_barrier((message, give_west, give_east))

    for number in range(len(rounds) - 1, 0, -1):
        if number == 1:
            message, get_east, get_west, block_out = lax.optimization_barrier(
                (message, get_east, get_west, block_out)
            )
        got = swap(message, mesh_shape, rounds[number])
        if number == 1:
            key_grad, value_grad = pl.pallas_call(
                functools.partial(join_kernel, lat_dev, lon_dev, cols_pad),
                in_specs=[smem] + [vmem] * 7,
                out_shape=[shape((tokens, width))] * 2,
                scratch_shapes=[pltpu.VMEM((tokens, width), F32)],
                compiler_params=room(6),
                name="join",
            )(info, mid_s, mid_k, get_a, get_b, get_s, get_west, get_east)
            got, key_grad = lax.optimization_barrier((got, key_grad))
        note = shape((2 * message.shape[0] - heads, model))
        kernel = functools.partial(grow_kernel, 3 + number, count, heads)
        message = step_call(kernel, "grow", note, info, message, got)
    got = swap(message, mesh_shape, rounds[0])
    weight_grad, bias_grad = step_call(
        functools.partial(last_kernel, 3, norm, count),
        "last",
        [shape((width, model)), shape((SPAN, heads, SPAN), F32)],
        info, message, got,
    )
    return (
        block_out.reshape(lat_dev, lon_dev, model),
        query_grad.reshape(queries.shape),
        key_grad.reshape(keys.shape),
        value_grad.reshape(values.shape),
        weight_grad,
        bias_grad.transpose(1, 0, 2),
    )


def solution(mesh):
    spec = P("lat", "lon", None)
    return jax.shard_map(
        functools.partial(shards, dict(mesh.shape)),
        mesh=mesh,
        in_specs=(spec, spec, spec, P(), P(), spec),
        out_specs=(spec, spec, spec, spec, P(), P()),
        check_vma=False,
    )
```
